32 devices in a mesh: shard: 16 (over z, y, x), rep: 2 (over core).
Axes of the slice: x: 2, y: 2, z: 4, core: 2. Of those that a mesh axis runs over, the one named last changes fastest.
Arguments:
- user_emb: bfloat16 [256, 1024, 256], P('shard', 'rep'), may hold values from -6 to 6
- elig_owner: int32 [256, 4], P('shard'), may hold values from 0 to 15, all different within a row; in each aligned block of 16 rows (0 to 15, 16 to 31, ...) at most 8 rows name the same one
- elig_local: int32 [256, 4], P('shard'), may hold values from 0 to 127
- cluster_size: int32 [256], P('shard'), may hold values from 1 to 1024, 163840 in all
- camp_emb: bfloat16 [2048, 128, 256], P('shard'), may hold values from -6 to 6
- camp_count: int32 [2048], P('shard'), may hold values from 1 to 128, 196608 in all
- dual_init: float32 [2048, 128], P('shard'), may hold values from 0 to 2
- spend_limit: float32 [2048, 128], P('shard'), may hold values from 0.1 to 10
Outputs:
- user_dual: float32 [256, 1024], P('shard', 'rep')
- campaign_dual: float32 [2048, 128], P('shard')
The draws below stay inside these ranges and needn't reach their ends.
Inputs may be any that keep to these rules, and one draw needn't show every extreme that they name: `elig_owner`: each row names 4 different owners; among the 16 rows of one shard index no owner is named more than 8 times.
All inputs are finite; a program needn't handle non-finite values. No bound on the sum of `cluster_size` or of `camp_count` on one device may be relied on, other than what follows from the above.
Results may differ from the reference program's by a relative error of at most 0.0015.
Values may be sent and summed in bfloat16 or wider, within the bound.
No kernel may reach another device: no remote copies, remote signals or barrier semaphores. Data moves between devices by JAX's collectives and lax.ppermute only.
A program may use at most 128 MiB of HBM per device.

```python
import math
import jax
import jax.numpy as jnp
import numpy as np
from jax import lax

H = 256
CB = 128
E = 4
CS = 1024
CL_DEV = 16
BL_DEV = 128
CAP = 8
CLUSTERS = 256
NBLOCKS = 2048
N_SHARD = 16


def place_ends(array, stream_key, least, top_value):
    index_at = [jax.random.randint(jax.random.fold_in(stream_key, axis), (), 0, length) for axis, length in enumerate(array.shape)]
    longest = array.shape.index(max(array.shape))
    neighbour = index_at[:longest] + [(index_at[longest] + 1) % array.shape[longest]] + index_at[longest + 1:]
    return array.at[tuple(index_at)].set(least).at[tuple(neighbour)].set(top_value)


def block_levels(rng, extent, pieces, least, high):
    loudness, own = 1.0, jax.random.fold_in(rng, 6)
    for position, shards_of in pieces:
        steps = jnp.exp(jax.random.uniform(jax.random.fold_in(own, position), (shards_of,), jnp.float32, least / len(pieces), high / len(pieces)))
        loudness = loudness * jnp.repeat(steps, extent[position] // shards_of).reshape([-1 if axis == position else 1 for axis in range(len(extent))])
    return loudness


def length_profile(number_of, total, reach, lean):
    loads = [(1 << 20) // math.isqrt(standing ** lean) + 1 for standing in range(2, number_of + 1)]
    surplus, given = total - reach - (number_of - 1), [1] * (number_of - 1)
    while surplus > 0:
        movable = [i for i in range(number_of - 1) if given[i] < reach]
        mass, left = sum([loads[i] for i in movable]), surplus
        for i in movable:
            more = min(reach - given[i], max(1, left * loads[i] // mass), surplus)
            given[i] = given[i] + more
            surplus = surplus - more
    return np.array([reach] + given)


def ragged_sizes(key, amount, total, most, lean):
    if amount == 2:
        one = jax.random.randint(key, (), max(1, total - most), min(most, total - 1) + 1)
        return jnp.stack([one, total - one])
    tallies = jnp.asarray(length_profile(amount, total, most, lean), jnp.int32)
    pairs = (amount - 1) // 2
    giver, sink = tallies[1:1 + 2 * pairs:2], tallies[2:2 + 2 * pairs:2]
    margin = jnp.minimum(giver - 1, most - sink)
    shifted = jax.random.randint(jax.random.fold_in(key, 1), (pairs,), 0, 1 << 20) % (margin + 1)
    tallies = tallies.at[1:1 + 2 * pairs:2].set(giver - shifted).at[2:2 + 2 * pairs:2].set(sink + shifted)
    return tallies[jax.random.permutation(jax.random.fold_in(key, 2), amount)]


def deal_out(rng, own, number, rows, number_of, top, reach, slope):
    sequence = jax.random.permutation(rng, number_of)
    crowded, ordinary = portions_of(number_of, rows * top, reach, slope, True), portions_of(number_of, rows * top, reach, slope, False)
    places = jnp.arange(number_of)

    def named(tallies, offset_by):
        used = int((tallies > 0).sum())
        fixed = max(1, used // 4)
        shifted = fixed + (places - fixed + offset_by * (used - fixed)) % max(1, number_of - fixed)
        return jnp.zeros((number_of,), jnp.int32).at[sequence[jnp.where(places < fixed, places, shifted)]].set(jnp.asarray(tallies, jnp.int32))

    tallies = jnp.where(number % 4 == 0, named(crowded, number // 4), named(ordinary, number - number // 4 - 1))
    mixed = jax.random.permutation(jax.random.fold_in(own, 3), number_of)
    donor, sink = mixed[0:number_of // 2 * 2:2], mixed[1:number_of // 2 * 2:2]
    margin = jnp.minimum(tallies[donor] - 1, reach - tallies[sink]) // 2
    margin = jnp.where((donor == sequence[0]) | (sink == sequence[0]) | (tallies[sink] == 0), 0, jnp.maximum(margin, 0))
    shifted = jax.random.randint(jax.random.fold_in(own, 4), (number_of // 2,), 0, 1 << 20) % (margin + 1)
    tallies = tallies.at[donor].add(-shifted).at[sink].add(shifted)
    members = jnp.searchsorted(jnp.cumsum(tallies), jnp.arange(rows * top), side="right").astype(jnp.int32)
    listing = members.reshape(top, rows).T
    listing = listing[jax.random.permutation(jax.random.fold_in(own, 1), rows)]
    offset_by = jax.random.randint(jax.random.fold_in(own, 2), (rows, 1), 0, top)
    return jnp.take_along_axis(listing, (jnp.arange(top)[None, :] + offset_by) % top, axis=1)


def portions_of(amount, total, limit, slope, full):
    portions = [(1 << 20) // math.isqrt(standing ** slope) + 1 for standing in range(1, amount + 1)]
    largest = limit if full else min(limit, max(-(-total // amount), total * portions[0] // sum(portions)))
    least = 1 if total - largest >= amount - 1 else 0
    given, surplus = [largest] + [least] * (amount - 1), total - largest - least * (amount - 1)
    while surplus > 0:
        free = [i for i in range(1, amount) if given[i] < largest] or [i for i in range(1, amount) if given[i] < limit]
        pool, remaining = sum([portions[i] for i in free]), surplus
        for i in free:
            extra = min(limit - given[i], max(1, remaining * portions[i] // pool), surplus)
            given[i] = given[i] + extra
            surplus = surplus - extra
    return np.array(given)


def gaussian(key, dims, spread, most, pieces=(), dtype=jnp.bfloat16):
    factor_of = block_levels(key, dims, pieces, -0.22, 0.18) if pieces else 1.0
    values = jax.random.normal(key, dims, jnp.float32) * spread * factor_of
    return jnp.minimum(jnp.maximum(values, -most), most).astype(dtype)


def setup_inputs(seed: int = 0) -> dict:
    splits = jax.random.split(jax.random.key(seed), 9)
    user_emb = gaussian(splits[0], (CLUSTERS, CS, H), 1.0, 6.0, ((0, 16), (1, 2)))
    elig_owner_keys = jax.random.split(jax.random.fold_in(splits[1], 1), CLUSTERS // CL_DEV)
    elig_owner_turns = jax.random.permutation(jax.random.fold_in(splits[1], 3), CLUSTERS // CL_DEV)
    elig_owner = jax.vmap(lambda own, number: deal_out(jax.random.fold_in(splits[1], 2), own, number, CL_DEV, N_SHARD, E, CAP, 2))(elig_owner_keys, elig_owner_turns).reshape((CLUSTERS, E))
    elig_local = place_ends(jax.random.randint(splits[2], (CLUSTERS, E), 0, BL_DEV), jax.random.fold_in(splits[2], 1), 0, BL_DEV - 1).astype(jnp.int32)
    cluster_size = ragged_sizes(splits[3], CLUSTERS, CLUSTERS * CS * 5 // 8, CS, 1).astype(jnp.int32)
    camp_emb = gaussian(splits[4], (NBLOCKS, CB, H), 1.0, 6.0, ((0, 16),))
    camp_count = ragged_sizes(splits[5], NBLOCKS, NBLOCKS * CB * 3 // 4, CB, 1).astype(jnp.int32)
    dual_init = jnp.clip(2.0 * jax.random.uniform(splits[6], (NBLOCKS, CB), jnp.float32) ** block_levels(splits[6], (NBLOCKS, CB), ((0, 16),), -0.2, 0.2), 0.0, 2.0)
    spend_limit = jnp.clip(jnp.exp(math.log(10.0) - 4.6051702 * jax.random.uniform(splits[7], (NBLOCKS, CB), jnp.float32) ** block_levels(splits[7], (NBLOCKS, CB), ((0, 16),), -0.2, 0.2)), 0.1, 10.0)
    return {"user_emb": user_emb, "elig_owner": elig_owner, "elig_local": elig_local, "cluster_size": cluster_size, "camp_emb": camp_emb, "camp_count": camp_count, "dual_init": dual_init, "spend_limit": spend_limit}


epsilon = 1e-06
temper = 0.25
sharpness = 16.0

def reference(user_emb, elig_owner, elig_local, cluster_size, camp_emb, camp_count, dual_init, spend_limit):
    block_ids = (elig_owner * BL_DEV + elig_local).astype(jnp.int32)
    slot_pos = jnp.arange(CS)
    live_users = slot_pos[None, :] < cluster_size[:, None]
    camp_pos = jnp.arange(CB)

    def run(duals):

        def one_cluster(packed):
            emb_rows, blocks, live_u = packed
            user_f = emb_rows.astype(jnp.float32)
            user_scale = lax.rsqrt(lax.optimization_barrier(jnp.mean(user_f * user_f, axis=-1)) + epsilon)
            camp_f = jnp.take(camp_emb, blocks, axis=0).astype(jnp.float32)
            camp_scale = lax.rsqrt(lax.optimization_barrier(jnp.mean(camp_f * camp_f, axis=-1)) + epsilon)
            raw_dots = jnp.einsum('uh,ech->euc', user_f, camp_f)
            scores = sharpness / H * raw_dots * user_scale[None, :, None] * camp_scale[:, None, :]
            dual_rows = jnp.take(duals, blocks, axis=0)
            counts = jnp.take(camp_count, blocks, axis=0)
            live_c = camp_pos[None, :] < counts[:, None]
            weights = jnp.where(live_c[:, None, :], jnp.exp((scores - dual_rows[:, None, :]) / temper), 0.0)
            denominator = 1.0 + lax.optimization_barrier(jnp.sum(weights, axis=(0, 2)))
            user_val = jnp.where(live_u, temper * jnp.log(denominator), 0.0)
            alloc_share = weights / denominator[None, :, None]
            spend_rows = lax.optimization_barrier(jnp.sum(jnp.where(live_u[None, :, None], alloc_share, 0.0), axis=1))
            return (user_val, spend_rows)
        user_val, spend_rows = lax.map(one_cluster, (user_emb, block_ids, live_users))
        spend_total = jax.ops.segment_sum(spend_rows.reshape(-1, CB), block_ids.reshape(-1), num_segments=NBLOCKS)
        return (user_val, spend_total)

    def update(duals, spend_total):
        return jnp.maximum(0.0, duals + temper * jnp.log((spend_total + spend_limit) / (2.0 * spend_limit)))
    first_val, spend_one = run(dual_init)
    duals_one = update(dual_init, spend_one)
    second_val, spend_two = run(duals_one)
    duals_two = update(duals_one, spend_two)
    user_dual, spend_last = run(duals_two)
    return (user_dual, duals_two)
```

```python
import functools
import math

import jax
import jax.numpy as jnp
from jax import lax
from jax.experimental import pallas as pl
from jax.experimental.pallas import tpu as pltpu
from jax.sharding import PartitionSpec as P

epsilon = 1e-06
temper = 0.25
sharpness = 16.0
gain = 1.0 / (temper * math.log(2.0))
masked = 1e30


VMEM = pl.BlockSpec(memory_space=pltpu.VMEM)
SMEM = pl.BlockSpec(memory_space=pltpu.SMEM)
ANY = pl.BlockSpec(memory_space=pl.ANY)


def gather_kernel(half, where_ref, asked_ref, camp_ref, *rest):
    outs, sem = rest[:-1], rest[-1]
    me, rep = where_ref[0], where_ref[1]
    copies = []
    for n, out in enumerate(outs):
        for j in range(half):
            block = asked_ref[me ^ (n + 1), rep * half + j]
            copies.append(pltpu.make_async_copy(camp_ref.at[block], out.at[j], sem.at[n * half + j]))
    for copy in copies:
        copy.start()
    for copy in copies:
        copy.wait()


def updated(duals, spend, limit):
    return jnp.maximum(0.0, duals + temper * jnp.log((spend + limit) / (2.0 * limit)))


def totals(match_ref, mine_ref, other_ref):
    return jnp.dot(
        match_ref[0], mine_ref[...], preferred_element_type=jnp.float32
    ) + jnp.dot(match_ref[1], other_ref[...], preferred_element_type=jnp.float32)


def sweep_users(where_ref, size_ref, user_ref, scale_ref, item_ref, item_scale_ref, dual_scr, dots, finish, fanout):
    clusters, users, _ = user_ref.shape
    camps = item_ref.shape[1]
    width = item_ref.shape[2]
    rows = 64

    def cluster(k, carry):
        first = pl.multiple_of(k * fanout, fanout)
        blocks = item_ref[pl.ds(first, fanout)].reshape(fanout * camps, width)
        dots[...] = lax.dot_general(
            user_ref[k], blocks, (((1,), (1,)), ((), ())), preferred_element_type=jnp.float32
        )
        item_scale = item_scale_ref[pl.ds(first, fanout), :]
        shift = dual_scr[pl.ds(first, fanout), :]
        scales = [jnp.broadcast_to(item_scale[e : e + 1], (rows, camps)) for e in range(fanout)]
        shifts = [jnp.broadcast_to(shift[e : e + 1], (rows, camps)) for e in range(fanout)]
        sums = [jnp.zeros((8, camps), jnp.float32) for _ in range(fanout)]
        for start in range(0, users, rows):
            user_scale = scale_ref[k, start : start + rows, :]
            weights = []
            for e in range(fanout):
                raw = dots[start : start + rows, e * camps : (e + 1) * camps]
                weights.append(jnp.exp2(raw * user_scale * scales[e] - shifts[e]))
            den = 1.0 + jnp.sum(functools.reduce(jnp.add, weights), axis=1, keepdims=True)
            sums = finish(k, start, rows, weights, den, sums)
        return finish(k, None, rows, None, None, sums)

    lax.fori_loop(0, clusters, cluster, 0)


def spend_finish(where_ref, size_ref, users, fanout, spend_scr):
    def finish(k, start, rows, weights, den, sums):
        if start is None:
            for e in range(fanout):
                spend_scr[pl.ds(k * fanout + e, 1), :] = jnp.sum(sums[e], axis=0, keepdims=True)
            return 0
        place = where_ref[1] * users + start + lax.broadcasted_iota(jnp.int32, (rows, 1), 0)
        share = jnp.where(place < size_ref[k], 1.0 / den, 0.0)
        out = []
        for e in range(fanout):
            part = weights[e] * share
            total = sums[e]
            for r in range(0, rows, 8):
                total = total + part[r : r + 8]
            out.append(total)
        return out

    return finish


def halves(where_ref, spend_scr, mine_ref, theirs_ref):
    count = mine_ref.shape[0]
    rep = where_ref[1]
    mine_ref[...] = spend_scr[pl.ds(pl.multiple_of(rep * count, count), count), :]
    theirs_ref[...] = spend_scr[pl.ds(pl.multiple_of((1 - rep) * count, count), count), :]


def first_kernel(
    shards, half, fanout, where_ref, size_ref, item_at_ref, own_ref, user_ref, scale_ref, duals_ref, live_ref,
    item_scale_ref, camp_ref, *rest
):
    received, (mine_ref, theirs_ref, item_ref), (dots, dual_scr, spend_scr, sem) = (
        rest[: 2 * (shards - 1)], rest[-7:-4], rest[-4:]
    )
    cap = 2 * half
    rep = where_ref[1]
    users = user_ref.shape[1]

    def fetch(slot, source):
        item = item_at_ref[slot]

        @pl.when(item >= 0)
        def _():
            pltpu.make_async_copy(source, item_ref.at[item], sem.at[item]).start()

    for j in range(cap):
        fetch(j, camp_ref.at[own_ref[j]])
    for n in range(shards - 1):
        for j in range(half):
            fetch((n + 1) * cap + rep * half + j, received[2 * n].at[j])
            fetch((n + 1) * cap + (1 - rep) * half + j, received[2 * n + 1].at[j])
    dual_scr[...] = jnp.where(live_ref[...] > 0.5, duals_ref[...] * gain, masked)

    def landed(item, carry):
        pltpu.make_async_copy(camp_ref.at[0], item_ref.at[item], sem.at[item]).wait()
        return carry

    lax.fori_loop(0, item_ref.shape[0], landed, 0)
    finish = spend_finish(where_ref, size_ref, users, fanout, spend_scr)
    sweep_users(where_ref, size_ref, user_ref, scale_ref, item_ref, item_scale_ref, dual_scr, dots, finish, fanout)
    halves(where_ref, spend_scr, mine_ref, theirs_ref)


def second_kernel(
    fanout, where_ref, size_ref, user_ref, scale_ref, duals_ref, live_ref, item_scale_ref, limit_ref, match_ref,
    got_ref, other_ref, item_ref, mine_ref, theirs_ref, next_ref, dots, dual_scr, spend_scr
):
    duals = updated(duals_ref[...], totals(match_ref, got_ref, other_ref), limit_ref[...])
    next_ref[...] = duals
    dual_scr[...] = jnp.where(live_ref[...] > 0.5, duals * gain, masked)
    finish = spend_finish(where_ref, size_ref, user_ref.shape[1], fanout, spend_scr)
    sweep_users(where_ref, size_ref, user_ref, scale_ref, item_ref, item_scale_ref, dual_scr, dots, finish, fanout)
    halves(where_ref, spend_scr, mine_ref, theirs_ref)


def third_kernel(
    fanout, where_ref, size_ref, user_ref, scale_ref, duals_ref, live_ref, item_scale_ref, limit_ref, match_ref,
    got_ref, other_ref, item_ref, own_match_ref, got_one_ref, other_one_ref, own_dual_ref, own_limit_ref,
    user_dual_ref, own_out_ref, dots, dual_scr, row_scr
):
    duals = updated(duals_ref[...], totals(match_ref, got_ref, other_ref), limit_ref[...])
    dual_scr[...] = jnp.where(live_ref[...] > 0.5, duals * gain, masked)
    own = updated(own_dual_ref[...], totals(own_match_ref, got_one_ref, other_one_ref), own_limit_ref[...])
    own_out_ref[...] = updated(own, totals(own_match_ref, got_ref, other_ref), own_limit_ref[...])
    users = user_ref.shape[1]
    partial = []

    def finish(k, start, rows, weights, den, sums):
        if start is None:
            return 0
        lanes = 128
        offset = start % lanes
        wide = jnp.broadcast_to(den, (rows, lanes))
        eye = offset + lax.broadcasted_iota(jnp.int32, (rows, lanes), 0) == lax.broadcasted_iota(
            jnp.int32, (rows, lanes), 1
        )
        row = jnp.sum(jnp.where(eye, wide, 0.0), axis=0, keepdims=True)
        if offset:
            row = row + partial.pop()
        if offset + rows < lanes:
            partial.append(row)
            return sums
        base = start - offset
        place = where_ref[1] * users + base + lax.broadcasted_iota(jnp.int32, (1, lanes), 1)
        row_scr[k, base // lanes : base // lanes + 1, :] = jnp.where(
            place < size_ref[k], temper * jnp.log(row), 0.0
        )
        return sums

    sweep_users(where_ref, size_ref, user_ref, scale_ref, item_ref, item_scale_ref, dual_scr, dots, finish, fanout)
    for n in range(row_scr.shape[1]):
        user_dual_ref[:, n * 128 : (n + 1) * 128] = row_scr[:, n, :]


def body(
    user_emb, elig_owner, elig_local, cluster_size, camp_emb, camp_count, dual_init, spend_limit
):
    shards = lax.axis_size("shard")
    reps = lax.axis_size("rep")
    me = lax.axis_index("shard").astype(jnp.int32)
    rep = lax.axis_index("rep").astype(jnp.int32)
    clusters, users, width = user_emb.shape
    blocks, camps, _ = camp_emb.shape
    fanout = elig_owner.shape[1]
    items = clusters * fanout
    cap = 2 * items // shards
    half = cap // reps
    part = items // reps
    swap = [(0, 1), (1, 0)]
    f32 = jnp.float32

    owners = elig_owner.reshape(-1)
    locals_ = elig_local.reshape(-1)
    shard_ids = jnp.arange(shards, dtype=jnp.int32)
    hot = (owners[:, None] == shard_ids[None, :]).astype(jnp.int32)
    rank = jnp.sum((jnp.cumsum(hot, axis=0) - hot) * hot, axis=1)
    slot = owners * cap + rank
    hit = slot[:, None] == jnp.arange(shards * cap, dtype=jnp.int32)[None, :]
    wanted = jnp.sum(jnp.where(hit, locals_[:, None], 0), axis=0).reshape(shards, cap)
    names = owners * blocks + locals_
    ask = jnp.concatenate([wanted, jnp.broadcast_to(names[None, :], (shards, items))], axis=1)
    heard = lax.all_to_all(ask, "shard", split_axis=0, concat_axis=0, tiled=True)
    where = jnp.stack([me, rep])

    sent = pl.pallas_call(
        functools.partial(gather_kernel, half),
        out_shape=[jax.ShapeDtypeStruct((half, camps, width), camp_emb.dtype)] * (shards - 1),
        in_specs=[SMEM, SMEM, ANY],
        out_specs=[VMEM] * (shards - 1),
        scratch_shapes=[pltpu.SemaphoreType.DMA(((shards - 1) * half,))],
        cost_estimate=pl.CostEstimate(flops=0, bytes_accessed=8 * 2**20, transcendentals=0),
    )(where, heard, camp_emb)

    received = []
    for n in range(shards - 1):
        got = lax.ppermute(sent[n], "shard", [(i, i ^ (n + 1)) for i in range(shards)])
        received += [got, lax.ppermute(got, "rep", swap)]

    incoming = lax.dynamic_slice_in_dim(heard[:, :cap], rep * half, half, 1)
    all_names = heard[:, cap:]
    item_of_slot = (
        jnp.sum(
            jnp.where(
                ((owners ^ me) * cap + rank)[:, None] == jnp.arange(shards * cap, dtype=jnp.int32)[None, :],
                jnp.arange(1, items + 1, dtype=jnp.int32)[:, None],
                0,
            ),
            axis=0,
        )
        - 1
    )
    own_wanted = lax.dynamic_slice_in_dim(wanted, me, 1, 0).reshape(cap)
    camp_scale = lax.rsqrt(jnp.mean(jnp.square(camp_emb.astype(f32)), axis=-1) + epsilon)
    live = (jnp.arange(camps, dtype=jnp.int32)[None, :] < camp_count[:, None]).astype(f32)
    table = jnp.concatenate([dual_init, spend_limit, camp_scale, live], axis=1)
    facts = jnp.take(table, incoming.reshape(-1), axis=0, mode="clip").reshape(shards, half, 4 * camps)
    facts = lax.all_to_all(facts, "shard", split_axis=0, concat_axis=0, tiled=True)
    other_facts = lax.ppermute(facts, "rep", swap)
    pair = jnp.stack([facts, other_facts]).reshape(reps * shards * half, 4 * camps)
    spot = (rank // half ^ rep) * (shards * half) + owners * half + rank % half
    item_facts = jnp.take(pair, spot, axis=0, mode="clip")
    item_dual, item_limit, item_scale, item_live = (
        item_facts[:, n * camps : (n + 1) * camps] for n in range(4)
    )
    user_scale = (sharpness / width * gain) * lax.rsqrt(
        jnp.mean(jnp.square(user_emb.astype(f32)), axis=-1, keepdims=True) + epsilon
    )
    user_scale = jnp.broadcast_to(user_scale, (clusters, users, camps))

    def columns(which):
        return lax.dynamic_slice_in_dim(all_names, which * part, part, 1).reshape(1, -1)

    sides = (columns(rep), columns(1 - rep))
    own_names = me * blocks + jnp.arange(blocks, dtype=jnp.int32)
    match = jnp.stack([(names[:, None] == side).astype(jnp.bfloat16) for side in sides])
    own_match = jnp.stack([(own_names[:, None] == side).astype(jnp.bfloat16) for side in sides])

    def exchange(mine, theirs):
        total = mine + lax.ppermute(theirs, "rep", swap)
        spread = jnp.broadcast_to(total.astype(jnp.bfloat16)[None], (shards, part, camps))
        got = lax.all_to_all(spread, "shard", split_axis=0, concat_axis=0, tiled=True)
        got = got.reshape(shards * part, camps)
        return got, lax.ppermute(got, "rep", swap)

    spend_out = [jax.ShapeDtypeStruct((part, camps), f32)] * 2
    work = [pltpu.VMEM((users, fanout * camps), f32), pltpu.VMEM((items, camps), f32)]
    spend_work = [pltpu.VMEM((items, camps), f32)]

    mine, theirs, item_emb = pl.pallas_call(
        functools.partial(first_kernel, shards, half, fanout),
        out_shape=spend_out + [jax.ShapeDtypeStruct((items, camps, width), camp_emb.dtype)],
        in_specs=[SMEM] * 4 + [VMEM] * 5 + [ANY] * (1 + len(received)),
        out_specs=[VMEM] * 3,
        scratch_shapes=work + spend_work + [pltpu.SemaphoreType.DMA((items,))],
    )(where, cluster_size, item_of_slot, own_wanted, user_emb, user_scale, item_dual, item_live, item_scale,
      camp_emb, *received)
    got_one, other_one = exchange(mine, theirs)

    mine, theirs, next_dual = pl.pallas_call(
        functools.partial(second_kernel, fanout),
        out_shape=spend_out + [jax.ShapeDtypeStruct((items, camps), f32)],
        in_specs=[SMEM] * 2 + [VMEM] * 10,
        out_specs=[VMEM] * 3,
        scratch_shapes=work + spend_work,
    )(where, cluster_size, user_emb, user_scale, item_dual, item_live, item_scale, item_limit, match,
      got_one, other_one, item_emb)
    got_two, other_two = exchange(mine, theirs)

    user_dual, own_dual = pl.pallas_call(
        functools.partial(third_kernel, fanout),
        out_shape=[
            jax.ShapeDtypeStruct((clusters, users), f32),
            jax.ShapeDtypeStruct((blocks, camps), f32),
        ],
        in_specs=[SMEM] * 2 + [VMEM] * 15,
        out_specs=[VMEM] * 2,
        scratch_shapes=work + [pltpu.VMEM((clusters, users // 128, 128), f32)],
    )(where, cluster_size, user_emb, user_scale, next_dual, item_live, item_scale, item_limit, match,
      got_two, other_two, item_emb, own_match, got_one, other_one, dual_init, spend_limit)
    return (user_dual, own_dual)


def solution(mesh):
    return jax.shard_map(
        body,
        mesh=mesh,
        in_specs=(
            P("shard", "rep", None),
            P("shard", None),
            P("shard", None),
            P("shard"),
            P("shard", None, None),
            P("shard"),
            P("shard", None),
            P("shard", None),
        ),
        out_specs=(P("shard", "rep"), P("shard", None)),
        check_vma=False,
    )
```

```python
import functools
import math

import jax
import jax.numpy as jnp
from jax import lax
from jax.experimental import pallas as pl
from jax.experimental.pallas import tpu as pltpu
from jax.sharding import PartitionSpec as P

epsilon = 1e-06
temper = 0.25
sharpness = 16.0
gain = 1.0 / (temper * math.log(2.0))
masked = 1e30


VMEM = pl.BlockSpec(memory_space=pltpu.VMEM)
SMEM = pl.BlockSpec(memory_space=pltpu.SMEM)
ANY = pl.BlockSpec(memory_space=pl.ANY)


def gather_kernel(half, where_ref, asked_ref, camp_ref, *rest):
    outs, sem = rest[:-1], rest[-1]
    me, rep = where_ref[0], where_ref[1]
    copies = []
    for n, out in enumerate(outs):
        for j in range(half):
            block = asked_ref[me ^ (n + 1), rep * half + j]
            copies.append(pltpu.make_async_copy(camp_ref.at[block], out.at[j], sem.at[n * half + j]))
    for copy in copies:
        copy.start()
    for copy in copies:
        copy.wait()


def updated(duals, spend, limit):
    return jnp.maximum(0.0, duals + temper * jnp.log((spend + limit) / (2.0 * limit)))


def totals(match_ref, mine_ref, other_ref):
    return jnp.dot(
        match_ref[0], mine_ref[...], preferred_element_type=jnp.float32
    ) + jnp.dot(match_ref[1], other_ref[...], preferred_element_type=jnp.float32)


def sweep_users(where_ref, size_ref, user_ref, scale_ref, item_ref, item_scale_ref, dual_scr, dots_a, dots_b, finish, fanout):
    clusters, users, _ = user_ref.shape
    camps = item_ref.shape[1]
    width = item_ref.shape[2]
    rows = 64

    def multiply(k, dots):
        blocks = item_ref[pl.ds(pl.multiple_of(k * fanout, fanout), fanout)].reshape(fanout * camps, width)
        dots[...] = lax.dot_general(
            user_ref[k], blocks, (((1,), (1,)), ((), ())), preferred_element_type=jnp.float32
        )

    def cluster(k, dots):
        first = pl.multiple_of(k * fanout, fanout)
        item_scale = item_scale_ref[pl.ds(first, fanout), :]
        shift = dual_scr[pl.ds(first, fanout), :]
        scales = [jnp.broadcast_to(item_scale[e : e + 1], (rows, camps)) for e in range(fanout)]
        shifts = [jnp.broadcast_to(shift[e : e + 1], (rows, camps)) for e in range(fanout)]
        sums = [jnp.zeros((8, camps), jnp.float32) for _ in range(fanout)]
        for start in range(0, users, rows):
            user_scale = scale_ref[k, start : start + rows, :]
            weights = []
            for e in range(fanout):
                raw = dots[start : start + rows, e * camps : (e + 1) * camps]
                weights.append(jnp.exp2(raw * user_scale * scales[e] - shifts[e]))
            den = 1.0 + jnp.sum(functools.reduce(jnp.add, weights), axis=1, keepdims=True)
            sums = finish(k, start, rows, weights, den, sums)
        finish(k, None, rows, None, None, sums)

    multiply(0, dots_a)

    def two(n, carry):
        k = 2 * n
        multiply(k + 1, dots_b)
        cluster(k, dots_a)
        multiply(jnp.minimum(k + 2, clusters - 1), dots_a)
        cluster(k + 1, dots_b)
        return carry

    lax.fori_loop(0, clusters // 2, two, 0)


def spend_finish(where_ref, size_ref, users, fanout, spend_scr):
    def finish(k, start, rows, weights, den, sums):
        if start is None:
            for e in range(fanout):
                spend_scr[pl.ds(k * fanout + e, 1), :] = jnp.sum(sums[e], axis=0, keepdims=True)
            return 0
        place = where_ref[1] * users + start + lax.broadcasted_iota(jnp.int32, (rows, 1), 0)
        share = jnp.where(place < size_ref[k], 1.0 / den, 0.0)
        out = []
        for e in range(fanout):
            part = weights[e] * share
            total = sums[e]
            for r in range(0, rows, 8):
                total = total + part[r : r + 8]
            out.append(total)
        return out

    return finish


def halves(where_ref, spend_scr, mine_ref, theirs_ref):
    count = mine_ref.shape[0]
    rep = where_ref[1]
    mine_ref[...] = spend_scr[pl.ds(pl.multiple_of(rep * count, count), count), :]
    theirs_ref[...] = spend_scr[pl.ds(pl.multiple_of((1 - rep) * count, count), count), :]


def first_kernel(
    shards, half, fanout, where_ref, size_ref, item_at_ref, own_ref, user_ref, scale_ref, duals_ref, live_ref,
    item_scale_ref, camp_ref, *rest
):
    received, (mine_ref, theirs_ref, item_ref), (dots_a, dots_b, dual_scr, spend_scr, sem) = (
        rest[: 2 * (shards - 1)], rest[-8:-5], rest[-5:]
    )
    cap = 2 * half
    rep = where_ref[1]
    users = user_ref.shape[1]

    def fetch(slot, source):
        item = item_at_ref[slot]

        @pl.when(item >= 0)
        def _():
            pltpu.make_async_copy(source, item_ref.at[item], sem.at[item]).start()

    for j in range(cap):
        fetch(j, camp_ref.at[own_ref[j]])
    for n in range(shards - 1):
        for j in range(half):
            fetch((n + 1) * cap + rep * half + j, received[2 * n].at[j])
            fetch((n + 1) * cap + (1 - rep) * half + j, received[2 * n + 1].at[j])
    dual_scr[...] = jnp.where(live_ref[...] > 0.5, duals_ref[...] * gain, masked)

    def landed(item, carry):
        pltpu.make_async_copy(camp_ref.at[0], item_ref.at[item], sem.at[item]).wait()
        return carry

    lax.fori_loop(0, item_ref.shape[0], landed, 0)
    finish = spend_finish(where_ref, size_ref, users, fanout, spend_scr)
    sweep_users(where_ref, size_ref, user_ref, scale_ref, item_ref, item_scale_ref, dual_scr, dots_a, dots_b, finish, fanout)
    halves(where_ref, spend_scr, mine_ref, theirs_ref)


def second_kernel(
    fanout, where_ref, size_ref, user_ref, scale_ref, duals_ref, live_ref, item_scale_ref, limit_ref, match_ref,
    got_ref, other_ref, item_ref, mine_ref, theirs_ref, next_ref, dots_a, dots_b, dual_scr, spend_scr
):
    duals = updated(duals_ref[...], totals(match_ref, got_ref, other_ref), limit_ref[...])
    next_ref[...] = duals
    dual_scr[...] = jnp.where(live_ref[...] > 0.5, duals * gain, masked)
    finish = spend_finish(where_ref, size_ref, user_ref.shape[1], fanout, spend_scr)
    sweep_users(where_ref, size_ref, user_ref, scale_ref, item_ref, item_scale_ref, dual_scr, dots_a, dots_b, finish, fanout)
    halves(where_ref, spend_scr, mine_ref, theirs_ref)


def third_kernel(
    fanout, where_ref, size_ref, user_ref, scale_ref, duals_ref, live_ref, item_scale_ref, limit_ref, match_ref,
    got_ref, other_ref, item_ref, own_match_ref, got_one_ref, other_one_ref, own_dual_ref, own_limit_ref,
    user_dual_ref, own_out_ref, dots_a, dots_b, dual_scr, row_scr
):
    duals = updated(duals_ref[...], totals(match_ref, got_ref, other_ref), limit_ref[...])
    dual_scr[...] = jnp.where(live_ref[...] > 0.5, duals * gain, masked)
    own = updated(own_dual_ref[...], totals(own_match_ref, got_one_ref, other_one_ref), own_limit_ref[...])
    own_out_ref[...] = updated(own, totals(own_match_ref, got_ref, other_ref), own_limit_ref[...])
    users = user_ref.shape[1]
    partial = []

    def finish(k, start, rows, weights, den, sums):
        if start is None:
            return 0
        lanes = 128
        offset = start % lanes
        wide = jnp.broadcast_to(den, (rows, lanes))
        eye = offset + lax.broadcasted_iota(jnp.int32, (rows, lanes), 0) == lax.broadcasted_iota(
            jnp.int32, (rows, lanes), 1
        )
        row = jnp.sum(jnp.where(eye, wide, 0.0), axis=0, keepdims=True)
        if offset:
            row = row + partial.pop()
        if offset + rows < lanes:
            partial.append(row)
            return sums
        base = start - offset
        place = where_ref[1] * users + base + lax.broadcasted_iota(jnp.int32, (1, lanes), 1)
        row_scr[k, base // lanes : base // lanes + 1, :] = jnp.where(
            place < size_ref[k], temper * jnp.log(row), 0.0
        )
        return sums

    sweep_users(where_ref, size_ref, user_ref, scale_ref, item_ref, item_scale_ref, dual_scr, dots_a, dots_b, finish, fanout)
    for n in range(row_scr.shape[1]):
        user_dual_ref[:, n * 128 : (n + 1) * 128] = row_scr[:, n, :]


def body(
    user_emb, elig_owner, elig_local, cluster_size, camp_emb, camp_count, dual_init, spend_limit
):
    shards = lax.axis_size("shard")
    reps = lax.axis_size("rep")
    me = lax.axis_index("shard").astype(jnp.int32)
    rep = lax.axis_index("rep").astype(jnp.int32)
    clusters, users, width = user_emb.shape
    blocks, camps, _ = camp_emb.shape
    fanout = elig_owner.shape[1]
    items = clusters * fanout
    cap = 2 * items // shards
    half = cap // reps
    part = items // reps
    swap = [(0, 1), (1, 0)]
    f32 = jnp.float32

    owners = elig_owner.reshape(-1)
    locals_ = elig_local.reshape(-1)
    shard_ids = jnp.arange(shards, dtype=jnp.int32)
    hot = (owners[:, None] == shard_ids[None, :]).astype(jnp.int32)
    rank = jnp.sum((jnp.cumsum(hot, axis=0) - hot) * hot, axis=1)
    slot = owners * cap + rank
    hit = slot[:, None] == jnp.arange(shards * cap, dtype=jnp.int32)[None, :]
    wanted = jnp.sum(jnp.where(hit, locals_[:, None], 0), axis=0).reshape(shards, cap)
    names = owners * blocks + locals_
    ask = jnp.concatenate([wanted, jnp.broadcast_to(names[None, :], (shards, items))], axis=1)
    heard = lax.all_to_all(ask, "shard", split_axis=0, concat_axis=0, tiled=True)
    where = jnp.stack([me, rep])

    sent = pl.pallas_call(
        functools.partial(gather_kernel, half),
        out_shape=[jax.ShapeDtypeStruct((half, camps, width), camp_emb.dtype)] * (shards - 1),
        in_specs=[SMEM, SMEM, ANY],
        out_specs=[VMEM] * (shards - 1),
        scratch_shapes=[pltpu.SemaphoreType.DMA(((shards - 1) * half,))],
        cost_estimate=pl.CostEstimate(flops=0, bytes_accessed=8 * 2**20, transcendentals=0),
    )(where, heard, camp_emb)

    received = []
    for n in range(shards - 1):
        got = lax.ppermute(sent[n], "shard", [(i, i ^ (n + 1)) for i in range(shards)])
        received += [got, lax.ppermute(got, "rep", swap)]

    heard, camp_late, user_late, _ = lax.optimization_barrier((heard, camp_emb, user_emb, sent[0]))
    incoming = lax.dynamic_slice_in_dim(heard[:, :cap], rep * half, half, 1)
    all_names = heard[:, cap:]
    item_of_slot = (
        jnp.sum(
            jnp.where(
                ((owners ^ me) * cap + rank)[:, None] == jnp.arange(shards * cap, dtype=jnp.int32)[None, :],
                jnp.arange(1, items + 1, dtype=jnp.int32)[:, None],
                0,
            ),
            axis=0,
        )
        - 1
    )
    own_wanted = lax.dynamic_slice_in_dim(wanted, me, 1, 0).reshape(cap)
    camp_scale = lax.rsqrt(jnp.mean(jnp.square(camp_late.astype(f32)), axis=-1) + epsilon)
    live = (jnp.arange(camps, dtype=jnp.int32)[None, :] < camp_count[:, None]).astype(f32)
    table = jnp.concatenate([dual_init, spend_limit, camp_scale, live], axis=1)
    facts = jnp.take(table, incoming.reshape(-1), axis=0, mode="clip").reshape(shards, half, 4 * camps)
    facts = lax.all_to_all(facts, "shard", split_axis=0, concat_axis=0, tiled=True)
    other_facts = lax.ppermute(facts, "rep", swap)
    pair = jnp.stack([facts, other_facts]).reshape(reps * shards * half, 4 * camps)
    spot = (rank // half ^ rep) * (shards * half) + owners * half + rank % half
    item_facts = jnp.take(pair, spot, axis=0, mode="clip")
    item_dual, item_limit, item_scale, item_live = (
        item_facts[:, n * camps : (n + 1) * camps] for n in range(4)
    )
    user_scale = (sharpness / width * gain) * lax.rsqrt(
        jnp.mean(jnp.square(user_late.astype(f32)), axis=-1, keepdims=True) + epsilon
    )
    user_scale = jnp.broadcast_to(user_scale, (clusters, users, camps))

    def columns(which):
        return lax.dynamic_slice_in_dim(all_names, which * part, part, 1).reshape(1, -1)

    sides = (columns(rep), columns(1 - rep))
    own_names = me * blocks + jnp.arange(blocks, dtype=jnp.int32)
    match = jnp.stack([(names[:, None] == side).astype(jnp.bfloat16) for side in sides])
    own_match = jnp.stack([(own_names[:, None] == side).astype(jnp.bfloat16) for side in sides])

    def exchange(mine, theirs):
        total = mine + lax.ppermute(theirs, "rep", swap)
        spread = jnp.broadcast_to(total.astype(jnp.bfloat16)[None], (shards, part, camps))
        got = lax.all_to_all(spread, "shard", split_axis=0, concat_axis=0, tiled=True)
        got = got.reshape(shards * part, camps)
        return got, lax.ppermute(got, "rep", swap)

    spend_out = [jax.ShapeDtypeStruct((part, camps), f32)] * 2
    work = [pltpu.VMEM((users, fanout * camps), f32)] * 2 + [pltpu.VMEM((items, camps), f32)]
    spend_work = [pltpu.VMEM((items, camps), f32)]

    mine, theirs, item_emb = pl.pallas_call(
        functools.partial(first_kernel, shards, half, fanout),
        out_shape=spend_out + [jax.ShapeDtypeStruct((items, camps, width), camp_emb.dtype)],
        in_specs=[SMEM] * 4 + [VMEM] * 5 + [ANY] * (1 + len(received)),
        out_specs=[VMEM] * 3,
        scratch_shapes=work + spend_work + [pltpu.SemaphoreType.DMA((items,))],
    )(where, cluster_size, item_of_slot, own_wanted, user_emb, user_scale, item_dual, item_live, item_scale,
      camp_emb, *received)
    got_one, other_one = exchange(mine, theirs)

    mine, theirs, next_dual = pl.pallas_call(
        functools.partial(second_kernel, fanout),
        out_shape=spend_out + [jax.ShapeDtypeStruct((items, camps), f32)],
        in_specs=[SMEM] * 2 + [VMEM] * 10,
        out_specs=[VMEM] * 3,
        scratch_shapes=work + spend_work,
    )(where, cluster_size, user_emb, user_scale, item_dual, item_live, item_scale, item_limit, match,
      got_one, other_one, item_emb)
    got_two, other_two = exchange(mine, theirs)

    user_dual, own_dual = pl.pallas_call(
        functools.partial(third_kernel, fanout),
        out_shape=[
            jax.ShapeDtypeStruct((clusters, users), f32),
            jax.ShapeDtypeStruct((blocks, camps), f32),
        ],
        in_specs=[SMEM] * 2 + [VMEM] * 15,
        out_specs=[VMEM] * 2,
        scratch_shapes=work + [pltpu.VMEM((clusters, users // 128, 128), f32)],
    )(where, cluster_size, user_emb, user_scale, next_dual, item_live, item_scale, item_limit, match,
      got_two, other_two, item_emb, own_match, got_one, other_one, dual_init, spend_limit)
    return (user_dual, own_dual)


def solution(mesh):
    return jax.shard_map(
        body,
        mesh=mesh,
        in_specs=(
            P("shard", "rep", None),
            P("shard", None),
            P("shard", None),
            P("shard"),
            P("shard", None, None),
            P("shard"),
            P("shard", None),
            P("shard", None),
        ),
        out_specs=(P("shard", "rep"), P("shard", None)),
        check_vma=False,
    )
```

```python
import functools
import math

import jax
import jax.numpy as jnp
from jax import lax
from jax.experimental import pallas as pl
from jax.experimental.pallas import tpu as pltpu
from jax.sharding import PartitionSpec as P


epsilon = 1e-06
temper = 0.25
sharpness = 16.0
gain = 1.0 / (temper * math.log(2.0))
masked = 1e30


VMEM = pl.BlockSpec(memory_space=pltpu.VMEM)
SMEM = pl.BlockSpec(memory_space=pltpu.SMEM)
ANY = pl.BlockSpec(memory_space=pl.ANY)
HBM = pl.BlockSpec(memory_space=pltpu.HBM)


def in_hbm(x):
    return pltpu.with_memory_space_constraint(x, pltpu.HBM)


def in_vmem(x):
    return pltpu.with_memory_space_constraint(x, pltpu.VMEM)


def send_order(shards):
    top = shards // 2
    far = [top + n for n in range(top)]
    first = far[: top // 2]
    return first + list(range(1, top)) + far[top // 2 :]


def gather_kernel(half, where_ref, asked_ref, camp_ref, *rest):
    outs, sem = rest[:-1], rest[-1]
    me, rep = where_ref[0], where_ref[1]
    copies = []
    for n, out in enumerate(outs):
        for j in range(half):
            block = asked_ref[me ^ (n + 1), rep * half + j]
            copies.append(pltpu.make_async_copy(camp_ref.at[block], out.at[j], sem.at[n * half + j]))
    for copy in copies:
        copy.start()
    for copy in copies:
        copy.wait()


def user_kernel(user_ref, scale_ref):
    rows = user_ref[0].astype(jnp.float32)
    scale = lax.rsqrt(jnp.sum(rows * rows, axis=1, keepdims=True) * (1.0 / rows.shape[1]) + epsilon)
    scale_ref[0] = jnp.broadcast_to(scale * (sharpness / rows.shape[1] * gain), scale_ref.shape[1:])


def updated(duals, spend, limit):
    return jnp.maximum(0.0, duals + temper * jnp.log((spend + limit) / (2.0 * limit)))


def totals(match_ref, mine_ref, other_ref):
    return jnp.dot(
        match_ref[0], mine_ref[...], preferred_element_type=jnp.float32
    ) + jnp.dot(match_ref[1], other_ref[...], preferred_element_type=jnp.float32)


def start_rows(user_hbm, scale_hbm, user_ref, scale_ref, sem):
    def start(k, carry):
        pltpu.make_async_copy(user_hbm.at[k], user_ref.at[k], sem.at[0, k]).start()
        pltpu.make_async_copy(scale_hbm.at[k], scale_ref.at[k], sem.at[1, k]).start()
        return carry

    lax.fori_loop(0, user_ref.shape[0], start, 0)


def start_items(item_hbm, item_ref, sem):
    def start(k, carry):
        pltpu.make_async_copy(item_hbm.at[k], item_ref.at[k], sem.at[k]).start()
        return carry

    lax.fori_loop(0, item_ref.shape[0], start, 0)


def sweep_users(
    user_hbm, scale_hbm, user_ref, scale_ref, item_ref, row_sem, item_sem, item_scale_ref, dual_scr,
    dots_a, dots_b, finish, fanout
):
    clusters, users, _ = user_ref.shape
    camps = item_ref.shape[1]
    width = item_ref.shape[2]
    rows = 64

    def landed(k):
        pltpu.make_async_copy(user_hbm.at[k], user_ref.at[k], row_sem.at[0, k]).wait()
        pltpu.make_async_copy(scale_hbm.at[k], scale_ref.at[k], row_sem.at[1, k]).wait()
        for e in range(fanout):
            item = k * fanout + e
            pltpu.make_async_copy(item_ref.at[item], item_ref.at[item], item_sem.at[item]).wait()

    def multiply(k, dots):
        blocks = item_ref[pl.ds(pl.multiple_of(k * fanout, fanout), fanout)].reshape(fanout * camps, width)
        dots[...] = lax.dot_general(
            user_ref[k], blocks, (((1,), (1,)), ((), ())), preferred_element_type=jnp.float32
        )

    def cluster(k, dots):
        first = pl.multiple_of(k * fanout, fanout)
        item_scale = item_scale_ref[pl.ds(first, fanout), :]
        shift = dual_scr[pl.ds(first, fanout), :]
        scales = [jnp.broadcast_to(item_scale[e : e + 1], (rows, camps)) for e in range(fanout)]
        shifts = [jnp.broadcast_to(shift[e : e + 1], (rows, camps)) for e in range(fanout)]
        sums = [jnp.zeros((8, camps), jnp.float32) for _ in range(fanout)]
        for start in range(0, users, rows):
            user_scale = scale_ref[k, start : start + rows, :]
            weights = []
            for e in range(fanout):
                raw = dots[start : start + rows, e * camps : (e + 1) * camps]
                weights.append(jnp.exp2(raw * user_scale * scales[e] - shifts[e]))
            den = 1.0 + jnp.sum(functools.reduce(jnp.add, weights), axis=1, keepdims=True)
            sums = finish(k, start, rows, weights, den, sums)
        finish(k, None, rows, None, None, sums)

    landed(0)
    multiply(0, dots_a)

    def two(n, carry):
        k = 2 * n
        landed(k + 1)

        @pl.when(k + 2 < clusters)
        def _():
            landed(k + 2)

        multiply(k + 1, dots_b)
        cluster(k, dots_a)
        multiply(jnp.minimum(k + 2, clusters - 1), dots_a)
        cluster(k + 1, dots_b)
        return carry

    lax.fori_loop(0, clusters // 2, two, 0)


def spend_finish(where_ref, size_ref, users, fanout, spend_scr):
    def finish(k, start, rows, weights, den, sums):
        if start is None:
            for e in range(fanout):
                spend_scr[pl.ds(k * fanout + e, 1), :] = jnp.sum(sums[e], axis=0, keepdims=True)
            return 0
        place = where_ref[1] * users + start + lax.broadcasted_iota(jnp.int32, (rows, 1), 0)
        share = jnp.where(place < size_ref[k], 1.0 / den, 0.0)
        out = []
        for e in range(fanout):
            part = weights[e] * share
            total = sums[e]
            for r in range(0, rows, 8):
                total = total + part[r : r + 8]
            out.append(total)
        return out

    return finish


def halves(where_ref, spend_scr, mine_ref, theirs_ref):
    count = mine_ref.shape[0]
    rep = where_ref[1]
    mine_ref[...] = spend_scr[pl.ds(pl.multiple_of(rep * count, count), count), :]
    theirs_ref[...] = spend_scr[pl.ds(pl.multiple_of((1 - rep) * count, count), count), :]


def first_kernel(
    shards, half, fanout, where_ref, size_ref, item_at_ref, own_ref, duals_ref, live_ref, item_scale_ref, user_hbm,
    scale_hbm, camp_ref, *rest
):
    received, (mine_ref, theirs_ref, item_out) = rest[: 2 * (shards - 1)], rest[2 * (shards - 1) :][:3]
    user_ref, scale_ref, item_ref, row_sem, item_sem, dots_a, dots_b, dual_scr, spend_scr, out_sem = rest[-10:]
    cap = 2 * half
    rep = where_ref[1]
    users = user_ref.shape[1]

    def fetch(slot, source):
        item = item_at_ref[slot]

        @pl.when(item >= 0)
        def _():
            pltpu.make_async_copy(source, item_ref.at[item], item_sem.at[item]).start()

    for j in range(cap):
        fetch(j, camp_ref.at[own_ref[j]])
    for n in range(shards - 1):
        for j in range(half):
            fetch((n + 1) * cap + rep * half + j, received[2 * n].at[j])
            fetch((n + 1) * cap + (1 - rep) * half + j, received[2 * n + 1].at[j])
    start_rows(user_hbm, scale_hbm, user_ref, scale_ref, row_sem)
    dual_scr[...] = jnp.where(live_ref[...] > 0.5, duals_ref[...] * gain, masked)
    finish = spend_finish(where_ref, size_ref, users, fanout, spend_scr)
    sweep_users(
        user_hbm, scale_hbm, user_ref, scale_ref, item_ref, row_sem, item_sem, item_scale_ref,
        dual_scr, dots_a, dots_b, finish, fanout
    )
    keep = pltpu.make_async_copy(item_ref, item_out, out_sem)
    keep.start()
    halves(where_ref, spend_scr, mine_ref, theirs_ref)
    keep.wait()


def second_kernel(
    fanout, where_ref, size_ref, duals_ref, live_ref, item_scale_ref, limit_ref, match_ref, got_ref, other_ref,
    user_hbm, scale_hbm, item_hbm, mine_ref, theirs_ref, next_ref, user_ref, scale_ref, item_ref, row_sem, item_sem,
    dots_a, dots_b, dual_scr, spend_scr
):
    start_items(item_hbm, item_ref, item_sem)
    start_rows(user_hbm, scale_hbm, user_ref, scale_ref, row_sem)
    duals = updated(duals_ref[...], totals(match_ref, got_ref, other_ref), limit_ref[...])
    next_ref[...] = duals
    dual_scr[...] = jnp.where(live_ref[...] > 0.5, duals * gain, masked)
    finish = spend_finish(where_ref, size_ref, user_ref.shape[1], fanout, spend_scr)
    sweep_users(
        user_hbm, scale_hbm, user_ref, scale_ref, item_ref, row_sem, item_sem, item_scale_ref,
        dual_scr, dots_a, dots_b, finish, fanout
    )
    halves(where_ref, spend_scr, mine_ref, theirs_ref)


def third_kernel(
    fanout, where_ref, size_ref, duals_ref, live_ref, item_scale_ref, limit_ref, match_ref, got_ref, other_ref,
    own_match_ref, got_one_ref, other_one_ref, own_dual_ref, own_limit_ref, user_hbm, scale_hbm, item_hbm,
    user_dual_ref, own_out_ref, user_ref, scale_ref, item_ref, row_sem, item_sem, dots_a, dots_b, dual_scr, row_scr
):
    start_items(item_hbm, item_ref, item_sem)
    start_rows(user_hbm, scale_hbm, user_ref, scale_ref, row_sem)
    duals = updated(duals_ref[...], totals(match_ref, got_ref, other_ref), limit_ref[...])
    dual_scr[...] = jnp.where(live_ref[...] > 0.5, duals * gain, masked)
    own = updated(own_dual_ref[...], totals(own_match_ref, got_one_ref, other_one_ref), own_limit_ref[...])
    own_out_ref[...] = updated(own, totals(own_match_ref, got_ref, other_ref), own_limit_ref[...])
    users = user_ref.shape[1]
    partial = []

    def finish(k, start, rows, weights, den, sums):
        if start is None:
            return 0
        lanes = 128
        offset = start % lanes
        wide = jnp.broadcast_to(den, (rows, lanes))
        eye = offset + lax.broadcasted_iota(jnp.int32, (rows, lanes), 0) == lax.broadcasted_iota(
            jnp.int32, (rows, lanes), 1
        )
        row = jnp.sum(jnp.where(eye, wide, 0.0), axis=0, keepdims=True)
        if offset:
            row = row + partial.pop()
        if offset + rows < lanes:
            partial.append(row)
            return sums
        base = start - offset
        place = where_ref[1] * users + base + lax.broadcasted_iota(jnp.int32, (1, lanes), 1)
        row_scr[k, base // lanes : base // lanes + 1, :] = jnp.where(
            place < size_ref[k], temper * jnp.log(row), 0.0
        )
        return sums

    sweep_users(
        user_hbm, scale_hbm, user_ref, scale_ref, item_ref, row_sem, item_sem, item_scale_ref,
        dual_scr, dots_a, dots_b, finish, fanout
    )
    for n in range(row_scr.shape[1]):
        user_dual_ref[:, n * 128 : (n + 1) * 128] = row_scr[:, n, :]


def program(
    user_emb, elig_owner, elig_local, cluster_size, camp_emb, camp_count, dual_init, spend_limit
):
    shards = lax.axis_size("shard")
    reps = lax.axis_size("rep")
    me = lax.axis_index("shard").astype(jnp.int32)
    rep = lax.axis_index("rep").astype(jnp.int32)
    clusters, users, width = user_emb.shape
    blocks, camps, _ = camp_emb.shape
    fanout = elig_owner.shape[1]
    items = clusters * fanout
    cap = 2 * items // shards
    half = cap // reps
    part = items // reps
    swap = [(0, 1), (1, 0)]
    f32 = jnp.float32

    owners = elig_owner.reshape(-1)
    locals_ = elig_local.reshape(-1)
    shard_ids = jnp.arange(shards, dtype=jnp.int32)
    hot = (owners[:, None] == shard_ids[None, :]).astype(jnp.int32)
    rank = jnp.sum((jnp.cumsum(hot, axis=0) - hot) * hot, axis=1)
    slot = owners * cap + rank
    hit = slot[:, None] == jnp.arange(shards * cap, dtype=jnp.int32)[None, :]
    wanted = jnp.sum(jnp.where(hit, locals_[:, None], 0), axis=0).reshape(shards, cap)
    names = owners * blocks + locals_
    ask = jnp.concatenate([wanted, jnp.broadcast_to(names[None, :], (shards, items))], axis=1)
    heard = lax.all_to_all(ask, "shard", split_axis=0, concat_axis=0, tiled=True)
    where = jnp.stack([me, rep])

    sent = pl.pallas_call(
        functools.partial(gather_kernel, half),
        out_shape=[pltpu.VMEM((half, camps, width), camp_emb.dtype)] * (shards - 1),
        in_specs=[SMEM, SMEM, HBM],
        out_specs=[VMEM] * (shards - 1),
        scratch_shapes=[pltpu.SemaphoreType.DMA(((shards - 1) * half,))],
        compiler_params=pltpu.CompilerParams(vmem_limit_bytes=8 * 2**20),
        cost_estimate=pl.CostEstimate(flops=0, bytes_accessed=8 * 2**20, transcendentals=0),
    )(where, heard, in_hbm(camp_emb))

    got_blocks = []
    for n in range(shards - 1):
        got_blocks.append(lax.ppermute(sent[n], "shard", [(i, i ^ (n + 1)) for i in range(shards)]))

    heard, camp_late, user_late, _ = lax.optimization_barrier((heard, camp_emb, user_emb, got_blocks[0]))
    incoming = lax.dynamic_slice_in_dim(heard[:, :cap], rep * half, half, 1)
    all_names = heard[:, cap:]
    item_of_slot = (
        jnp.sum(
            jnp.where(
                ((owners ^ me) * cap + rank)[:, None] == jnp.arange(shards * cap, dtype=jnp.int32)[None, :],
                jnp.arange(1, items + 1, dtype=jnp.int32)[:, None],
                0,
            ),
            axis=0,
        )
        - 1
    )
    own_wanted = lax.dynamic_slice_in_dim(wanted, me, 1, 0).reshape(cap)
    camp_scale = lax.rsqrt(jnp.mean(jnp.square(camp_late.astype(f32)), axis=-1) + epsilon)
    live = (jnp.arange(camps, dtype=jnp.int32)[None, :] < camp_count[:, None]).astype(f32)
    table = jnp.concatenate([dual_init, spend_limit, camp_scale, live], axis=1)
    facts = jnp.take(table, incoming.reshape(-1), axis=0, mode="clip").reshape(shards, half, 4 * camps)
    facts = lax.all_to_all(facts, "shard", split_axis=0, concat_axis=0, tiled=True)
    other_facts = lax.ppermute(facts, "rep", swap)
    pair = jnp.stack([facts, other_facts]).reshape(reps * shards * half, 4 * camps)
    spot = (rank // half ^ rep) * (shards * half) + owners * half + rank % half
    item_facts = jnp.take(pair, spot, axis=0, mode="clip")
    item_dual, item_limit, item_scale, item_live = (
        item_facts[:, n * camps : (n + 1) * camps] for n in range(4)
    )
    user_scale = pl.pallas_call(
        user_kernel,
        out_shape=jax.ShapeDtypeStruct((clusters, users, camps), f32),
        grid=(clusters,),
        in_specs=[pl.BlockSpec((1, users, width), lambda k: (k, 0, 0))],
        out_specs=pl.BlockSpec((1, users, camps), lambda k: (k, 0, 0)),
        compiler_params=pltpu.CompilerParams(vmem_limit_bytes=16 * 2**20),
        cost_estimate=pl.CostEstimate(flops=8 * 2**20, bytes_accessed=8 * 2**20, transcendentals=0),
    )(user_late)

    def columns(which):
        return lax.dynamic_slice_in_dim(all_names, which * part, part, 1).reshape(1, -1)

    sides = (columns(rep), columns(1 - rep))
    own_names = me * blocks + jnp.arange(blocks, dtype=jnp.int32)
    match = jnp.stack([(names[:, None] == side).astype(jnp.bfloat16) for side in sides])
    own_match = jnp.stack([(own_names[:, None] == side).astype(jnp.bfloat16) for side in sides])

    last = send_order(shards)[-1] - 1
    (got_blocks[last], item_dual, item_limit, item_scale, item_live, user_scale, match, own_match) = (
        lax.optimization_barrier(
            (got_blocks[last], item_dual, item_limit, item_scale, item_live, user_scale, match, own_match)
        )
    )
    received = []
    for got in got_blocks:
        received += [got, lax.ppermute(got, "rep", swap)]
    user_rows, user_scale = in_hbm(user_emb), in_hbm(user_scale)

    def exchange(mine, theirs):
        total = mine + lax.ppermute(theirs, "rep", swap)
        spread = jnp.broadcast_to(total.astype(jnp.bfloat16)[None], (shards, part, camps))
        got = lax.all_to_all(spread, "shard", split_axis=0, concat_axis=0, tiled=True)
        got = got.reshape(shards * part, camps)
        return in_vmem(got), in_vmem(lax.ppermute(got, "rep", swap))

    spend_out = [jax.ShapeDtypeStruct((part, camps), f32)] * 2
    work = [
        pltpu.VMEM((clusters, users, width), user_emb.dtype),
        pltpu.VMEM((clusters, users, camps), f32),
        pltpu.VMEM((items, camps, width), camp_emb.dtype),
        pltpu.SemaphoreType.DMA((2, clusters)),
        pltpu.SemaphoreType.DMA((items,)),
        pltpu.VMEM((users, fanout * camps), f32),
        pltpu.VMEM((users, fanout * camps), f32),
        pltpu.VMEM((items, camps), f32),
    ]
    spend_work = [pltpu.VMEM((items, camps), f32)]
    limits = pltpu.CompilerParams(vmem_limit_bytes=24 * 2**20)

    mine, theirs, item_emb = pl.pallas_call(
        functools.partial(first_kernel, shards, half, fanout),
        out_shape=spend_out + [pltpu.HBM((items, camps, width), camp_emb.dtype)],
        in_specs=[SMEM] * 4 + [VMEM] * 3 + [HBM] * 3 + [ANY] * len(received),
        out_specs=[VMEM] * 2 + [HBM],
        scratch_shapes=work + spend_work + [pltpu.SemaphoreType.DMA],
        compiler_params=limits,
    )(where, cluster_size, item_of_slot, own_wanted, item_dual, item_live, item_scale, user_rows, user_scale,
      in_hbm(camp_emb), *received)
    item_emb = in_hbm(item_emb)
    got_one, other_one = exchange(mine, theirs)

    mine, theirs, next_dual = pl.pallas_call(
        functools.partial(second_kernel, fanout),
        out_shape=spend_out + [jax.ShapeDtypeStruct((items, camps), f32)],
        in_specs=[SMEM] * 2 + [VMEM] * 7 + [HBM] * 3,
        out_specs=[VMEM] * 3,
        scratch_shapes=work + spend_work,
        compiler_params=limits,
    )(where, cluster_size, item_dual, item_live, item_scale, item_limit, match, got_one, other_one, user_rows,
      user_scale, item_emb)
    got_two, other_two = exchange(mine, theirs)

    user_dual, own_dual = pl.pallas_call(
        functools.partial(third_kernel, fanout),
        out_shape=[
            jax.ShapeDtypeStruct((clusters, users), f32),
            jax.ShapeDtypeStruct((blocks, camps), f32),
        ],
        in_specs=[SMEM] * 2 + [VMEM] * 12 + [HBM] * 3,
        out_specs=[VMEM] * 2,
        scratch_shapes=work + [pltpu.VMEM((clusters, users // 128, 128), f32)],
        compiler_params=limits,
    )(where, cluster_size, next_dual, item_live, item_scale, item_limit, match, got_two, other_two, own_match,
      got_one, other_one, dual_init, spend_limit, user_rows, user_scale, item_emb)
    return (user_dual, own_dual)


def solution(mesh):
    return jax.shard_map(
        program,
        mesh=mesh,
        in_specs=(
            P("shard", "rep", None),
            P("shard", None),
            P("shard", None),
            P("shard"),
            P("shard", None, None),
            P("shard"),
            P("shard", None),
            P("shard", None),
        ),
        out_specs=(P("shard", "rep"), P("shard", None)),
        check_vma=False,
    )
```

```python
import functools
import math

import jax
import jax.numpy as jnp
from jax import lax
from jax.experimental import pallas as pl
from jax.experimental.pallas import tpu as pltpu
from jax.sharding import PartitionSpec as P


epsilon = 1e-06
temper = 0.25
sharpness = 16.0
gain = 1.0 / (temper * math.log(2.0))
masked = 1e30


VMEM = pl.BlockSpec(memory_space=pltpu.VMEM)
SMEM = pl.BlockSpec(memory_space=pltpu.SMEM)
ANY = pl.BlockSpec(memory_space=pl.ANY)
HBM = pl.BlockSpec(memory_space=pltpu.HBM)


def in_hbm(x):
    return pltpu.with_memory_space_constraint(x, pltpu.HBM)


def in_vmem(x):
    return pltpu.with_memory_space_constraint(x, pltpu.VMEM)


def send_order(shards):
    top = shards // 2
    far = [top + n for n in range(top)]
    first = far[: top // 2]
    return first + list(range(1, top)) + far[top // 2 :]


def gather_kernel(half, shifts, where_ref, asked_ref, camp_ref, fact_ref, *rest):
    outs, (stage, sem) = rest[:-2], rest[-2:]
    me, rep = where_ref[0], where_ref[1]
    camps = camp_ref.shape[1]
    arriving, leaving = [], []
    for n, (shift, out) in enumerate(zip(shifts, outs)):
        for j in range(half):
            at = n * half + j
            block = asked_ref[me ^ shift, rep * half + j]
            for part, source, rows in (
                (0, camp_ref, pl.ds(0, camps)),
                (1, fact_ref, pl.ds(camps, fact_ref.shape[1])),
            ):
                copy = pltpu.make_async_copy(source.at[block], stage.at[at, rows], sem.at[part, at])
                copy.start()
                arriving.append(copy)
            leaving.append(pltpu.make_async_copy(stage.at[at], out.at[j], sem.at[2, at]))
    for at, copy in enumerate(leaving):
        arriving[2 * at].wait()
        arriving[2 * at + 1].wait()
        copy.start()
    for copy in leaving:
        copy.wait()


def user_kernel(user_ref, scale_ref):
    rows = user_ref[0].astype(jnp.float32)
    scale = lax.rsqrt(jnp.sum(rows * rows, axis=1, keepdims=True) * (1.0 / rows.shape[1]) + epsilon)
    scale_ref[0] = jnp.broadcast_to(scale * (sharpness / rows.shape[1] * gain), scale_ref.shape[1:])


def updated(duals, spend, limit):
    return jnp.maximum(0.0, duals + temper * jnp.log((spend + limit) / (2.0 * limit)))


def totals(match_ref, mine_ref, other_ref):
    return jnp.dot(
        match_ref[0], mine_ref[...], preferred_element_type=jnp.float32
    ) + jnp.dot(match_ref[1], other_ref[...], preferred_element_type=jnp.float32)


def start_rows(user_hbm, scale_hbm, user_ref, scale_ref, sem):
    def start(k, carry):
        pltpu.make_async_copy(user_hbm.at[k], user_ref.at[k], sem.at[0, k]).start()
        pltpu.make_async_copy(scale_hbm.at[k], scale_ref.at[k], sem.at[1, k]).start()
        return carry

    lax.fori_loop(0, user_ref.shape[0], start, 0)


def start_items(item_hbm, item_ref, sem):
    def start(k, carry):
        pltpu.make_async_copy(item_hbm.at[k], item_ref.at[k], sem.at[k]).start()
        return carry

    lax.fori_loop(0, item_ref.shape[0], start, 0)


def item_landed(item, item_ref, item_sem):
    pltpu.make_async_copy(item_ref.at[item], item_ref.at[item], item_sem.at[item]).wait()


def sweep_users(
    user_hbm, scale_hbm, user_ref, scale_ref, item_ref, row_sem, item_sem, item_scale_ref, dual_scr,
    dots_a, dots_b, finish, fanout
):
    clusters, users, _ = user_ref.shape
    camps = item_scale_ref.shape[1]
    width = item_ref.shape[2]
    rows = 64

    def landed(k):
        pltpu.make_async_copy(user_hbm.at[k], user_ref.at[k], row_sem.at[0, k]).wait()
        pltpu.make_async_copy(scale_hbm.at[k], scale_ref.at[k], row_sem.at[1, k]).wait()
        if item_sem is not None:
            for e in range(fanout):
                item_landed(k * fanout + e, item_ref, item_sem)

    def multiply(k, dots):
        blocks = item_ref[pl.ds(pl.multiple_of(k * fanout, fanout), fanout), :camps].reshape(fanout * camps, width)
        dots[...] = lax.dot_general(
            user_ref[k], blocks, (((1,), (1,)), ((), ())), preferred_element_type=jnp.float32
        )

    def cluster(k, dots):
        first = pl.multiple_of(k * fanout, fanout)
        item_scale = item_scale_ref[pl.ds(first, fanout), :]
        shift = dual_scr[pl.ds(first, fanout), :]
        scales = [jnp.broadcast_to(item_scale[e : e + 1], (rows, camps)) for e in range(fanout)]
        shifts = [jnp.broadcast_to(shift[e : e + 1], (rows, camps)) for e in range(fanout)]
        sums = [jnp.zeros((8, camps), jnp.float32) for _ in range(fanout)]
        for start in range(0, users, rows):
            user_scale = scale_ref[k, start : start + rows, :]
            weights = []
            for e in range(fanout):
                raw = dots[start : start + rows, e * camps : (e + 1) * camps]
                weights.append(jnp.exp2(raw * user_scale * scales[e] - shifts[e]))
            den = 1.0 + jnp.sum(functools.reduce(jnp.add, weights), axis=1, keepdims=True)
            sums = finish(k, start, rows, weights, den, sums)
        finish(k, None, rows, None, None, sums)

    landed(0)
    multiply(0, dots_a)

    def two(n, carry):
        k = 2 * n
        landed(k + 1)

        @pl.when(k + 2 < clusters)
        def _():
            landed(k + 2)

        multiply(k + 1, dots_b)
        cluster(k, dots_a)
        multiply(jnp.minimum(k + 2, clusters - 1), dots_a)
        cluster(k + 1, dots_b)
        return carry

    lax.fori_loop(0, clusters // 2, two, 0)


def spend_finish(where_ref, size_ref, users, fanout, spend_scr):
    def finish(k, start, rows, weights, den, sums):
        if start is None:
            for e in range(fanout):
                spend_scr[pl.ds(k * fanout + e, 1), :] = jnp.sum(sums[e], axis=0, keepdims=True)
            return 0
        place = where_ref[1] * users + start + lax.broadcasted_iota(jnp.int32, (rows, 1), 0)
        share = jnp.where(place < size_ref[k], 1.0 / den, 0.0)
        out = []
        for e in range(fanout):
            part = weights[e] * share
            total = sums[e]
            for r in range(0, rows, 8):
                total = total + part[r : r + 8]
            out.append(total)
        return out

    return finish


def halves(where_ref, spend_scr, mine_ref, theirs_ref):
    count = mine_ref.shape[0]
    rep = where_ref[1]
    mine_ref[...] = spend_scr[pl.ds(pl.multiple_of(rep * count, count), count), :]
    theirs_ref[...] = spend_scr[pl.ds(pl.multiple_of((1 - rep) * count, count), count), :]


def item_facts(item_ref, item_sem, dual_ref, limit_ref, live_ref, item_scale_ref):
    items, camps = dual_ref.shape
    width = item_ref.shape[2]
    eye = lax.broadcasted_iota(jnp.int32, (camps, camps), 0) == lax.broadcasted_iota(jnp.int32, (camps, camps), 1)

    def one(item, carry):
        item_landed(item, item_ref, item_sem)
        facts = item_ref[item, camps:, :camps].astype(jnp.float32)
        dual_ref[pl.ds(item, 1), :] = facts[0:1] + facts[1:2] + facts[2:3]
        limit_ref[pl.ds(item, 1), :] = facts[3:4] + facts[4:5] + facts[5:6]
        live_ref[pl.ds(item, 1), :] = facts[6:7]
        rows = item_ref[item, :camps].astype(jnp.float32)
        total = jnp.broadcast_to(jnp.sum(rows * rows, axis=1, keepdims=True), (camps, camps))
        total = jnp.sum(jnp.where(eye, total, 0.0), axis=0, keepdims=True)
        item_scale_ref[pl.ds(item, 1), :] = lax.rsqrt(total * (1.0 / width) + epsilon)
        return carry

    lax.fori_loop(0, items, one, 0, unroll=4)


def first_kernel(
    shards, half, fanout, where_ref, size_ref, item_at_ref, own_ref, user_hbm, scale_hbm, camp_ref, fact_ref, *rest
):
    received, outs = rest[: 2 * (shards - 1)], rest[2 * (shards - 1) :][:7]
    mine_ref, theirs_ref, duals_ref, limit_ref, live_ref, item_scale_ref, item_out = outs
    user_ref, scale_ref, item_ref, row_sem, item_sem, dots_a, dots_b, dual_scr, spend_scr, out_sem = rest[-10:]
    cap = 2 * half
    rep = where_ref[1]
    users = user_ref.shape[1]
    camps = camp_ref.shape[1]

    def fetch(slot, pairs):
        item = item_at_ref[slot]

        @pl.when(item >= 0)
        def _():
            for source, rows in pairs:
                pltpu.make_async_copy(source, item_ref.at[item, rows], item_sem.at[item]).start()

    everything = pl.ds(0, item_ref.shape[1])
    for j in range(cap):
        fetch(
            j,
            [
                (camp_ref.at[own_ref[j]], pl.ds(0, camps)),
                (fact_ref.at[own_ref[j]], pl.ds(camps, fact_ref.shape[1])),
            ],
        )
    for n in range(shards - 1):
        for j in range(half):
            fetch((n + 1) * cap + rep * half + j, [(received[2 * n].at[j], everything)])
            fetch((n + 1) * cap + (1 - rep) * half + j, [(received[2 * n + 1].at[j], everything)])
    start_rows(user_hbm, scale_hbm, user_ref, scale_ref, row_sem)
    item_facts(item_ref, item_sem, duals_ref, limit_ref, live_ref, item_scale_ref)
    keep = pltpu.make_async_copy(item_ref, item_out, out_sem)
    keep.start()
    dual_scr[...] = jnp.where(live_ref[...] > 0.5, duals_ref[...] * gain, masked)
    finish = spend_finish(where_ref, size_ref, users, fanout, spend_scr)
    sweep_users(
        user_hbm, scale_hbm, user_ref, scale_ref, item_ref, row_sem, None, item_scale_ref,
        dual_scr, dots_a, dots_b, finish, fanout
    )
    halves(where_ref, spend_scr, mine_ref, theirs_ref)
    keep.wait()


def second_kernel(
    fanout, where_ref, size_ref, duals_ref, live_ref, item_scale_ref, limit_ref, match_ref, got_ref, other_ref,
    user_hbm, scale_hbm, item_hbm, mine_ref, theirs_ref, next_ref, user_ref, scale_ref, item_ref, row_sem, item_sem,
    dots_a, dots_b, dual_scr, spend_scr
):
    start_items(item_hbm, item_ref, item_sem)
    start_rows(user_hbm, scale_hbm, user_ref, scale_ref, row_sem)
    duals = updated(duals_ref[...], totals(match_ref, got_ref, other_ref), limit_ref[...])
    next_ref[...] = duals
    dual_scr[...] = jnp.where(live_ref[...] > 0.5, duals * gain, masked)
    finish = spend_finish(where_ref, size_ref, user_ref.shape[1], fanout, spend_scr)
    sweep_users(
        user_hbm, scale_hbm, user_ref, scale_ref, item_ref, row_sem, item_sem, item_scale_ref,
        dual_scr, dots_a, dots_b, finish, fanout
    )
    halves(where_ref, spend_scr, mine_ref, theirs_ref)


def third_kernel(
    fanout, where_ref, size_ref, duals_ref, live_ref, item_scale_ref, limit_ref, match_ref, got_ref, other_ref,
    own_match_ref, got_one_ref, other_one_ref, own_dual_ref, own_limit_ref, user_hbm, scale_hbm, item_hbm,
    user_dual_ref, own_out_ref, user_ref, scale_ref, item_ref, row_sem, item_sem, dots_a, dots_b, dual_scr, row_scr
):
    start_items(item_hbm, item_ref, item_sem)
    start_rows(user_hbm, scale_hbm, user_ref, scale_ref, row_sem)
    duals = updated(duals_ref[...], totals(match_ref, got_ref, other_ref), limit_ref[...])
    dual_scr[...] = jnp.where(live_ref[...] > 0.5, duals * gain, masked)
    own = updated(own_dual_ref[...], totals(own_match_ref, got_one_ref, other_one_ref), own_limit_ref[...])
    own_out_ref[...] = updated(own, totals(own_match_ref, got_ref, other_ref), own_limit_ref[...])
    users = user_ref.shape[1]
    partial = []

    def finish(k, start, rows, weights, den, sums):
        if start is None:
            return 0
        lanes = 128
        offset = start % lanes
        wide = jnp.broadcast_to(den, (rows, lanes))
        eye = offset + lax.broadcasted_iota(jnp.int32, (rows, lanes), 0) == lax.broadcasted_iota(
            jnp.int32, (rows, lanes), 1
        )
        row = jnp.sum(jnp.where(eye, wide, 0.0), axis=0, keepdims=True)
        if offset:
            row = row + partial.pop()
        if offset + rows < lanes:
            partial.append(row)
            return sums
        base = start - offset
        place = where_ref[1] * users + base + lax.broadcasted_iota(jnp.int32, (1, lanes), 1)
        row_scr[k, base // lanes : base // lanes + 1, :] = jnp.where(
            place < size_ref[k], temper * jnp.log(row), 0.0
        )
        return sums

    sweep_users(
        user_hbm, scale_hbm, user_ref, scale_ref, item_ref, row_sem, item_sem, item_scale_ref,
        dual_scr, dots_a, dots_b, finish, fanout
    )
    for n in range(row_scr.shape[1]):
        user_dual_ref[:, n * 128 : (n + 1) * 128] = row_scr[:, n, :]


def program(
    user_emb, elig_owner, elig_local, cluster_size, camp_emb, camp_count, dual_init, spend_limit
):
    shards = lax.axis_size("shard")
    reps = lax.axis_size("rep")
    me = lax.axis_index("shard").astype(jnp.int32)
    rep = lax.axis_index("rep").astype(jnp.int32)
    clusters, users, width = user_emb.shape
    blocks, camps, _ = camp_emb.shape
    fanout = elig_owner.shape[1]
    items = clusters * fanout
    cap = 2 * items // shards
    half = cap // reps
    part = items // reps
    swap = [(0, 1), (1, 0)]
    f32 = jnp.float32

    owners = elig_owner.reshape(-1)
    locals_ = elig_local.reshape(-1)
    shard_ids = jnp.arange(shards, dtype=jnp.int32)
    hot = (owners[:, None] == shard_ids[None, :]).astype(jnp.int32)
    rank = jnp.sum((jnp.cumsum(hot, axis=0) - hot) * hot, axis=1)
    slot = owners * cap + rank
    hit = slot[:, None] == jnp.arange(shards * cap, dtype=jnp.int32)[None, :]
    wanted = jnp.sum(jnp.where(hit, locals_[:, None], 0), axis=0).reshape(shards, cap)
    names = owners * blocks + locals_
    ask = jnp.concatenate([wanted, jnp.broadcast_to(names[None, :], (shards, items))], axis=1)
    heard = lax.all_to_all(ask, "shard", split_axis=0, concat_axis=0, tiled=True)
    where = jnp.stack([me, rep])

    def pieces(x):
        out = []
        for _ in range(3):
            piece = lax.reduce_precision(x, exponent_bits=8, mantissa_bits=7)
            out.append(piece)
            x = x - piece
        return out

    live = (jnp.arange(camps, dtype=jnp.int32)[None, :] < camp_count[:, None]).astype(f32)
    rows = pieces(dual_init) + pieces(spend_limit) + [live, jnp.zeros_like(live)]
    facts = jnp.stack(rows, axis=1).astype(camp_emb.dtype)
    facts = jnp.concatenate([facts, jnp.zeros_like(facts)], axis=2)
    fact_rows = len(rows)
    camp_rows, facts = in_hbm(camp_emb), in_hbm(facts)

    order = send_order(shards)
    sent = {}
    for shifts in (order[:4], order[4:]):
        outs = pl.pallas_call(
            functools.partial(gather_kernel, half, shifts),
            out_shape=[pltpu.HBM((half, camps + fact_rows, width), camp_emb.dtype)] * len(shifts),
            in_specs=[SMEM, SMEM, HBM, HBM],
            out_specs=[HBM] * len(shifts),
            scratch_shapes=[
                pltpu.VMEM((len(shifts) * half, camps + fact_rows, width), camp_emb.dtype),
                pltpu.SemaphoreType.DMA((3, len(shifts) * half)),
            ],
            compiler_params=pltpu.CompilerParams(vmem_limit_bytes=8 * 2**20),
            cost_estimate=pl.CostEstimate(flops=0, bytes_accessed=len(shifts) * 2**19, transcendentals=0),
        )(where, heard, camp_rows, facts)
        sent.update(zip(shifts, outs))

    got_blocks = {}
    for shift in order:
        got_blocks[shift] = lax.ppermute(sent[shift], "shard", [(i, i ^ shift) for i in range(shards)])

    heard, user_late, _ = lax.optimization_barrier((heard, user_emb, got_blocks[1]))
    all_names = heard[:, cap:]
    item_of_slot = (
        jnp.sum(
            jnp.where(
                ((owners ^ me) * cap + rank)[:, None] == jnp.arange(shards * cap, dtype=jnp.int32)[None, :],
                jnp.arange(1, items + 1, dtype=jnp.int32)[:, None],
                0,
            ),
            axis=0,
        )
        - 1
    )
    own_wanted = lax.dynamic_slice_in_dim(wanted, me, 1, 0).reshape(cap)
    user_scale = pl.pallas_call(
        user_kernel,
        out_shape=jax.ShapeDtypeStruct((clusters, users, camps), f32),
        grid=(clusters,),
        in_specs=[pl.BlockSpec((1, users, width), lambda k: (k, 0, 0))],
        out_specs=pl.BlockSpec((1, users, camps), lambda k: (k, 0, 0)),
        compiler_params=pltpu.CompilerParams(vmem_limit_bytes=16 * 2**20),
        cost_estimate=pl.CostEstimate(flops=8 * 2**20, bytes_accessed=8 * 2**20, transcendentals=0),
    )(in_hbm(user_late))

    def columns(which):
        return lax.dynamic_slice_in_dim(all_names, which * part, part, 1).reshape(1, -1)

    sides = (columns(rep), columns(1 - rep))
    own_names = me * blocks + jnp.arange(blocks, dtype=jnp.int32)
    match = jnp.stack([(names[:, None] == side).astype(jnp.bfloat16) for side in sides])
    own_match = jnp.stack([(own_names[:, None] == side).astype(jnp.bfloat16) for side in sides])

    last = order[-1]
    got_blocks[last], item_of_slot, own_wanted, user_scale, match, own_match = lax.optimization_barrier(
        (got_blocks[last], item_of_slot, own_wanted, user_scale, match, own_match)
    )
    received = []
    for shift in range(1, shards):
        received += [got_blocks[shift], lax.ppermute(got_blocks[shift], "rep", swap)]
    user_rows, user_scale = in_hbm(user_emb), in_hbm(user_scale)

    def exchange(mine, theirs):
        total = mine + lax.ppermute(theirs, "rep", swap)
        spread = jnp.broadcast_to(total.astype(jnp.bfloat16)[None], (shards, part, camps))
        got = lax.all_to_all(spread, "shard", split_axis=0, concat_axis=0, tiled=True)
        got = got.reshape(shards * part, camps)
        return in_vmem(got), in_vmem(lax.ppermute(got, "rep", swap))

    spend_out = [jax.ShapeDtypeStruct((part, camps), f32)] * 2
    work = [
        pltpu.VMEM((clusters, users, width), user_emb.dtype),
        pltpu.VMEM((clusters, users, camps), f32),
        pltpu.VMEM((items, camps + fact_rows, width), camp_emb.dtype),
        pltpu.SemaphoreType.DMA((2, clusters)),
        pltpu.SemaphoreType.DMA((items,)),
        pltpu.VMEM((users, fanout * camps), f32),
        pltpu.VMEM((users, fanout * camps), f32),
        pltpu.VMEM((items, camps), f32),
    ]
    spend_work = [pltpu.VMEM((items, camps), f32)]
    limits = pltpu.CompilerParams(vmem_limit_bytes=24 * 2**20)

    mine, theirs, item_dual, item_limit, item_live, item_scale, item_emb = pl.pallas_call(
        functools.partial(first_kernel, shards, half, fanout),
        out_shape=spend_out
        + [jax.ShapeDtypeStruct((items, camps), f32)] * 4
        + [pltpu.HBM((items, camps + fact_rows, width), camp_emb.dtype)],
        in_specs=[SMEM] * 4 + [HBM] * 4 + [ANY] * len(received),
        out_specs=[VMEM] * 6 + [HBM],
        scratch_shapes=work + spend_work + [pltpu.SemaphoreType.DMA],
        compiler_params=limits,
    )(where, cluster_size, item_of_slot, own_wanted, user_rows, user_scale, camp_rows, facts, *received)
    item_emb = in_hbm(item_emb)
    got_one, other_one = exchange(mine, theirs)

    mine, theirs, next_dual = pl.pallas_call(
        functools.partial(second_kernel, fanout),
        out_shape=spend_out + [jax.ShapeDtypeStruct((items, camps), f32)],
        in_specs=[SMEM] * 2 + [VMEM] * 7 + [HBM] * 3,
        out_specs=[VMEM] * 3,
        scratch_shapes=work + spend_work,
        compiler_params=limits,
    )(where, cluster_size, item_dual, item_live, item_scale, item_limit, match, got_one, other_one, user_rows,
      user_scale, item_emb)
    got_two, other_two = exchange(mine, theirs)

    user_dual, own_dual = pl.pallas_call(
        functools.partial(third_kernel, fanout),
        out_shape=[
            jax.ShapeDtypeStruct((clusters, users), f32),
            jax.ShapeDtypeStruct((blocks, camps), f32),
        ],
        in_specs=[SMEM] * 2 + [VMEM] * 12 + [HBM] * 3,
        out_specs=[VMEM] * 2,
        scratch_shapes=work + [pltpu.VMEM((clusters, users // 128, 128), f32)],
        compiler_params=limits,
    )(where, cluster_size, next_dual, item_live, item_scale, item_limit, match, got_two, other_two, own_match,
      got_one, other_one, dual_init, spend_limit, user_rows, user_scale, item_emb)
    return (user_dual, own_dual)


def solution(mesh):
    return jax.shard_map(
        program,
        mesh=mesh,
        in_specs=(
            P("shard", "rep", None),
            P("shard", None),
            P("shard", None),
            P("shard"),
            P("shard", None, None),
            P("shard"),
            P("shard", None),
            P("shard", None),
        ),
        out_specs=(P("shard", "rep"), P("shard", None)),
        check_vma=False,
    )
```

```python
import functools
import math

import jax
import jax.numpy as jnp
from jax import lax
from jax.experimental import pallas as pl
from jax.experimental.pallas import tpu as pltpu
from jax.sharding import PartitionSpec as P


epsilon = 1e-06
temper = 0.25
sharpness = 16.0
gain = 1.0 / (temper * math.log(2.0))
masked = 1e30


VMEM = pl.BlockSpec(memory_space=pltpu.VMEM)
SMEM = pl.BlockSpec(memory_space=pltpu.SMEM)
ANY = pl.BlockSpec(memory_space=pl.ANY)
HBM = pl.BlockSpec(memory_space=pltpu.HBM)


def in_hbm(x):
    return pltpu.with_memory_space_constraint(x, pltpu.HBM)


def in_vmem(x):
    return pltpu.with_memory_space_constraint(x, pltpu.VMEM)


def send_order(shards):
    top = shards // 2
    far = [top + n for n in range(top)]
    first = far[: top // 2]
    return first + list(range(1, top)) + far[top // 2 :]


def fact_place(j, half, camps, pieces, width):
    across = width // camps
    return pl.ds(half * camps + j // across * pieces, pieces), pl.ds(j % across * camps, camps)


def gather_kernel(half, shifts, where_ref, asked_ref, camp_ref, fact_ref, *rest):
    outs, (stage, sem) = rest[:-2], rest[-2:]
    me, rep = where_ref[0], where_ref[1]
    _, camps, width = camp_ref.shape
    arriving, leaving = [], []
    for n, (shift, out) in enumerate(zip(shifts, outs)):
        for j in range(half):
            block = asked_ref[me ^ shift, rep * half + j]
            rows, lanes = fact_place(j, half, camps, fact_ref.shape[1], width)
            for copy in (
                pltpu.make_async_copy(
                    camp_ref.at[block], stage.at[n, pl.ds(j * camps, camps)], sem.at[0, n * half + j]
                ),
                pltpu.make_async_copy(fact_ref.at[block], stage.at[n, rows, lanes], sem.at[1, n * half + j]),
            ):
                copy.start()
                arriving.append(copy)
        leaving.append(pltpu.make_async_copy(stage.at[n], out, sem.at[2, n]))
    for n, copy in enumerate(leaving):
        for part in arriving[2 * half * n : 2 * half * (n + 1)]:
            part.wait()
        copy.start()
    for copy in leaving:
        copy.wait()


def user_kernel(user_ref, scale_ref):
    rows = user_ref[0].astype(jnp.float32)
    scale = lax.rsqrt(jnp.sum(rows * rows, axis=1, keepdims=True) * (1.0 / rows.shape[1]) + epsilon)
    scale_ref[0] = jnp.broadcast_to(scale * (sharpness / rows.shape[1] * gain), scale_ref.shape[1:])


def updated(duals, spend, limit):
    return jnp.maximum(0.0, duals + temper * jnp.log((spend + limit) / (2.0 * limit)))


def totals(match_ref, mine_ref, other_ref):
    return jnp.dot(
        match_ref[0], mine_ref[...], preferred_element_type=jnp.float32
    ) + jnp.dot(match_ref[1], other_ref[...], preferred_element_type=jnp.float32)


def start_rows(user_hbm, scale_hbm, user_ref, scale_ref, sem):
    def start(k, carry):
        pltpu.make_async_copy(user_hbm.at[k], user_ref.at[k], sem.at[0, k]).start()
        pltpu.make_async_copy(scale_hbm.at[k], scale_ref.at[k], sem.at[1, k]).start()
        return carry

    lax.fori_loop(0, user_ref.shape[0], start, 0)


def start_items(item_hbm, item_ref, sem):
    def start(k, carry):
        pltpu.make_async_copy(item_hbm.at[k], item_ref.at[k], sem.at[k]).start()
        return carry

    lax.fori_loop(0, item_ref.shape[0], start, 0)


def item_landed(item, item_ref, item_sem):
    pltpu.make_async_copy(item_ref.at[item], item_ref.at[item], item_sem.at[item]).wait()


def sweep_users(
    user_hbm, scale_hbm, user_ref, scale_ref, item_ref, row_sem, item_sem, item_scale_ref, dual_scr,
    dots_a, dots_b, finish, fanout
):
    clusters, users, _ = user_ref.shape
    camps = item_scale_ref.shape[1]
    width = item_ref.shape[2]
    rows = 64

    def landed(k):
        pltpu.make_async_copy(user_hbm.at[k], user_ref.at[k], row_sem.at[0, k]).wait()
        pltpu.make_async_copy(scale_hbm.at[k], scale_ref.at[k], row_sem.at[1, k]).wait()
        if item_sem is not None:
            for e in range(fanout):
                item_landed(k * fanout + e, item_ref, item_sem)

    def multiply(k, dots):
        blocks = item_ref[pl.ds(pl.multiple_of(k * fanout, fanout), fanout)].reshape(fanout * camps, width)
        dots[...] = lax.dot_general(
            user_ref[k], blocks, (((1,), (1,)), ((), ())), preferred_element_type=jnp.float32
        )

    def cluster(k, dots):
        first = pl.multiple_of(k * fanout, fanout)
        item_scale = item_scale_ref[pl.ds(first, fanout), :]
        shift = dual_scr[pl.ds(first, fanout), :]
        scales = [jnp.broadcast_to(item_scale[e : e + 1], (rows, camps)) for e in range(fanout)]
        shifts = [jnp.broadcast_to(shift[e : e + 1], (rows, camps)) for e in range(fanout)]
        sums = [jnp.zeros((8, camps), jnp.float32) for _ in range(fanout)]
        for start in range(0, users, rows):
            user_scale = scale_ref[k, start : start + rows, :]
            weights = []
            for e in range(fanout):
                raw = dots[start : start + rows, e * camps : (e + 1) * camps]
                weights.append(jnp.exp2(raw * user_scale * scales[e] - shifts[e]))
            den = 1.0 + jnp.sum(functools.reduce(jnp.add, weights), axis=1, keepdims=True)
            sums = finish(k, start, rows, weights, den, sums)
        finish(k, None, rows, None, None, sums)

    landed(0)
    multiply(0, dots_a)

    def two(n, carry):
        k = 2 * n
        landed(k + 1)

        @pl.when(k + 2 < clusters)
        def _():
            landed(k + 2)

        multiply(k + 1, dots_b)
        cluster(k, dots_a)
        multiply(jnp.minimum(k + 2, clusters - 1), dots_a)
        cluster(k + 1, dots_b)
        return carry

    lax.fori_loop(0, clusters // 2, two, 0)


def spend_finish(where_ref, size_ref, users, fanout, spend_scr):
    def finish(k, start, rows, weights, den, sums):
        if start is None:
            for e in range(fanout):
                spend_scr[pl.ds(k * fanout + e, 1), :] = jnp.sum(sums[e], axis=0, keepdims=True)
            return 0
        place = where_ref[1] * users + start + lax.broadcasted_iota(jnp.int32, (rows, 1), 0)
        share = jnp.where(place < size_ref[k], 1.0 / den, 0.0)
        out = []
        for e in range(fanout):
            part = weights[e] * share
            total = sums[e]
            for r in range(0, rows, 8):
                total = total + part[r : r + 8]
            out.append(total)
        return out

    return finish


def halves(where_ref, spend_scr, mine_ref, theirs_ref):
    count = mine_ref.shape[0]
    rep = where_ref[1]
    mine_ref[...] = spend_scr[pl.ds(pl.multiple_of(rep * count, count), count), :]
    theirs_ref[...] = spend_scr[pl.ds(pl.multiple_of((1 - rep) * count, count), count), :]


def item_facts(fact_ref, item_ref, item_sem, fact_sem, dual_ref, limit_ref, live_ref, item_scale_ref):
    items, camps = dual_ref.shape
    width = item_ref.shape[2]
    eye = lax.broadcasted_iota(jnp.int32, (camps, camps), 0) == lax.broadcasted_iota(jnp.int32, (camps, camps), 1)

    def wait(item, carry):
        item_landed(item, item_ref, item_sem)
        pltpu.make_async_copy(fact_ref.at[item], fact_ref.at[item], fact_sem.at[item]).wait()
        return carry

    lax.fori_loop(0, items, wait, 0, unroll=8)
    group = 8

    def some(n, carry):
        first = pl.multiple_of(n * group, group)
        facts = fact_ref[pl.ds(first, group)].astype(jnp.float32)
        dual_ref[pl.ds(first, group), :] = facts[:, 0] + facts[:, 1] + facts[:, 2]
        limit_ref[pl.ds(first, group), :] = facts[:, 3] + facts[:, 4] + facts[:, 5]
        live_ref[pl.ds(first, group), :] = facts[:, 6]
        totals_here = []
        for e in range(group):
            rows = item_ref[first + e].astype(jnp.float32)
            total = jnp.broadcast_to(jnp.sum(rows * rows, axis=1, keepdims=True), (camps, camps))
            totals_here.append(jnp.sum(jnp.where(eye, total, 0.0), axis=0, keepdims=True))
        mean = jnp.concatenate(totals_here, axis=0) * (1.0 / width)
        item_scale_ref[pl.ds(first, group), :] = lax.rsqrt(mean + epsilon)
        return carry

    lax.fori_loop(0, items // group, some, 0)


def first_kernel(
    shards, half, fanout, where_ref, size_ref, item_at_ref, own_ref, user_hbm, scale_hbm, camp_ref, fact_ref, *rest
):
    received, outs = rest[: 2 * (shards - 1)], rest[2 * (shards - 1) :][:7]
    mine_ref, theirs_ref, duals_ref, limit_ref, live_ref, item_scale_ref, item_out = outs
    user_ref, scale_ref, item_ref, row_sem, item_sem, dots_a, dots_b, dual_scr, spend_scr = rest[-12:-3]
    landed_ref, fact_sem, out_sem = rest[-3:]
    cap = 2 * half
    rep = where_ref[1]
    users = user_ref.shape[1]
    _, camps, width = camp_ref.shape
    pieces = fact_ref.shape[1]

    def fetch(slot, block, facts):
        item = item_at_ref[slot]

        @pl.when(item >= 0)
        def _():
            pltpu.make_async_copy(block, item_ref.at[item], item_sem.at[item]).start()
            pltpu.make_async_copy(facts, landed_ref.at[item], fact_sem.at[item]).start()

    for j in range(cap):
        fetch(j, camp_ref.at[own_ref[j]], fact_ref.at[own_ref[j]])
    for n in range(shards - 1):
        for j in range(half):
            for side, message in ((rep, received[2 * n]), (1 - rep, received[2 * n + 1])):
                rows, lanes = fact_place(j, half, camps, pieces, width)
                fetch((n + 1) * cap + side * half + j, message.at[pl.ds(j * camps, camps)], message.at[rows, lanes])
    start_rows(user_hbm, scale_hbm, user_ref, scale_ref, row_sem)
    item_facts(landed_ref, item_ref, item_sem, fact_sem, duals_ref, limit_ref, live_ref, item_scale_ref)
    keep = pltpu.make_async_copy(item_ref, item_out, out_sem)
    keep.start()
    dual_scr[...] = jnp.where(live_ref[...] > 0.5, duals_ref[...] * gain, masked)
    finish = spend_finish(where_ref, size_ref, users, fanout, spend_scr)
    sweep_users(
        user_hbm, scale_hbm, user_ref, scale_ref, item_ref, row_sem, None, item_scale_ref,
        dual_scr, dots_a, dots_b, finish, fanout
    )
    halves(where_ref, spend_scr, mine_ref, theirs_ref)
    keep.wait()


def second_kernel(
    fanout, where_ref, size_ref, duals_ref, live_ref, item_scale_ref, limit_ref, match_ref, got_ref, other_ref,
    user_hbm, scale_hbm, item_hbm, mine_ref, theirs_ref, next_ref, user_ref, scale_ref, item_ref, row_sem, item_sem,
    dots_a, dots_b, dual_scr, spend_scr
):
    start_items(item_hbm, item_ref, item_sem)
    start_rows(user_hbm, scale_hbm, user_ref, scale_ref, row_sem)
    duals = updated(duals_ref[...], totals(match_ref, got_ref, other_ref), limit_ref[...])
    next_ref[...] = duals
    dual_scr[...] = jnp.where(live_ref[...] > 0.5, duals * gain, masked)
    finish = spend_finish(where_ref, size_ref, user_ref.shape[1], fanout, spend_scr)
    sweep_users(
        user_hbm, scale_hbm, user_ref, scale_ref, item_ref, row_sem, item_sem, item_scale_ref,
        dual_scr, dots_a, dots_b, finish, fanout
    )
    halves(where_ref, spend_scr, mine_ref, theirs_ref)


def third_kernel(
    fanout, where_ref, size_ref, duals_ref, live_ref, item_scale_ref, limit_ref, match_ref, got_ref, other_ref,
    own_match_ref, got_one_ref, other_one_ref, own_dual_ref, own_limit_ref, user_hbm, scale_hbm, item_hbm,
    user_dual_ref, own_out_ref, user_ref, scale_ref, item_ref, row_sem, item_sem, dots_a, dots_b, dual_scr, row_scr
):
    start_items(item_hbm, item_ref, item_sem)
    start_rows(user_hbm, scale_hbm, user_ref, scale_ref, row_sem)
    duals = updated(duals_ref[...], totals(match_ref, got_ref, other_ref), limit_ref[...])
    dual_scr[...] = jnp.where(live_ref[...] > 0.5, duals * gain, masked)
    own = updated(own_dual_ref[...], totals(own_match_ref, got_one_ref, other_one_ref), own_limit_ref[...])
    own_out_ref[...] = updated(own, totals(own_match_ref, got_ref, other_ref), own_limit_ref[...])
    users = user_ref.shape[1]
    partial = []

    def finish(k, start, rows, weights, den, sums):
        if start is None:
            return 0
        lanes = 128
        offset = start % lanes
        wide = jnp.broadcast_to(den, (rows, lanes))
        eye = offset + lax.broadcasted_iota(jnp.int32, (rows, lanes), 0) == lax.broadcasted_iota(
            jnp.int32, (rows, lanes), 1
        )
        row = jnp.sum(jnp.where(eye, wide, 0.0), axis=0, keepdims=True)
        if offset:
            row = row + partial.pop()
        if offset + rows < lanes:
            partial.append(row)
            return sums
        base = start - offset
        place = where_ref[1] * users + base + lax.broadcasted_iota(jnp.int32, (1, lanes), 1)
        row_scr[k, base // lanes : base // lanes + 1, :] = jnp.where(
            place < size_ref[k], temper * jnp.log(row), 0.0
        )
        return sums

    sweep_users(
        user_hbm, scale_hbm, user_ref, scale_ref, item_ref, row_sem, item_sem, item_scale_ref,
        dual_scr, dots_a, dots_b, finish, fanout
    )
    for n in range(row_scr.shape[1]):
        user_dual_ref[:, n * 128 : (n + 1) * 128] = row_scr[:, n, :]


def program(
    user_emb, elig_owner, elig_local, cluster_size, camp_emb, camp_count, dual_init, spend_limit
):
    shards = lax.axis_size("shard")
    reps = lax.axis_size("rep")
    me = lax.axis_index("shard").astype(jnp.int32)
    rep = lax.axis_index("rep").astype(jnp.int32)
    clusters, users, width = user_emb.shape
    blocks, camps, _ = camp_emb.shape
    fanout = elig_owner.shape[1]
    items = clusters * fanout
    cap = 2 * items // shards
    half = cap // reps
    part = items // reps
    swap = [(0, 1), (1, 0)]
    f32 = jnp.float32

    owners = elig_owner.reshape(-1)
    locals_ = elig_local.reshape(-1)
    shard_ids = jnp.arange(shards, dtype=jnp.int32)
    hot = (owners[:, None] == shard_ids[None, :]).astype(jnp.int32)
    rank = jnp.sum((jnp.cumsum(hot, axis=0) - hot) * hot, axis=1)
    slot = owners * cap + rank
    hit = slot[:, None] == jnp.arange(shards * cap, dtype=jnp.int32)[None, :]
    wanted = jnp.sum(jnp.where(hit, locals_[:, None], 0), axis=0).reshape(shards, cap)
    names = owners * blocks + locals_
    ask = jnp.concatenate([wanted, jnp.broadcast_to(names[None, :], (shards, items))], axis=1)
    heard = lax.all_to_all(ask, "shard", split_axis=0, concat_axis=0, tiled=True)
    where = jnp.stack([me, rep])

    def pieces(x):
        out = []
        for _ in range(3):
            piece = lax.reduce_precision(x, exponent_bits=8, mantissa_bits=7)
            out.append(piece)
            x = x - piece
        return out

    live = (jnp.arange(camps, dtype=jnp.int32)[None, :] < camp_count[:, None]).astype(f32)
    rows = pieces(dual_init) + pieces(spend_limit) + [live, jnp.zeros_like(live)]
    facts = jnp.stack(rows, axis=1).astype(camp_emb.dtype)
    message = half * camps + -(-half * camps // width) * len(rows)
    camp_rows, facts = in_hbm(camp_emb), in_hbm(facts)

    order = send_order(shards)
    sent = {}
    for shifts in (order[:4], order[4:]):
        outs = pl.pallas_call(
            functools.partial(gather_kernel, half, shifts),
            out_shape=[pltpu.HBM((message, width), camp_emb.dtype)] * len(shifts),
            in_specs=[SMEM, SMEM, HBM, HBM],
            out_specs=[HBM] * len(shifts),
            scratch_shapes=[
                pltpu.VMEM((len(shifts), message, width), camp_emb.dtype),
                pltpu.SemaphoreType.DMA((3, len(shifts) * half)),
            ],
            compiler_params=pltpu.CompilerParams(vmem_limit_bytes=8 * 2**20),
            cost_estimate=pl.CostEstimate(flops=0, bytes_accessed=len(shifts) * 2**19, transcendentals=0),
        )(where, heard, camp_rows, facts)
        sent.update(zip(shifts, outs))

    got_blocks = {}
    for shift in order:
        got_blocks[shift] = lax.ppermute(sent[shift], "shard", [(i, i ^ shift) for i in range(shards)])

    heard, user_late, _ = lax.optimization_barrier((heard, user_emb, got_blocks[1]))
    all_names = heard[:, cap:]
    item_of_slot = (
        jnp.sum(
            jnp.where(
                ((owners ^ me) * cap + rank)[:, None] == jnp.arange(shards * cap, dtype=jnp.int32)[None, :],
                jnp.arange(1, items + 1, dtype=jnp.int32)[:, None],
                0,
            ),
            axis=0,
        )
        - 1
    )
    own_wanted = lax.dynamic_slice_in_dim(wanted, me, 1, 0).reshape(cap)
    user_scale = pl.pallas_call(
        user_kernel,
        out_shape=jax.ShapeDtypeStruct((clusters, users, camps), f32),
        grid=(clusters,),
        in_specs=[pl.BlockSpec((1, users, width), lambda k: (k, 0, 0))],
        out_specs=pl.BlockSpec((1, users, camps), lambda k: (k, 0, 0)),
        compiler_params=pltpu.CompilerParams(vmem_limit_bytes=16 * 2**20),
        cost_estimate=pl.CostEstimate(flops=8 * 2**20, bytes_accessed=8 * 2**20, transcendentals=0),
    )(in_hbm(user_late))

    def columns(which):
        return lax.dynamic_slice_in_dim(all_names, which * part, part, 1).reshape(1, -1)

    sides = (columns(rep), columns(1 - rep))
    own_names = me * blocks + jnp.arange(blocks, dtype=jnp.int32)
    match = jnp.stack([(names[:, None] == side).astype(jnp.bfloat16) for side in sides])
    own_match = jnp.stack([(own_names[:, None] == side).astype(jnp.bfloat16) for side in sides])

    last = order[-1]
    got_blocks[last], item_of_slot, own_wanted, user_scale, match, own_match = lax.optimization_barrier(
        (got_blocks[last], item_of_slot, own_wanted, user_scale, match, own_match)
    )
    received = []
    for shift in range(1, shards):
        received += [got_blocks[shift], lax.ppermute(got_blocks[shift], "rep", swap)]
    user_rows, user_scale = in_hbm(user_emb), in_hbm(user_scale)

    def exchange(mine, theirs):
        total = mine + lax.ppermute(theirs, "rep", swap)
        spread = jnp.broadcast_to(total.astype(jnp.bfloat16)[None], (shards, part, camps))
        got = lax.all_to_all(spread, "shard", split_axis=0, concat_axis=0, tiled=True)
        got = got.reshape(shards * part, camps)
        return in_vmem(got), in_vmem(lax.ppermute(got, "rep", swap))

    spend_out = [jax.ShapeDtypeStruct((part, camps), f32)] * 2
    work = [
        pltpu.VMEM((clusters, users, width), user_emb.dtype),
        pltpu.VMEM((clusters, users, camps), f32),
        pltpu.VMEM((items, camps, width), camp_emb.dtype),
        pltpu.SemaphoreType.DMA((2, clusters)),
        pltpu.SemaphoreType.DMA((items,)),
        pltpu.VMEM((users, fanout * camps), f32),
        pltpu.VMEM((users, fanout * camps), f32),
        pltpu.VMEM((items, camps), f32),
    ]
    spend_work = [pltpu.VMEM((items, camps), f32)]
    limits = pltpu.CompilerParams(vmem_limit_bytes=24 * 2**20)

    mine, theirs, item_dual, item_limit, item_live, item_scale, item_emb = pl.pallas_call(
        functools.partial(first_kernel, shards, half, fanout),
        out_shape=spend_out
        + [jax.ShapeDtypeStruct((items, camps), f32)] * 4
        + [pltpu.HBM((items, camps, width), camp_emb.dtype)],
        in_specs=[SMEM] * 4 + [HBM] * 4 + [ANY] * len(received),
        out_specs=[VMEM] * 6 + [HBM],
        scratch_shapes=work
        + spend_work
        + [
            pltpu.VMEM((items, len(rows), camps), camp_emb.dtype),
            pltpu.SemaphoreType.DMA((items,)),
            pltpu.SemaphoreType.DMA,
        ],
        compiler_params=limits,
    )(where, cluster_size, item_of_slot, own_wanted, user_rows, user_scale, camp_rows, facts, *received)
    item_emb = in_hbm(item_emb)
    got_one, other_one = exchange(mine, theirs)

    mine, theirs, next_dual = pl.pallas_call(
        functools.partial(second_kernel, fanout),
        out_shape=spend_out + [jax.ShapeDtypeStruct((items, camps), f32)],
        in_specs=[SMEM] * 2 + [VMEM] * 7 + [HBM] * 3,
        out_specs=[VMEM] * 3,
        scratch_shapes=work + spend_work,
        compiler_params=limits,
    )(where, cluster_size, item_dual, item_live, item_scale, item_limit, match, got_one, other_one, user_rows,
      user_scale, item_emb)
    got_two, other_two = exchange(mine, theirs)

    user_dual, own_dual = pl.pallas_call(
        functools.partial(third_kernel, fanout),
        out_shape=[
            jax.ShapeDtypeStruct((clusters, users), f32),
            jax.ShapeDtypeStruct((blocks, camps), f32),
        ],
        in_specs=[SMEM] * 2 + [VMEM] * 12 + [HBM] * 3,
        out_specs=[VMEM] * 2,
        scratch_shapes=work + [pltpu.VMEM((clusters, users // 128, 128), f32)],
        compiler_params=limits,
    )(where, cluster_size, next_dual, item_live, item_scale, item_limit, match, got_two, other_two, own_match,
      got_one, other_one, dual_init, spend_limit, user_rows, user_scale, item_emb)
    return (user_dual, own_dual)


def solution(mesh):
    return jax.shard_map(
        program,
        mesh=mesh,
        in_specs=(
            P("shard", "rep", None),
            P("shard", None),
            P("shard", None),
            P("shard"),
            P("shard", None, None),
            P("shard"),
            P("shard", None),
            P("shard", None),
        ),
        out_specs=(P("shard", "rep"), P("shard", None)),
        check_vma=False,
    )
```

```python
import functools
import math

import jax
import jax.numpy as jnp
from jax import lax
from jax.experimental import pallas as pl
from jax.experimental.pallas import tpu as pltpu
from jax.sharding import PartitionSpec as P


epsilon = 1e-06
temper = 0.25
sharpness = 16.0
gain = 1.0 / (temper * math.log(2.0))
masked = 1e30


VMEM = pl.BlockSpec(memory_space=pltpu.VMEM)
SMEM = pl.BlockSpec(memory_space=pltpu.SMEM)
ANY = pl.BlockSpec(memory_space=pl.ANY)
HBM = pl.BlockSpec(memory_space=pltpu.HBM)


def in_hbm(x):
    return pltpu.with_memory_space_constraint(x, pltpu.HBM)


def in_vmem(x):
    return pltpu.with_memory_space_constraint(x, pltpu.VMEM)


def send_order(shards):
    top = shards // 2
    far = [top + n for n in range(top)]
    first = far[: top // 2]
    return first + list(range(1, top)) + far[top // 2 :]


def fact_place(j, half, camps, pieces, width):
    across = width // camps
    return pl.ds(half * camps + j // across * pieces, pieces), pl.ds(j % across * camps, camps)


def gather_kernel(half, shifts, where_ref, asked_ref, camp_ref, fact_ref, *rest):
    outs, (stage, sem) = rest[:-2], rest[-2:]
    me, rep = where_ref[0], where_ref[1]
    _, camps, width = camp_ref.shape
    arriving, leaving = [], []
    for n, (shift, out) in enumerate(zip(shifts, outs)):
        for j in range(half):
            block = asked_ref[me ^ shift, rep * half + j]
            rows, lanes = fact_place(j, half, camps, fact_ref.shape[1], width)
            for copy in (
                pltpu.make_async_copy(
                    camp_ref.at[block], stage.at[n, pl.ds(j * camps, camps)], sem.at[0, n * half + j]
                ),
                pltpu.make_async_copy(fact_ref.at[block], stage.at[n, rows, lanes], sem.at[1, n * half + j]),
            ):
                copy.start()
                arriving.append(copy)
        leaving.append(pltpu.make_async_copy(stage.at[n], out, sem.at[2, n]))
    for n, copy in enumerate(leaving):
        for part in arriving[2 * half * n : 2 * half * (n + 1)]:
            part.wait()
        copy.start()
    for copy in leaving:
        copy.wait()


def user_kernel(user_ref, scale_ref):
    rows = user_ref[0].astype(jnp.float32)
    scale = lax.rsqrt(jnp.sum(rows * rows, axis=1, keepdims=True) * (1.0 / rows.shape[1]) + epsilon)
    scale_ref[0] = jnp.broadcast_to(scale * (sharpness / rows.shape[1] * gain), scale_ref.shape[1:])


def updated(duals, spend, limit):
    return jnp.maximum(0.0, duals + temper * jnp.log((spend + limit) / (2.0 * limit)))


def totals(match_ref, mine_ref, other_ref):
    return jnp.dot(
        match_ref[0], mine_ref[...], preferred_element_type=jnp.float32
    ) + jnp.dot(match_ref[1], other_ref[...], preferred_element_type=jnp.float32)


def start_rows(user_hbm, scale_hbm, user_ref, scale_ref, sem):
    def start(k, carry):
        pltpu.make_async_copy(user_hbm.at[k], user_ref.at[k], sem.at[0, k]).start()
        pltpu.make_async_copy(scale_hbm.at[k], scale_ref.at[k], sem.at[1, k]).start()
        return carry

    lax.fori_loop(0, user_ref.shape[0], start, 0)


def start_items(item_hbm, item_ref, sem):
    def start(k, carry):
        pltpu.make_async_copy(item_hbm.at[k], item_ref.at[k], sem.at[k]).start()
        return carry

    lax.fori_loop(0, item_ref.shape[0], start, 0)


def item_landed(item, item_ref, item_sem):
    pltpu.make_async_copy(item_ref.at[item], item_ref.at[item], item_sem.at[item]).wait()


def sweep_users(
    user_hbm, scale_hbm, user_ref, scale_ref, item_ref, row_sem, item_sem, item_scale_ref, dual_scr,
    dots_a, dots_b, finish, fanout
):
    clusters, users, _ = user_ref.shape
    camps = item_scale_ref.shape[1]
    width = item_ref.shape[2]
    rows = 64

    def landed(k):
        pltpu.make_async_copy(user_hbm.at[k], user_ref.at[k], row_sem.at[0, k]).wait()
        pltpu.make_async_copy(scale_hbm.at[k], scale_ref.at[k], row_sem.at[1, k]).wait()
        if item_sem is not None:
            for e in range(fanout):
                item_landed(k * fanout + e, item_ref, item_sem)

    def multiply(k, dots):
        blocks = item_ref[pl.ds(pl.multiple_of(k * fanout, fanout), fanout)].reshape(fanout * camps, width)
        dots[...] = lax.dot_general(
            user_ref[k], blocks, (((1,), (1,)), ((), ())), preferred_element_type=jnp.float32
        )

    def cluster(k, dots):
        first = pl.multiple_of(k * fanout, fanout)
        item_scale = item_scale_ref[pl.ds(first, fanout), :]
        shift = dual_scr[pl.ds(first, fanout), :]
        scales = [jnp.broadcast_to(item_scale[e : e + 1], (rows, camps)) for e in range(fanout)]
        shifts = [jnp.broadcast_to(shift[e : e + 1], (rows, camps)) for e in range(fanout)]
        sums = [jnp.zeros((8, camps), jnp.float32) for _ in range(fanout)]
        for start in range(0, users, rows):
            user_scale = scale_ref[k, start : start + rows, :]
            weights = []
            for e in range(fanout):
                raw = dots[start : start + rows, e * camps : (e + 1) * camps]
                weights.append(jnp.exp2(raw * user_scale * scales[e] - shifts[e]))
            den = 1.0 + jnp.sum(functools.reduce(jnp.add, weights), axis=1, keepdims=True)
            sums = finish(k, start, rows, weights, den, sums)
        finish(k, None, rows, None, None, sums)

    landed(0)
    multiply(0, dots_a)

    def two(n, carry):
        k = 2 * n
        landed(k + 1)

        @pl.when(k + 2 < clusters)
        def _():
            landed(k + 2)

        multiply(k + 1, dots_b)
        cluster(k, dots_a)
        multiply(jnp.minimum(k + 2, clusters - 1), dots_a)
        cluster(k + 1, dots_b)
        return carry

    lax.fori_loop(0, clusters // 2, two, 0)


def spend_finish(where_ref, size_ref, users, fanout, spend_scr):
    def finish(k, start, rows, weights, den, sums):
        if start is None:
            for e in range(fanout):
                spend_scr[pl.ds(k * fanout + e, 1), :] = jnp.sum(sums[e], axis=0, keepdims=True)
            return 0
        place = where_ref[1] * users + start + lax.broadcasted_iota(jnp.int32, (rows, 1), 0)
        share = jnp.where(place < size_ref[k], 1.0 / den, 0.0)
        out = []
        for e in range(fanout):
            part = weights[e] * share
            total = sums[e]
            for r in range(0, rows, 8):
                total = total + part[r : r + 8]
            out.append(total)
        return out

    return finish


def halves(where_ref, spend_scr, mine_ref, theirs_ref):
    count = mine_ref.shape[0]
    rep = where_ref[1]
    mine_ref[...] = spend_scr[pl.ds(pl.multiple_of(rep * count, count), count), :]
    theirs_ref[...] = spend_scr[pl.ds(pl.multiple_of((1 - rep) * count, count), count), :]


def item_facts(fact_ref, item_ref, item_sem, fact_sem, dual_ref, limit_ref, live_ref, item_scale_ref):
    items, camps = dual_ref.shape
    width = item_ref.shape[2]
    eye = lax.broadcasted_iota(jnp.int32, (camps, camps), 0) == lax.broadcasted_iota(jnp.int32, (camps, camps), 1)

    def wait(item, carry):
        item_landed(item, item_ref, item_sem)
        pltpu.make_async_copy(fact_ref.at[item], fact_ref.at[item], fact_sem.at[item]).wait()
        return carry

    lax.fori_loop(0, items, wait, 0, unroll=8)
    group = 8

    def some(n, carry):
        first = pl.multiple_of(n * group, group)
        facts = fact_ref[pl.ds(first, group)].astype(jnp.float32)
        dual_ref[pl.ds(first, group), :] = facts[:, 0] + facts[:, 1] + facts[:, 2]
        limit_ref[pl.ds(first, group), :] = facts[:, 3] + facts[:, 4] + facts[:, 5]
        live_ref[pl.ds(first, group), :] = facts[:, 6]
        totals_here = []
        for e in range(group):
            rows = item_ref[first + e].astype(jnp.float32)
            total = jnp.broadcast_to(jnp.sum(rows * rows, axis=1, keepdims=True), (camps, camps))
            totals_here.append(jnp.sum(jnp.where(eye, total, 0.0), axis=0, keepdims=True))
        mean = jnp.concatenate(totals_here, axis=0) * (1.0 / width)
        item_scale_ref[pl.ds(first, group), :] = lax.rsqrt(mean + epsilon)
        return carry

    lax.fori_loop(0, items // group, some, 0)


def first_kernel(
    shards, half, fanout, where_ref, size_ref, item_at_ref, own_ref, user_hbm, scale_hbm, camp_ref, fact_ref, *rest
):
    received, outs = rest[: 2 * (shards - 1)], rest[2 * (shards - 1) :][:7]
    mine_ref, theirs_ref, duals_ref, limit_ref, live_ref, item_scale_ref, item_out = outs
    user_ref, scale_ref, item_ref, row_sem, item_sem, dots_a, dots_b, dual_scr, spend_scr = rest[-12:-3]
    landed_ref, fact_sem, out_sem = rest[-3:]
    cap = 2 * half
    rep = where_ref[1]
    users = user_ref.shape[1]
    _, camps, width = camp_ref.shape
    pieces = fact_ref.shape[1]

    def fetch(slot, block, facts):
        item = item_at_ref[slot]

        @pl.when(item >= 0)
        def _():
            pltpu.make_async_copy(block, item_ref.at[item], item_sem.at[item]).start()
            pltpu.make_async_copy(facts, landed_ref.at[item], fact_sem.at[item]).start()

    for j in range(cap):
        fetch(j, camp_ref.at[own_ref[j]], fact_ref.at[own_ref[j]])
    for n in range(shards - 1):
        for j in range(half):
            for side, message in ((rep, received[2 * n]), (1 - rep, received[2 * n + 1])):
                rows, lanes = fact_place(j, half, camps, pieces, width)
                fetch((n + 1) * cap + side * half + j, message.at[pl.ds(j * camps, camps)], message.at[rows, lanes])
    start_rows(user_hbm, scale_hbm, user_ref, scale_ref, row_sem)
    item_facts(landed_ref, item_ref, item_sem, fact_sem, duals_ref, limit_ref, live_ref, item_scale_ref)
    keep = pltpu.make_async_copy(item_ref, item_out, out_sem)
    keep.start()
    dual_scr[...] = jnp.where(live_ref[...] > 0.5, duals_ref[...] * gain, masked)
    finish = spend_finish(where_ref, size_ref, users, fanout, spend_scr)
    sweep_users(
        user_hbm, scale_hbm, user_ref, scale_ref, item_ref, row_sem, None, item_scale_ref,
        dual_scr, dots_a, dots_b, finish, fanout
    )
    halves(where_ref, spend_scr, mine_ref, theirs_ref)
    keep.wait()


def second_kernel(
    fanout, where_ref, size_ref, duals_ref, live_ref, item_scale_ref, limit_ref, match_ref, got_ref, other_ref,
    user_hbm, scale_hbm, item_hbm, mine_ref, theirs_ref, next_ref, user_ref, scale_ref, item_ref, row_sem, item_sem,
    dots_a, dots_b, dual_scr, spend_scr
):
    start_items(item_hbm, item_ref, item_sem)
    start_rows(user_hbm, scale_hbm, user_ref, scale_ref, row_sem)
    duals = updated(duals_ref[...], totals(match_ref, got_ref, other_ref), limit_ref[...])
    next_ref[...] = duals
    dual_scr[...] = jnp.where(live_ref[...] > 0.5, duals * gain, masked)
    finish = spend_finish(where_ref, size_ref, user_ref.shape[1], fanout, spend_scr)
    sweep_users(
        user_hbm, scale_hbm, user_ref, scale_ref, item_ref, row_sem, item_sem, item_scale_ref,
        dual_scr, dots_a, dots_b, finish, fanout
    )
    halves(where_ref, spend_scr, mine_ref, theirs_ref)


def third_kernel(
    fanout, where_ref, size_ref, duals_ref, live_ref, item_scale_ref, limit_ref, match_ref, got_ref, other_ref,
    own_match_ref, got_one_ref, other_one_ref, own_dual_ref, own_limit_ref, user_hbm, scale_hbm, item_hbm,
    user_dual_ref, own_out_ref, user_ref, scale_ref, item_ref, row_sem, item_sem, dots_a, dots_b, dual_scr, row_scr
):
    start_items(item_hbm, item_ref, item_sem)
    start_rows(user_hbm, scale_hbm, user_ref, scale_ref, row_sem)
    duals = updated(duals_ref[...], totals(match_ref, got_ref, other_ref), limit_ref[...])
    dual_scr[...] = jnp.where(live_ref[...] > 0.5, duals * gain, masked)
    own = updated(own_dual_ref[...], totals(own_match_ref, got_one_ref, other_one_ref), own_limit_ref[...])
    own_out_ref[...] = updated(own, totals(own_match_ref, got_ref, other_ref), own_limit_ref[...])
    users = user_ref.shape[1]
    partial = []

    def finish(k, start, rows, weights, den, sums):
        if start is None:
            return 0
        lanes = 128
        offset = start % lanes
        wide = jnp.broadcast_to(den, (rows, lanes))
        eye = offset + lax.broadcasted_iota(jnp.int32, (rows, lanes), 0) == lax.broadcasted_iota(
            jnp.int32, (rows, lanes), 1
        )
        row = jnp.sum(jnp.where(eye, wide, 0.0), axis=0, keepdims=True)
        if offset:
            row = row + partial.pop()
        if offset + rows < lanes:
            partial.append(row)
            return sums
        base = start - offset
        place = where_ref[1] * users + base + lax.broadcasted_iota(jnp.int32, (1, lanes), 1)
        row_scr[k, base // lanes : base // lanes + 1, :] = jnp.where(
            place < size_ref[k], temper * jnp.log(row), 0.0
        )
        return sums

    sweep_users(
        user_hbm, scale_hbm, user_ref, scale_ref, item_ref, row_sem, item_sem, item_scale_ref,
        dual_scr, dots_a, dots_b, finish, fanout
    )
    for n in range(row_scr.shape[1]):
        user_dual_ref[:, n * 128 : (n + 1) * 128] = row_scr[:, n, :]


def program(
    user_emb, elig_owner, elig_local, cluster_size, camp_emb, camp_count, dual_init, spend_limit
):
    shards = lax.axis_size("shard")
    reps = lax.axis_size("rep")
    me = lax.axis_index("shard").astype(jnp.int32)
    rep = lax.axis_index("rep").astype(jnp.int32)
    clusters, users, width = user_emb.shape
    blocks, camps, _ = camp_emb.shape
    fanout = elig_owner.shape[1]
    items = clusters * fanout
    cap = 2 * items // shards
    half = cap // reps
    part = items // reps
    swap = [(0, 1), (1, 0)]
    f32 = jnp.float32

    owners = elig_owner.reshape(-1)
    locals_ = elig_local.reshape(-1)
    shard_ids = jnp.arange(shards, dtype=jnp.int32)
    hot = (owners[:, None] == shard_ids[None, :]).astype(jnp.int32)
    rank = jnp.sum((jnp.cumsum(hot, axis=0) - hot) * hot, axis=1)
    slot = owners * cap + rank
    hit = slot[:, None] == jnp.arange(shards * cap, dtype=jnp.int32)[None, :]
    wanted = jnp.sum(jnp.where(hit, locals_[:, None], 0), axis=0).reshape(shards, cap)
    names = owners * blocks + locals_
    ask = jnp.concatenate([wanted, jnp.broadcast_to(names[None, :], (shards, items))], axis=1)
    heard = lax.all_to_all(ask, "shard", split_axis=0, concat_axis=0, tiled=True)
    where = jnp.stack([me, rep])

    def pieces(x):
        out = []
        for _ in range(3):
            piece = lax.reduce_precision(x, exponent_bits=8, mantissa_bits=7)
            out.append(piece)
            x = x - piece
        return out

    live = (jnp.arange(camps, dtype=jnp.int32)[None, :] < camp_count[:, None]).astype(f32)
    rows = pieces(dual_init) + pieces(spend_limit) + [live, jnp.zeros_like(live)]
    facts = jnp.stack(rows, axis=1).astype(camp_emb.dtype)
    message = half * camps + -(-half * camps // width) * len(rows)
    camp_rows, facts = in_hbm(camp_emb), in_hbm(facts)

    order = send_order(shards)
    sent = {}
    for shifts in (order[:4], order[4:]):
        outs = pl.pallas_call(
            functools.partial(gather_kernel, half, shifts),
            out_shape=[pltpu.HBM((message, width), camp_emb.dtype)] * len(shifts),
            in_specs=[SMEM, SMEM, HBM, HBM],
            out_specs=[HBM] * len(shifts),
            scratch_shapes=[
                pltpu.VMEM((len(shifts), message, width), camp_emb.dtype),
                pltpu.SemaphoreType.DMA((3, len(shifts) * half)),
            ],
            compiler_params=pltpu.CompilerParams(vmem_limit_bytes=8 * 2**20),
            cost_estimate=pl.CostEstimate(flops=0, bytes_accessed=len(shifts) * 2**19, transcendentals=0),
        )(where, heard, camp_rows, facts)
        sent.update(zip(shifts, outs))

    got_blocks = {}
    for shift in order:
        got_blocks[shift] = lax.ppermute(sent[shift], "shard", [(i, i ^ shift) for i in range(shards)])

    heard, user_late, _ = lax.optimization_barrier((heard, user_emb, got_blocks[1]))
    all_names = heard[:, cap:]
    item_of_slot = (
        jnp.sum(
            jnp.where(
                ((owners ^ me) * cap + rank)[:, None] == jnp.arange(shards * cap, dtype=jnp.int32)[None, :],
                jnp.arange(1, items + 1, dtype=jnp.int32)[:, None],
                0,
            ),
            axis=0,
        )
        - 1
    )
    own_wanted = lax.dynamic_slice_in_dim(wanted, me, 1, 0).reshape(cap)
    user_scale = pl.pallas_call(
        user_kernel,
        out_shape=jax.ShapeDtypeStruct((clusters, users, camps), f32),
        grid=(clusters,),
        in_specs=[pl.BlockSpec((1, users, width), lambda k: (k, 0, 0))],
        out_specs=pl.BlockSpec((1, users, camps), lambda k: (k, 0, 0)),
        compiler_params=pltpu.CompilerParams(vmem_limit_bytes=16 * 2**20),
        cost_estimate=pl.CostEstimate(flops=8 * 2**20, bytes_accessed=8 * 2**20, transcendentals=0),
    )(in_hbm(user_late))

    def columns(which):
        return lax.dynamic_slice_in_dim(all_names, which * part, part, 1).reshape(1, -1)

    sides = (columns(rep), columns(1 - rep))
    own_names = me * blocks + jnp.arange(blocks, dtype=jnp.int32)
    match = jnp.stack([(names[:, None] == side).astype(jnp.bfloat16) for side in sides])
    own_match = jnp.stack([(own_names[:, None] == side).astype(jnp.bfloat16) for side in sides])

    gate = 2
    got_blocks[gate], item_of_slot, own_wanted, user_scale, match, own_match = lax.optimization_barrier(
        (got_blocks[gate], item_of_slot, own_wanted, user_scale, match, own_match)
    )
    received = []
    for shift in range(1, shards):
        received += [got_blocks[shift], lax.ppermute(got_blocks[shift], "rep", swap)]
    user_rows, user_scale = in_hbm(user_emb), in_hbm(user_scale)

    def exchange(mine, theirs):
        total = mine + lax.ppermute(theirs, "rep", swap)
        spread = jnp.broadcast_to(total.astype(jnp.bfloat16)[None], (shards, part, camps))
        got = lax.all_to_all(spread, "shard", split_axis=0, concat_axis=0, tiled=True)
        got = got.reshape(shards * part, camps)
        return in_vmem(got), in_vmem(lax.ppermute(got, "rep", swap))

    spend_out = [jax.ShapeDtypeStruct((part, camps), f32)] * 2
    work = [
        pltpu.VMEM((clusters, users, width), user_emb.dtype),
        pltpu.VMEM((clusters, users, camps), f32),
        pltpu.VMEM((items, camps, width), camp_emb.dtype),
        pltpu.SemaphoreType.DMA((2, clusters)),
        pltpu.SemaphoreType.DMA((items,)),
        pltpu.VMEM((users, fanout * camps), f32),
        pltpu.VMEM((users, fanout * camps), f32),
        pltpu.VMEM((items, camps), f32),
    ]
    spend_work = [pltpu.VMEM((items, camps), f32)]
    limits = pltpu.CompilerParams(vmem_limit_bytes=24 * 2**20)

    mine, theirs, item_dual, item_limit, item_live, item_scale, item_emb = pl.pallas_call(
        functools.partial(first_kernel, shards, half, fanout),
        out_shape=spend_out
        + [jax.ShapeDtypeStruct((items, camps), f32)] * 4
        + [pltpu.HBM((items, camps, width), camp_emb.dtype)],
        in_specs=[SMEM] * 4 + [HBM] * 4 + [ANY] * len(received),
        out_specs=[VMEM] * 6 + [HBM],
        scratch_shapes=work
        + spend_work
        + [
            pltpu.VMEM((items, len(rows), camps), camp_emb.dtype),
            pltpu.SemaphoreType.DMA((items,)),
            pltpu.SemaphoreType.DMA,
        ],
        compiler_params=limits,
    )(where, cluster_size, item_of_slot, own_wanted, user_rows, user_scale, camp_rows, facts, *received)
    item_emb = in_hbm(item_emb)
    got_one, other_one = exchange(mine, theirs)

    mine, theirs, next_dual = pl.pallas_call(
        functools.partial(second_kernel, fanout),
        out_shape=spend_out + [jax.ShapeDtypeStruct((items, camps), f32)],
        in_specs=[SMEM] * 2 + [VMEM] * 7 + [HBM] * 3,
        out_specs=[VMEM] * 3,
        scratch_shapes=work + spend_work,
        compiler_params=limits,
    )(where, cluster_size, item_dual, item_live, item_scale, item_limit, match, got_one, other_one, user_rows,
      user_scale, item_emb)
    got_two, other_two = exchange(mine, theirs)

    user_dual, own_dual = pl.pallas_call(
        functools.partial(third_kernel, fanout),
        out_shape=[
            jax.ShapeDtypeStruct((clusters, users), f32),
            jax.ShapeDtypeStruct((blocks, camps), f32),
        ],
        in_specs=[SMEM] * 2 + [VMEM] * 12 + [HBM] * 3,
        out_specs=[VMEM] * 2,
        scratch_shapes=work + [pltpu.VMEM((clusters, users // 128, 128), f32)],
        compiler_params=limits,
    )(where, cluster_size, next_dual, item_live, item_scale, item_limit, match, got_two, other_two, own_match,
      got_one, other_one, dual_init, spend_limit, user_rows, user_scale, item_emb)
    return (user_dual, own_dual)


def solution(mesh):
    return jax.shard_map(
        program,
        mesh=mesh,
        in_specs=(
            P("shard", "rep", None),
            P("shard", None),
            P("shard", None),
            P("shard"),
            P("shard", None, None),
            P("shard"),
            P("shard", None),
            P("shard", None),
        ),
        out_specs=(P("shard", "rep"), P("shard", None)),
        check_vma=False,
    )
```

```python
import functools
import math

import jax
import jax.numpy as jnp
from jax import lax
from jax.experimental import pallas as pl
from jax.experimental.pallas import tpu as pltpu
from jax.sharding import PartitionSpec as P


epsilon = 1e-06
temper = 0.25
sharpness = 16.0
gain = 1.0 / (temper * math.log(2.0))
masked = 1e30


VMEM = pl.BlockSpec(memory_space=pltpu.VMEM)
SMEM = pl.BlockSpec(memory_space=pltpu.SMEM)
ANY = pl.BlockSpec(memory_space=pl.ANY)
HBM = pl.BlockSpec(memory_space=pltpu.HBM)


def in_hbm(x):
    return pltpu.with_memory_space_constraint(x, pltpu.HBM)


def in_vmem(x):
    return pltpu.with_memory_space_constraint(x, pltpu.VMEM)


def send_order(shards):
    top = shards // 2
    far = [top + n for n in range(top)]
    first = far[: top // 2]
    return first + list(range(1, top)) + far[top // 2 :]


def fact_place(j, half, camps, pieces, width):
    across = width // camps
    return pl.ds(half * camps + j // across * pieces, pieces), pl.ds(j % across * camps, camps)


def gather_kernel(half, sends, where_ref, asked_ref, camp_ref, fact_ref, *rest):
    outs, (stage, sem) = rest[:-2], rest[-2:]
    me, rep = where_ref[0], where_ref[1]
    _, camps, width = camp_ref.shape
    pieces = fact_ref.shape[1]
    arriving, leaving = [], []
    for n, ((shift, other), out) in enumerate(zip(sends, outs)):
        for j in range(half):
            block = asked_ref[me ^ shift, (1 - rep if other else rep) * half + j]
            rows, lanes = fact_place(j, half, camps, pieces, width)
            for copy in (
                pltpu.make_async_copy(
                    camp_ref.at[block], stage.at[n, pl.ds(j * camps, camps)], sem.at[0, n * half + j]
                ),
                pltpu.make_async_copy(fact_ref.at[block], stage.at[n, rows, lanes], sem.at[1, n * half + j]),
            ):
                copy.start()
                arriving.append(copy)
        leaving.append(pltpu.make_async_copy(stage.at[n], out, sem.at[2, n]))
    for copy in arriving:
        copy.wait()
    eye = lax.broadcasted_iota(jnp.int32, (camps, camps), 0) == lax.broadcasted_iota(jnp.int32, (camps, camps), 1)
    piece = lax.broadcasted_iota(jnp.int32, (pieces, camps), 0)

    def scales(n, carry):
        for j in range(half):
            block = stage[n, j * camps : (j + 1) * camps].astype(jnp.float32)
            total = jnp.broadcast_to(jnp.sum(block * block, axis=1, keepdims=True), (camps, camps))
            total = jnp.sum(jnp.where(eye, total, 0.0), axis=0, keepdims=True)
            rows, lanes = fact_place(j, half, camps, pieces, width)
            facts = stage[n, rows, lanes].astype(jnp.float32)
            scale = lax.rsqrt(total * (1.0 / width) + epsilon) * facts[pieces - 2 : pieces - 1]
            high = scale.astype(jnp.bfloat16).astype(jnp.float32)
            facts = jnp.where(piece == pieces - 2, high, jnp.where(piece == pieces - 1, scale - high, facts))
            stage[n, rows, lanes] = facts.astype(stage.dtype)
        return carry

    lax.fori_loop(0, len(sends), scales, 0, unroll=3 if len(sends) % 3 == 0 else 2 if len(sends) % 2 == 0 else 1)
    for copy in leaving:
        copy.start()
    for copy in leaving:
        copy.wait()


def user_kernel(user_ref, scale_ref):
    rows = user_ref[0].astype(jnp.float32)
    scale = lax.rsqrt(jnp.sum(rows * rows, axis=1, keepdims=True) * (1.0 / rows.shape[1]) + epsilon)
    scale_ref[0] = jnp.broadcast_to(scale * (sharpness / rows.shape[1] * gain), scale_ref.shape[1:])


def updated(duals, spend, limit):
    return jnp.maximum(0.0, duals + temper * jnp.log((spend + limit) / (2.0 * limit)))


def totals(match_ref, mine_ref, other_ref):
    return jnp.dot(
        match_ref[0], mine_ref[...], preferred_element_type=jnp.float32
    ) + jnp.dot(match_ref[1], other_ref[...], preferred_element_type=jnp.float32)


def start_rows(user_hbm, scale_hbm, user_ref, scale_ref, sem):
    def start(k, carry):
        pltpu.make_async_copy(user_hbm.at[k], user_ref.at[k], sem.at[0, k]).start()
        pltpu.make_async_copy(scale_hbm.at[k], scale_ref.at[k], sem.at[1, k]).start()
        return carry

    lax.fori_loop(0, user_ref.shape[0], start, 0)


def start_items(item_hbm, item_ref, sem):
    def start(k, carry):
        pltpu.make_async_copy(item_hbm.at[k], item_ref.at[k], sem.at[k]).start()
        return carry

    lax.fori_loop(0, item_ref.shape[0], start, 0)


def item_landed(item, item_ref, item_sem):
    pltpu.make_async_copy(item_ref.at[item], item_ref.at[item], item_sem.at[item]).wait()


def sweep_users(
    user_hbm, scale_hbm, user_ref, scale_ref, item_ref, row_sem, item_sem, item_scale_ref, dual_scr,
    dots_a, dots_b, finish, fanout
):
    clusters, users, _ = user_ref.shape
    camps = item_scale_ref.shape[1]
    width = item_ref.shape[2]
    rows = 64

    def landed(k):
        pltpu.make_async_copy(user_hbm.at[k], user_ref.at[k], row_sem.at[0, k]).wait()
        pltpu.make_async_copy(scale_hbm.at[k], scale_ref.at[k], row_sem.at[1, k]).wait()
        if item_sem is not None:
            for e in range(fanout):
                item_landed(k * fanout + e, item_ref, item_sem)

    def multiply(k, dots):
        blocks = item_ref[pl.ds(pl.multiple_of(k * fanout, fanout), fanout)].reshape(fanout * camps, width)
        dots[...] = lax.dot_general(
            user_ref[k], blocks, (((1,), (1,)), ((), ())), preferred_element_type=jnp.float32
        )

    def cluster(k, dots):
        first = pl.multiple_of(k * fanout, fanout)
        item_scale = item_scale_ref[pl.ds(first, fanout), :]
        shift = dual_scr[pl.ds(first, fanout), :]
        scales = [jnp.broadcast_to(item_scale[e : e + 1], (rows, camps)) for e in range(fanout)]
        shifts = [jnp.broadcast_to(shift[e : e + 1], (rows, camps)) for e in range(fanout)]
        sums = [jnp.zeros((8, camps), jnp.float32) for _ in range(fanout)]
        for start in range(0, users, rows):
            user_scale = scale_ref[k, start : start + rows, :]
            weights = []
            for e in range(fanout):
                raw = dots[start : start + rows, e * camps : (e + 1) * camps]
                weights.append(jnp.exp2(raw * user_scale * scales[e] - shifts[e]))
            den = 1.0 + jnp.sum(functools.reduce(jnp.add, weights), axis=1, keepdims=True)
            sums = finish(k, start, rows, weights, den, sums)
        finish(k, None, rows, None, None, sums)

    landed(0)
    multiply(0, dots_a)

    def two(n, carry):
        k = 2 * n
        landed(k + 1)

        @pl.when(k + 2 < clusters)
        def _():
            landed(k + 2)

        multiply(k + 1, dots_b)
        cluster(k, dots_a)
        multiply(jnp.minimum(k + 2, clusters - 1), dots_a)
        cluster(k + 1, dots_b)
        return carry

    lax.fori_loop(0, clusters // 2, two, 0)


def spend_finish(where_ref, size_ref, users, fanout, spend_scr):
    def finish(k, start, rows, weights, den, sums):
        if start is None:
            for e in range(fanout):
                spend_scr[pl.ds(k * fanout + e, 1), :] = jnp.sum(sums[e], axis=0, keepdims=True)
            return 0
        left = size_ref[k] - where_ref[1] * users - start
        share = jnp.where(lax.broadcasted_iota(jnp.int32, (rows, 1), 0) < left, 1.0 / den, 0.0)
        out = []
        for e in range(fanout):
            part = weights[e] * share
            total = sums[e]
            for r in range(0, rows, 8):
                total = total + part[r : r + 8]
            out.append(total)
        return out

    return finish


def halves(where_ref, spend_scr, mine_ref, theirs_ref):
    count = mine_ref.shape[0]
    rep = where_ref[1]
    mine_ref[...] = spend_scr[pl.ds(pl.multiple_of(rep * count, count), count), :]
    theirs_ref[...] = spend_scr[pl.ds(pl.multiple_of((1 - rep) * count, count), count), :]


def item_facts(fact_ref, item_ref, item_sem, fact_sem, dual_ref, limit_ref, live_ref, item_scale_ref):
    items = dual_ref.shape[0]

    def wait(item, carry):
        item_landed(item, item_ref, item_sem)
        pltpu.make_async_copy(fact_ref.at[item], fact_ref.at[item], fact_sem.at[item]).wait()
        return carry

    lax.fori_loop(0, items, wait, 0, unroll=8)
    group = 8
    for first in range(0, items, group):
        facts = fact_ref[first : first + group].astype(jnp.float32)
        here = slice(first, first + group)
        dual_ref[here, :] = facts[:, 0] + facts[:, 1] + facts[:, 2]
        limit_ref[here, :] = facts[:, 3] + facts[:, 4] + facts[:, 5]
        live_ref[here, :] = facts[:, 6]
        item_scale_ref[here, :] = facts[:, 6] + facts[:, 7]


def first_kernel(
    shards, half, fanout, camps, pieces, where_ref, size_ref, item_at_ref, user_hbm, scale_hbm, *rest
):
    received, outs = rest[: 2 * shards], rest[2 * shards :][:7]
    mine_ref, theirs_ref, duals_ref, limit_ref, live_ref, item_scale_ref, item_out = outs
    user_ref, scale_ref, item_ref, row_sem, item_sem, dots_a, dots_b, dual_scr, spend_scr = rest[-12:-3]
    landed_ref, fact_sem, out_sem = rest[-3:]
    cap = 2 * half
    rep = where_ref[1]
    users = user_ref.shape[1]
    width = item_ref.shape[2]

    def fetch(slot, block, facts):
        item = item_at_ref[slot]

        @pl.when(item >= 0)
        def _():
            pltpu.make_async_copy(block, item_ref.at[item], item_sem.at[item]).start()
            pltpu.make_async_copy(facts, landed_ref.at[item], fact_sem.at[item]).start()

    for n in range(shards):
        for j in range(half):
            for side, message in ((rep, received[2 * n]), (1 - rep, received[2 * n + 1])):
                rows, lanes = fact_place(j, half, camps, pieces, width)
                fetch(n * cap + side * half + j, message.at[pl.ds(j * camps, camps)], message.at[rows, lanes])
    start_rows(user_hbm, scale_hbm, user_ref, scale_ref, row_sem)
    item_facts(landed_ref, item_ref, item_sem, fact_sem, duals_ref, limit_ref, live_ref, item_scale_ref)
    keep = pltpu.make_async_copy(item_ref, item_out, out_sem)
    keep.start()
    dual_scr[...] = jnp.where(live_ref[...] > 0.0, duals_ref[...] * gain, masked)
    finish = spend_finish(where_ref, size_ref, users, fanout, spend_scr)
    sweep_users(
        user_hbm, scale_hbm, user_ref, scale_ref, item_ref, row_sem, None, item_scale_ref,
        dual_scr, dots_a, dots_b, finish, fanout
    )
    halves(where_ref, spend_scr, mine_ref, theirs_ref)
    keep.wait()


def second_kernel(
    fanout, where_ref, size_ref, duals_ref, live_ref, item_scale_ref, limit_ref, match_ref, got_ref, other_ref,
    user_hbm, scale_hbm, item_hbm, mine_ref, theirs_ref, next_ref, user_ref, scale_ref, item_ref, row_sem, item_sem,
    dots_a, dots_b, dual_scr, spend_scr
):
    start_items(item_hbm, item_ref, item_sem)
    start_rows(user_hbm, scale_hbm, user_ref, scale_ref, row_sem)
    duals = updated(duals_ref[...], totals(match_ref, got_ref, other_ref), limit_ref[...])
    next_ref[...] = duals
    dual_scr[...] = jnp.where(live_ref[...] > 0.0, duals * gain, masked)
    finish = spend_finish(where_ref, size_ref, user_ref.shape[1], fanout, spend_scr)
    sweep_users(
        user_hbm, scale_hbm, user_ref, scale_ref, item_ref, row_sem, item_sem, item_scale_ref,
        dual_scr, dots_a, dots_b, finish, fanout
    )
    halves(where_ref, spend_scr, mine_ref, theirs_ref)


def third_kernel(
    fanout, where_ref, size_ref, duals_ref, live_ref, item_scale_ref, limit_ref, match_ref, got_ref, other_ref,
    own_match_ref, got_one_ref, other_one_ref, own_dual_ref, own_limit_ref, user_hbm, scale_hbm, item_hbm,
    user_dual_ref, own_out_ref, user_ref, scale_ref, item_ref, row_sem, item_sem, dots_a, dots_b, dual_scr, row_scr
):
    start_items(item_hbm, item_ref, item_sem)
    start_rows(user_hbm, scale_hbm, user_ref, scale_ref, row_sem)
    duals = updated(duals_ref[...], totals(match_ref, got_ref, other_ref), limit_ref[...])
    dual_scr[...] = jnp.where(live_ref[...] > 0.0, duals * gain, masked)
    own = updated(own_dual_ref[...], totals(own_match_ref, got_one_ref, other_one_ref), own_limit_ref[...])
    own_out_ref[...] = updated(own, totals(own_match_ref, got_ref, other_ref), own_limit_ref[...])
    users = user_ref.shape[1]
    partial = []

    def finish(k, start, rows, weights, den, sums):
        if start is None:
            return 0
        lanes = 128
        offset = start % lanes
        wide = jnp.broadcast_to(den, (rows, lanes))
        eye = offset + lax.broadcasted_iota(jnp.int32, (rows, lanes), 0) == lax.broadcasted_iota(
            jnp.int32, (rows, lanes), 1
        )
        row = jnp.sum(jnp.where(eye, wide, 0.0), axis=0, keepdims=True)
        if offset:
            row = row + partial.pop()
        if offset + rows < lanes:
            partial.append(row)
            return sums
        base = start - offset
        place = where_ref[1] * users + base + lax.broadcasted_iota(jnp.int32, (1, lanes), 1)
        row_scr[k, base // lanes : base // lanes + 1, :] = jnp.where(
            place < size_ref[k], temper * jnp.log(row), 0.0
        )
        return sums

    sweep_users(
        user_hbm, scale_hbm, user_ref, scale_ref, item_ref, row_sem, item_sem, item_scale_ref,
        dual_scr, dots_a, dots_b, finish, fanout
    )
    for n in range(row_scr.shape[1]):
        user_dual_ref[:, n * 128 : (n + 1) * 128] = row_scr[:, n, :]


def program(
    user_emb, elig_owner, elig_local, cluster_size, camp_emb, camp_count, dual_init, spend_limit
):
    shards = lax.axis_size("shard")
    reps = lax.axis_size("rep")
    me = lax.axis_index("shard").astype(jnp.int32)
    rep = lax.axis_index("rep").astype(jnp.int32)
    clusters, users, width = user_emb.shape
    blocks, camps, _ = camp_emb.shape
    fanout = elig_owner.shape[1]
    items = clusters * fanout
    cap = 2 * items // shards
    half = cap // reps
    part = items // reps
    swap = [(0, 1), (1, 0)]
    f32 = jnp.float32

    owners = elig_owner.T.reshape(-1)
    locals_ = elig_local.T.reshape(-1)
    asked = jnp.arange(items, dtype=jnp.int32)
    item_ids = asked % clusters * fanout + asked // clusters
    shard_ids = jnp.arange(shards, dtype=jnp.int32)
    hot = (owners[:, None] == shard_ids[None, :]).astype(jnp.int32)
    rank = jnp.sum((jnp.cumsum(hot, axis=0) - hot) * hot, axis=1)
    slot = owners * cap + rank
    hit = slot[:, None] == jnp.arange(shards * cap, dtype=jnp.int32)[None, :]
    wanted = jnp.sum(jnp.where(hit, locals_[:, None], 0), axis=0).reshape(shards, cap)
    names = owners * blocks + locals_
    ask = jnp.concatenate([wanted, jnp.broadcast_to(names[None, :], (shards, items))], axis=1)
    heard = lax.all_to_all(ask, "shard", split_axis=0, concat_axis=0, tiled=True)
    where = jnp.stack([me, rep])

    def pieces(x):
        out = []
        for _ in range(3):
            piece = lax.reduce_precision(x, exponent_bits=8, mantissa_bits=7)
            out.append(piece)
            x = x - piece
        return out

    live = (jnp.arange(camps, dtype=jnp.int32)[None, :] < camp_count[:, None]).astype(f32)
    rows = pieces(dual_init) + pieces(spend_limit) + [live, jnp.zeros_like(live)]
    facts = jnp.stack(rows, axis=1).astype(camp_emb.dtype)
    message = half * camps + -(-half * camps // width) * len(rows)
    camp_rows, facts = in_hbm(camp_emb), in_hbm(facts)

    order = send_order(shards)
    sent = {}
    sends = [(shift, False) for shift in order] + [(0, False), (0, True)]
    for some in (sends[:2], sends[2:]):
        outs = pl.pallas_call(
            functools.partial(gather_kernel, half, some),
            out_shape=[pltpu.HBM((message, width), camp_emb.dtype)] * len(some),
            in_specs=[SMEM, SMEM, HBM, HBM],
            out_specs=[HBM] * len(some),
            scratch_shapes=[
                pltpu.VMEM((len(some), message, width), camp_emb.dtype),
                pltpu.SemaphoreType.DMA((3, len(some) * half)),
            ],
            compiler_params=pltpu.CompilerParams(vmem_limit_bytes=12 * 2**20),
            cost_estimate=pl.CostEstimate(flops=0, bytes_accessed=len(some) * 2**19, transcendentals=0),
        )(where, heard, camp_rows, facts)
        sent.update(zip(some, outs))

    got_blocks = {}
    for shift in order:
        got_blocks[shift] = lax.ppermute(sent[shift, False], "shard", [(i, i ^ shift) for i in range(shards)])

    heard, user_late, _ = lax.optimization_barrier((heard, user_emb, got_blocks[1]))
    all_names = heard[:, cap:].reshape(shards, fanout, clusters).transpose(0, 2, 1).reshape(shards, items)
    names = names.reshape(fanout, clusters).T.reshape(-1)
    item_of_slot = (
        jnp.sum(
            jnp.where(
                ((owners ^ me) * cap + rank)[:, None] == jnp.arange(shards * cap, dtype=jnp.int32)[None, :],
                (item_ids + 1)[:, None],
                0,
            ),
            axis=0,
        )
        - 1
    )
    user_scale = pl.pallas_call(
        user_kernel,
        out_shape=jax.ShapeDtypeStruct((clusters, users, camps), f32),
        grid=(clusters,),
        in_specs=[pl.BlockSpec((1, users, width), lambda k: (k, 0, 0))],
        out_specs=pl.BlockSpec((1, users, camps), lambda k: (k, 0, 0)),
        compiler_params=pltpu.CompilerParams(vmem_limit_bytes=16 * 2**20),
        cost_estimate=pl.CostEstimate(flops=8 * 2**20, bytes_accessed=8 * 2**20, transcendentals=0),
    )(in_hbm(user_late))

    def columns(which):
        return lax.dynamic_slice_in_dim(all_names, which * part, part, 1).reshape(1, -1)

    sides = (columns(rep), columns(1 - rep))
    own_names = me * blocks + jnp.arange(blocks, dtype=jnp.int32)
    match = jnp.stack([(names[:, None] == side).astype(jnp.bfloat16) for side in sides])
    own_match = jnp.stack([(own_names[:, None] == side).astype(jnp.bfloat16) for side in sides])

    gate = 2
    got_blocks[gate], item_of_slot, user_scale, match, own_match = lax.optimization_barrier(
        (got_blocks[gate], item_of_slot, user_scale, match, own_match)
    )
    received = [sent[0, False], sent[0, True]]
    for shift in range(1, shards):
        received += [got_blocks[shift], lax.ppermute(got_blocks[shift], "rep", swap)]
    user_rows, user_scale = in_hbm(user_emb), in_hbm(user_scale)

    def exchange(mine, theirs):
        total = mine + lax.ppermute(theirs, "rep", swap)
        spread = jnp.broadcast_to(total.astype(jnp.bfloat16)[None], (shards, part, camps))
        got = lax.all_to_all(spread, "shard", split_axis=0, concat_axis=0, tiled=True)
        got = got.reshape(shards * part, camps)
        return in_vmem(got), in_vmem(lax.ppermute(got, "rep", swap))

    spend_out = [jax.ShapeDtypeStruct((part, camps), f32)] * 2
    work = [
        pltpu.VMEM((clusters, users, width), user_emb.dtype),
        pltpu.VMEM((clusters, users, camps), f32),
        pltpu.VMEM((items, camps, width), camp_emb.dtype),
        pltpu.SemaphoreType.DMA((2, clusters)),
        pltpu.SemaphoreType.DMA((items,)),
        pltpu.VMEM((users, fanout * camps), f32),
        pltpu.VMEM((users, fanout * camps), f32),
        pltpu.VMEM((items, camps), f32),
    ]
    spend_work = [pltpu.VMEM((items, camps), f32)]
    limits = pltpu.CompilerParams(vmem_limit_bytes=24 * 2**20)

    mine, theirs, item_dual, item_limit, item_live, item_scale, item_emb = pl.pallas_call(
        functools.partial(first_kernel, shards, half, fanout, camps, len(rows)),
        out_shape=spend_out
        + [jax.ShapeDtypeStruct((items, camps), f32)] * 4
        + [pltpu.HBM((items, camps, width), camp_emb.dtype)],
        in_specs=[SMEM] * 3 + [HBM] * 2 + [ANY] * len(received),
        out_specs=[VMEM] * 6 + [HBM],
        scratch_shapes=work
        + spend_work
        + [
            pltpu.VMEM((items, len(rows), camps), camp_emb.dtype),
            pltpu.SemaphoreType.DMA((items,)),
            pltpu.SemaphoreType.DMA,
        ],
        compiler_params=limits,
    )(where, cluster_size, item_of_slot, user_rows, user_scale, *received)
    item_emb = in_hbm(item_emb)
    got_one, other_one = exchange(mine, theirs)

    mine, theirs, next_dual = pl.pallas_call(
        functools.partial(second_kernel, fanout),
        out_shape=spend_out + [jax.ShapeDtypeStruct((items, camps), f32)],
        in_specs=[SMEM] * 2 + [VMEM] * 7 + [HBM] * 3,
        out_specs=[VMEM] * 3,
        scratch_shapes=work + spend_work,
        compiler_params=limits,
    )(where, cluster_size, item_dual, item_live, item_scale, item_limit, match, got_one, other_one, user_rows,
      user_scale, item_emb)
    got_two, other_two = exchange(mine, theirs)

    user_dual, own_dual = pl.pallas_call(
        functools.partial(third_kernel, fanout),
        out_shape=[
            jax.ShapeDtypeStruct((clusters, users), f32),
            jax.ShapeDtypeStruct((blocks, camps), f32),
        ],
        in_specs=[SMEM] * 2 + [VMEM] * 12 + [HBM] * 3,
        out_specs=[VMEM] * 2,
        scratch_shapes=work + [pltpu.VMEM((clusters, users // 128, 128), f32)],
        compiler_params=limits,
    )(where, cluster_size, next_dual, item_live, item_scale, item_limit, match, got_two, other_two, own_match,
      got_one, other_one, dual_init, spend_limit, user_rows, user_scale, item_emb)
    return (user_dual, own_dual)


def solution(mesh):
    return jax.shard_map(
        program,
        mesh=mesh,
        in_specs=(
            P("shard", "rep", None),
            P("shard", None),
            P("shard", None),
            P("shard"),
            P("shard", None, None),
            P("shard"),
            P("shard", None),
            P("shard", None),
        ),
        out_specs=(P("shard", "rep"), P("shard", None)),
        check_vma=False,
    )
```

```python
import functools
import math

import jax
import jax.numpy as jnp
from jax import lax
from jax.experimental import pallas as pl
from jax.experimental.pallas import tpu as pltpu
from jax.sharding import PartitionSpec as P


epsilon = 1e-06
temper = 0.25
sharpness = 16.0
gain = 1.0 / (temper * math.log(2.0))
masked = 1e30


VMEM = pl.BlockSpec(memory_space=pltpu.VMEM)
SMEM = pl.BlockSpec(memory_space=pltpu.SMEM)
ANY = pl.BlockSpec(memory_space=pl.ANY)
HBM = pl.BlockSpec(memory_space=pltpu.HBM)


def in_hbm(x):
    return pltpu.with_memory_space_constraint(x, pltpu.HBM)


def in_vmem(x):
    return pltpu.with_memory_space_constraint(x, pltpu.VMEM)


def send_order(shards):
    top = shards // 2
    far = [top + n for n in range(top)]
    first = far[: top // 2]
    return first + list(range(1, top)) + far[top // 2 :]


def fact_place(j, half, camps, pieces, width):
    across = width // camps
    return pl.ds(half * camps + j // across * pieces, pieces), pl.ds(j % across * camps, camps)


def gather_kernel(half, sends, where_ref, asked_ref, camp_ref, fact_ref, *rest):
    outs, (stage, sem) = rest[:-2], rest[-2:]
    me, rep = where_ref[0], where_ref[1]
    _, camps, width = camp_ref.shape
    pieces = fact_ref.shape[1]
    arriving, leaving = [], []
    for n, ((shift, other), out) in enumerate(zip(sends, outs)):
        for j in range(half):
            block = asked_ref[me ^ shift, (1 - rep if other else rep) * half + j]
            rows, lanes = fact_place(j, half, camps, pieces, width)
            for copy in (
                pltpu.make_async_copy(
                    camp_ref.at[block], stage.at[n, pl.ds(j * camps, camps)], sem.at[0, n * half + j]
                ),
                pltpu.make_async_copy(fact_ref.at[block], stage.at[n, rows, lanes], sem.at[1, n * half + j]),
            ):
                copy.start()
                arriving.append(copy)
        leaving.append(pltpu.make_async_copy(stage.at[n], out, sem.at[2, n]))
    for copy in arriving:
        copy.wait()
    eye = lax.broadcasted_iota(jnp.int32, (camps, camps), 0) == lax.broadcasted_iota(jnp.int32, (camps, camps), 1)
    piece = lax.broadcasted_iota(jnp.int32, (pieces, camps), 0)

    def scales(n, carry):
        for j in range(half):
            block = stage[n, j * camps : (j + 1) * camps].astype(jnp.float32)
            total = jnp.broadcast_to(jnp.sum(block * block, axis=1, keepdims=True), (camps, camps))
            total = jnp.sum(jnp.where(eye, total, 0.0), axis=0, keepdims=True)
            rows, lanes = fact_place(j, half, camps, pieces, width)
            facts = stage[n, rows, lanes].astype(jnp.float32)
            scale = lax.rsqrt(total * (1.0 / width) + epsilon) * facts[pieces - 2 : pieces - 1]
            high = scale.astype(jnp.bfloat16).astype(jnp.float32)
            facts = jnp.where(piece == pieces - 2, high, jnp.where(piece == pieces - 1, scale - high, facts))
            stage[n, rows, lanes] = facts.astype(stage.dtype)
        return carry

    lax.fori_loop(0, len(sends), scales, 0, unroll=3 if len(sends) % 3 == 0 else 2 if len(sends) % 2 == 0 else 1)
    for copy in leaving:
        copy.start()
    for copy in leaving:
        copy.wait()


def user_kernel(user_ref, scale_ref):
    rows = user_ref[0].astype(jnp.float32)
    scale = lax.rsqrt(jnp.sum(rows * rows, axis=1, keepdims=True) * (1.0 / rows.shape[1]) + epsilon)
    scale_ref[0] = jnp.broadcast_to(scale * (sharpness / rows.shape[1] * gain), scale_ref.shape[1:])


def updated(duals, spend, limit):
    return jnp.maximum(0.0, duals + temper * jnp.log((spend + limit) / (2.0 * limit)))


def totals(match_ref, mine_ref, other_ref):
    return jnp.dot(
        match_ref[0], mine_ref[...], preferred_element_type=jnp.float32
    ) + jnp.dot(match_ref[1], other_ref[...], preferred_element_type=jnp.float32)


def start_rows(user_hbm, scale_hbm, user_ref, scale_ref, sem):
    def start(k, carry):
        pltpu.make_async_copy(user_hbm.at[k], user_ref.at[k], sem.at[0, k]).start()
        pltpu.make_async_copy(scale_hbm.at[k], scale_ref.at[k], sem.at[1, k]).start()
        return carry

    lax.fori_loop(0, user_ref.shape[0], start, 0)


def start_items(item_hbm, item_ref, sem):
    def start(k, carry):
        pltpu.make_async_copy(item_hbm.at[k], item_ref.at[k], sem.at[k]).start()
        return carry

    lax.fori_loop(0, item_ref.shape[0], start, 0)


def item_landed(item, item_ref, item_sem):
    pltpu.make_async_copy(item_ref.at[item], item_ref.at[item], item_sem.at[item]).wait()


def sweep_users(
    user_hbm, scale_hbm, user_ref, scale_ref, item_ref, row_sem, item_sem, item_scale_ref, dual_scr,
    dots_a, dots_b, finish, fanout, keep=None
):
    clusters, users, _ = user_ref.shape
    camps = item_scale_ref.shape[1]
    width = item_ref.shape[2]
    rows = 64

    def landed(k):
        pltpu.make_async_copy(user_hbm.at[k], user_ref.at[k], row_sem.at[0, k]).wait()
        pltpu.make_async_copy(scale_hbm.at[k], scale_ref.at[k], row_sem.at[1, k]).wait()
        for e in range(fanout):
            item_landed(k * fanout + e, item_ref, item_sem)
        if keep is not None:
            keep(k).start()

    def multiply(k, dots):
        blocks = item_ref[pl.ds(pl.multiple_of(k * fanout, fanout), fanout)].reshape(fanout * camps, width)
        dots[...] = lax.dot_general(
            user_ref[k], blocks, (((1,), (1,)), ((), ())), preferred_element_type=jnp.float32
        )

    def cluster(k, dots):
        first = pl.multiple_of(k * fanout, fanout)
        item_scale = item_scale_ref[pl.ds(first, fanout), :]
        shift = dual_scr[pl.ds(first, fanout), :]
        scales = [jnp.broadcast_to(item_scale[e : e + 1], (rows, camps)) for e in range(fanout)]
        shifts = [jnp.broadcast_to(shift[e : e + 1], (rows, camps)) for e in range(fanout)]
        sums = [jnp.zeros((8, camps), jnp.float32) for _ in range(fanout)]
        for start in range(0, users, rows):
            user_scale = scale_ref[k, start : start + rows, :]
            weights = []
            for e in range(fanout):
                raw = dots[start : start + rows, e * camps : (e + 1) * camps]
                weights.append(jnp.exp2(raw * user_scale * scales[e] - shifts[e]))
            den = 1.0 + jnp.sum(functools.reduce(jnp.add, weights), axis=1, keepdims=True)
            sums = finish(k, start, rows, weights, den, sums)
        finish(k, None, rows, None, None, sums)

    landed(0)
    multiply(0, dots_a)

    def two(n, carry):
        k = 2 * n
        landed(k + 1)

        @pl.when(k + 2 < clusters)
        def _():
            landed(k + 2)

        multiply(k + 1, dots_b)
        cluster(k, dots_a)
        multiply(jnp.minimum(k + 2, clusters - 1), dots_a)
        cluster(k + 1, dots_b)
        return carry

    lax.fori_loop(0, clusters // 2, two, 0)


def spend_finish(where_ref, size_ref, users, fanout, spend_scr):
    def finish(k, start, rows, weights, den, sums):
        if start is None:
            for e in range(fanout):
                spend_scr[pl.ds(k * fanout + e, 1), :] = jnp.sum(sums[e], axis=0, keepdims=True)
            return 0
        left = size_ref[k] - where_ref[1] * users - start
        share = jnp.where(lax.broadcasted_iota(jnp.int32, (rows, 1), 0) < left, 1.0 / den, 0.0)
        out = []
        for e in range(fanout):
            part = weights[e] * share
            total = sums[e]
            for r in range(0, rows, 8):
                total = total + part[r : r + 8]
            out.append(total)
        return out

    return finish


def halves(where_ref, spend_scr, mine_ref, theirs_ref):
    count = mine_ref.shape[0]
    rep = where_ref[1]
    mine_ref[...] = spend_scr[pl.ds(pl.multiple_of(rep * count, count), count), :]
    theirs_ref[...] = spend_scr[pl.ds(pl.multiple_of((1 - rep) * count, count), count), :]


def item_facts(fact_ref, fact_sem, dual_ref, limit_ref, live_ref, item_scale_ref):
    items = dual_ref.shape[0]

    def wait(item, carry):
        pltpu.make_async_copy(fact_ref.at[item], fact_ref.at[item], fact_sem.at[item]).wait()
        return carry

    lax.fori_loop(0, items, wait, 0, unroll=8)
    group = 8
    for first in range(0, items, group):
        facts = fact_ref[first : first + group].astype(jnp.float32)
        here = slice(first, first + group)
        dual_ref[here, :] = facts[:, 0] + facts[:, 1] + facts[:, 2]
        limit_ref[here, :] = facts[:, 3] + facts[:, 4] + facts[:, 5]
        live_ref[here, :] = facts[:, 6]
        item_scale_ref[here, :] = facts[:, 6] + facts[:, 7]


def first_kernel(
    shards, half, fanout, camps, pieces, where_ref, size_ref, item_at_ref, user_hbm, scale_hbm, *rest
):
    received, outs = rest[: 2 * shards], rest[2 * shards :][:7]
    mine_ref, theirs_ref, duals_ref, limit_ref, live_ref, item_scale_ref, item_out = outs
    user_ref, scale_ref, item_ref, row_sem, item_sem, dots_a, dots_b, dual_scr, spend_scr = rest[-12:-3]
    landed_ref, fact_sem, out_sem = rest[-3:]
    cap = 2 * half
    rep = where_ref[1]
    users = user_ref.shape[1]
    width = item_ref.shape[2]

    def fetch(slot, block, facts):
        item = item_at_ref[slot]

        @pl.when(item >= 0)
        def _():
            pltpu.make_async_copy(block, item_ref.at[item], item_sem.at[item]).start()
            pltpu.make_async_copy(facts, landed_ref.at[item], fact_sem.at[item]).start()

    for n in range(shards):
        for j in range(half):
            for side, message in ((rep, received[2 * n]), (1 - rep, received[2 * n + 1])):
                rows, lanes = fact_place(j, half, camps, pieces, width)
                fetch(n * cap + side * half + j, message.at[pl.ds(j * camps, camps)], message.at[rows, lanes])
    start_rows(user_hbm, scale_hbm, user_ref, scale_ref, row_sem)
    item_facts(landed_ref, fact_sem, duals_ref, limit_ref, live_ref, item_scale_ref)

    def keep(k):
        rows = pl.ds(pl.multiple_of(k * fanout, fanout), fanout)
        return pltpu.make_async_copy(item_ref.at[rows], item_out.at[rows], out_sem.at[k])

    dual_scr[...] = jnp.where(live_ref[...] > 0.0, duals_ref[...] * gain, masked)
    finish = spend_finish(where_ref, size_ref, users, fanout, spend_scr)
    sweep_users(
        user_hbm, scale_hbm, user_ref, scale_ref, item_ref, row_sem, item_sem, item_scale_ref,
        dual_scr, dots_a, dots_b, finish, fanout, keep
    )
    halves(where_ref, spend_scr, mine_ref, theirs_ref)

    def kept(k, carry):
        keep(k).wait()
        return carry

    lax.fori_loop(0, user_ref.shape[0], kept, 0)


def second_kernel(
    fanout, where_ref, size_ref, duals_ref, live_ref, item_scale_ref, limit_ref, match_ref, got_ref, other_ref,
    user_hbm, scale_hbm, item_hbm, mine_ref, theirs_ref, next_ref, user_ref, scale_ref, item_ref, row_sem, item_sem,
    dots_a, dots_b, dual_scr, spend_scr
):
    start_items(item_hbm, item_ref, item_sem)
    start_rows(user_hbm, scale_hbm, user_ref, scale_ref, row_sem)
    duals = updated(duals_ref[...], totals(match_ref, got_ref, other_ref), limit_ref[...])
    next_ref[...] = duals
    dual_scr[...] = jnp.where(live_ref[...] > 0.0, duals * gain, masked)
    finish = spend_finish(where_ref, size_ref, user_ref.shape[1], fanout, spend_scr)
    sweep_users(
        user_hbm, scale_hbm, user_ref, scale_ref, item_ref, row_sem, item_sem, item_scale_ref,
        dual_scr, dots_a, dots_b, finish, fanout
    )
    halves(where_ref, spend_scr, mine_ref, theirs_ref)


def third_kernel(
    fanout, where_ref, size_ref, duals_ref, live_ref, item_scale_ref, limit_ref, match_ref, got_ref, other_ref,
    own_match_ref, got_one_ref, other_one_ref, own_dual_ref, own_limit_ref, user_hbm, scale_hbm, item_hbm,
    user_dual_ref, own_out_ref, user_ref, scale_ref, item_ref, row_sem, item_sem, dots_a, dots_b, dual_scr, row_scr
):
    start_items(item_hbm, item_ref, item_sem)
    start_rows(user_hbm, scale_hbm, user_ref, scale_ref, row_sem)
    duals = updated(duals_ref[...], totals(match_ref, got_ref, other_ref), limit_ref[...])
    dual_scr[...] = jnp.where(live_ref[...] > 0.0, duals * gain, masked)
    own = updated(own_dual_ref[...], totals(own_match_ref, got_one_ref, other_one_ref), own_limit_ref[...])
    own_out_ref[...] = updated(own, totals(own_match_ref, got_ref, other_ref), own_limit_ref[...])
    users = user_ref.shape[1]
    partial = []

    def finish(k, start, rows, weights, den, sums):
        if start is None:
            return 0
        lanes = 128
        offset = start % lanes
        wide = jnp.broadcast_to(den, (rows, lanes))
        eye = offset + lax.broadcasted_iota(jnp.int32, (rows, lanes), 0) == lax.broadcasted_iota(
            jnp.int32, (rows, lanes), 1
        )
        row = jnp.sum(jnp.where(eye, wide, 0.0), axis=0, keepdims=True)
        if offset:
            row = row + partial.pop()
        if offset + rows < lanes:
            partial.append(row)
            return sums
        base = start - offset
        place = where_ref[1] * users + base + lax.broadcasted_iota(jnp.int32, (1, lanes), 1)
        row_scr[k, base // lanes : base // lanes + 1, :] = jnp.where(
            place < size_ref[k], temper * jnp.log(row), 0.0
        )
        return sums

    sweep_users(
        user_hbm, scale_hbm, user_ref, scale_ref, item_ref, row_sem, item_sem, item_scale_ref,
        dual_scr, dots_a, dots_b, finish, fanout
    )
    for n in range(row_scr.shape[1]):
        user_dual_ref[:, n * 128 : (n + 1) * 128] = row_scr[:, n, :]


def program(
    user_emb, elig_owner, elig_local, cluster_size, camp_emb, camp_count, dual_init, spend_limit
):
    shards = lax.axis_size("shard")
    reps = lax.axis_size("rep")
    me = lax.axis_index("shard").astype(jnp.int32)
    rep = lax.axis_index("rep").astype(jnp.int32)
    clusters, users, width = user_emb.shape
    blocks, camps, _ = camp_emb.shape
    fanout = elig_owner.shape[1]
    items = clusters * fanout
    cap = 2 * items // shards
    half = cap // reps
    part = items // reps
    swap = [(0, 1), (1, 0)]
    f32 = jnp.float32

    owners = elig_owner.T.reshape(-1)
    locals_ = elig_local.T.reshape(-1)
    asked = jnp.arange(items, dtype=jnp.int32)
    item_ids = asked % clusters * fanout + asked // clusters
    shard_ids = jnp.arange(shards, dtype=jnp.int32)
    hot = (owners[:, None] == shard_ids[None, :]).astype(jnp.int32)
    rank = jnp.sum((jnp.cumsum(hot, axis=0) - hot) * hot, axis=1)
    slot = owners * cap + rank
    hit = slot[:, None] == jnp.arange(shards * cap, dtype=jnp.int32)[None, :]
    wanted = jnp.sum(jnp.where(hit, locals_[:, None], 0), axis=0).reshape(shards, cap)
    names = owners * blocks + locals_
    ask = jnp.concatenate([wanted, jnp.broadcast_to(names[None, :], (shards, items))], axis=1)
    heard = lax.all_to_all(ask, "shard", split_axis=0, concat_axis=0, tiled=True)
    where = jnp.stack([me, rep])

    def pieces(x):
        out = []
        for _ in range(3):
            piece = lax.reduce_precision(x, exponent_bits=8, mantissa_bits=7)
            out.append(piece)
            x = x - piece
        return out

    live = (jnp.arange(camps, dtype=jnp.int32)[None, :] < camp_count[:, None]).astype(f32)
    rows = pieces(dual_init) + pieces(spend_limit) + [live, jnp.zeros_like(live)]
    facts = jnp.stack(rows, axis=1).astype(camp_emb.dtype)
    message = half * camps + -(-half * camps // width) * len(rows)
    camp_rows, facts = in_hbm(camp_emb), in_hbm(facts)

    order = send_order(shards)
    sent = {}
    sends = [(shift, False) for shift in order] + [(0, False), (0, True)]
    for some in (sends[:4], sends[4:]):
        outs = pl.pallas_call(
            functools.partial(gather_kernel, half, some),
            out_shape=[pltpu.HBM((message, width), camp_emb.dtype)] * len(some),
            in_specs=[SMEM, SMEM, HBM, HBM],
            out_specs=[HBM] * len(some),
            scratch_shapes=[
                pltpu.VMEM((len(some), message, width), camp_emb.dtype),
                pltpu.SemaphoreType.DMA((3, len(some) * half)),
            ],
            compiler_params=pltpu.CompilerParams(vmem_limit_bytes=12 * 2**20),
            cost_estimate=pl.CostEstimate(flops=0, bytes_accessed=len(some) * 2**19, transcendentals=0),
        )(where, heard, camp_rows, facts)
        sent.update(zip(some, outs))

    got_blocks = {}
    for shift in order:
        got_blocks[shift] = lax.ppermute(sent[shift, False], "shard", [(i, i ^ shift) for i in range(shards)])

    heard, user_late, _ = lax.optimization_barrier((heard, user_emb, got_blocks[1]))
    all_names = heard[:, cap:].reshape(shards, fanout, clusters).transpose(0, 2, 1).reshape(shards, items)
    names = names.reshape(fanout, clusters).T.reshape(-1)
    item_of_slot = (
        jnp.sum(
            jnp.where(
                ((owners ^ me) * cap + rank)[:, None] == jnp.arange(shards * cap, dtype=jnp.int32)[None, :],
                (item_ids + 1)[:, None],
                0,
            ),
            axis=0,
        )
        - 1
    )
    user_scale = pl.pallas_call(
        user_kernel,
        out_shape=jax.ShapeDtypeStruct((clusters, users, camps), f32),
        grid=(clusters,),
        in_specs=[pl.BlockSpec((1, users, width), lambda k: (k, 0, 0))],
        out_specs=pl.BlockSpec((1, users, camps), lambda k: (k, 0, 0)),
        compiler_params=pltpu.CompilerParams(vmem_limit_bytes=16 * 2**20),
        cost_estimate=pl.CostEstimate(flops=8 * 2**20, bytes_accessed=8 * 2**20, transcendentals=0),
    )(in_hbm(user_late))

    def columns(which):
        return lax.dynamic_slice_in_dim(all_names, which * part, part, 1).reshape(1, -1)

    sides = (columns(rep), columns(1 - rep))
    own_names = me * blocks + jnp.arange(blocks, dtype=jnp.int32)
    match = jnp.stack([(names[:, None] == side).astype(jnp.bfloat16) for side in sides])
    own_match = jnp.stack([(own_names[:, None] == side).astype(jnp.bfloat16) for side in sides])

    gate = 2
    got_blocks[gate], item_of_slot, user_scale, match, own_match = lax.optimization_barrier(
        (got_blocks[gate], item_of_slot, user_scale, match, own_match)
    )
    received = [sent[0, False], sent[0, True]]
    for shift in range(1, shards):
        received += [got_blocks[shift], lax.ppermute(got_blocks[shift], "rep", swap)]
    user_rows, user_scale = in_hbm(user_emb), in_hbm(user_scale)

    def exchange(mine, theirs):
        total = mine + lax.ppermute(theirs, "rep", swap)
        spread = jnp.broadcast_to(total.astype(jnp.bfloat16)[None], (shards, part, camps))
        got = lax.all_to_all(spread, "shard", split_axis=0, concat_axis=0, tiled=True)
        got = got.reshape(shards * part, camps)
        return in_vmem(got), in_vmem(lax.ppermute(got, "rep", swap))

    spend_out = [jax.ShapeDtypeStruct((part, camps), f32)] * 2
    work = [
        pltpu.VMEM((clusters, users, width), user_emb.dtype),
        pltpu.VMEM((clusters, users, camps), f32),
        pltpu.VMEM((items, camps, width), camp_emb.dtype),
        pltpu.SemaphoreType.DMA((2, clusters)),
        pltpu.SemaphoreType.DMA((items,)),
        pltpu.VMEM((users, fanout * camps), f32),
        pltpu.VMEM((users, fanout * camps), f32),
        pltpu.VMEM((items, camps), f32),
    ]
    spend_work = [pltpu.VMEM((items, camps), f32)]
    limits = pltpu.CompilerParams(vmem_limit_bytes=24 * 2**20)

    mine, theirs, item_dual, item_limit, item_live, item_scale, item_emb = pl.pallas_call(
        functools.partial(first_kernel, shards, half, fanout, camps, len(rows)),
        out_shape=spend_out
        + [jax.ShapeDtypeStruct((items, camps), f32)] * 4
        + [pltpu.HBM((items, camps, width), camp_emb.dtype)],
        in_specs=[SMEM] * 3 + [HBM] * 2 + [ANY] * len(received),
        out_specs=[VMEM] * 6 + [HBM],
        scratch_shapes=work
        + spend_work
        + [
            pltpu.VMEM((items, len(rows), camps), camp_emb.dtype),
            pltpu.SemaphoreType.DMA((items,)),
            pltpu.SemaphoreType.DMA((clusters,)),
        ],
        compiler_params=limits,
    )(where, cluster_size, item_of_slot, user_rows, user_scale, *received)
    item_emb = in_hbm(item_emb)
    got_one, other_one = exchange(mine, theirs)

    mine, theirs, next_dual = pl.pallas_call(
        functools.partial(second_kernel, fanout),
        out_shape=spend_out + [jax.ShapeDtypeStruct((items, camps), f32)],
        in_specs=[SMEM] * 2 + [VMEM] * 7 + [HBM] * 3,
        out_specs=[VMEM] * 3,
        scratch_shapes=work + spend_work,
        compiler_params=limits,
    )(where, cluster_size, item_dual, item_live, item_scale, item_limit, match, got_one, other_one, user_rows,
      user_scale, item_emb)
    got_two, other_two = exchange(mine, theirs)

    user_dual, own_dual = pl.pallas_call(
        functools.partial(third_kernel, fanout),
        out_shape=[
            jax.ShapeDtypeStruct((clusters, users), f32),
            jax.ShapeDtypeStruct((blocks, camps), f32),
        ],
        in_specs=[SMEM] * 2 + [VMEM] * 12 + [HBM] * 3,
        out_specs=[VMEM] * 2,
        scratch_shapes=work + [pltpu.VMEM((clusters, users // 128, 128), f32)],
        compiler_params=limits,
    )(where, cluster_size, next_dual, item_live, item_scale, item_limit, match, got_two, other_two, own_match,
      got_one, other_one, dual_init, spend_limit, user_rows, user_scale, item_emb)
    return (user_dual, own_dual)


def solution(mesh):
    return jax.shard_map(
        program,
        mesh=mesh,
        in_specs=(
            P("shard", "rep", None),
            P("shard", None),
            P("shard", None),
            P("shard"),
            P("shard", None, None),
            P("shard"),
            P("shard", None),
            P("shard", None),
        ),
        out_specs=(P("shard", "rep"), P("shard", None)),
        check_vma=False,
    )
```

```python
import functools
import math

import jax
import jax.numpy as jnp
from jax import lax
from jax.experimental import pallas as pl
from jax.experimental.pallas import tpu as pltpu
from jax.sharding import PartitionSpec as P


epsilon = 1e-06
temper = 0.25
sharpness = 16.0
gain = 1.0 / (temper * math.log(2.0))
masked = 1e30


VMEM = pl.BlockSpec(memory_space=pltpu.VMEM)
SMEM = pl.BlockSpec(memory_space=pltpu.SMEM)
ANY = pl.BlockSpec(memory_space=pl.ANY)
HBM = pl.BlockSpec(memory_space=pltpu.HBM)


def in_hbm(x):
    return pltpu.with_memory_space_constraint(x, pltpu.HBM)


def in_vmem(x):
    return pltpu.with_memory_space_constraint(x, pltpu.VMEM)


def send_order(shards):
    top = shards // 2
    far = [top + n for n in range(top)]
    first = far[: top // 2]
    return first + list(range(1, top)) + far[top // 2 :]


def fact_place(j, half, camps, pieces, width):
    across = width // camps
    return pl.ds(half * camps + j // across * pieces, pieces), pl.ds(j % across * camps, camps)


def gather_kernel(half, sends, where_ref, asked_ref, camp_ref, fact_ref, *rest):
    outs, (stage, sem) = rest[:-2], rest[-2:]
    me, rep = where_ref[0], where_ref[1]
    _, camps, width = camp_ref.shape
    pieces = fact_ref.shape[1]
    arriving, leaving = [], []
    for n, ((shift, other), out) in enumerate(zip(sends, outs)):
        for j in range(half):
            block = asked_ref[me ^ shift, (1 - rep if other else rep) * half + j]
            rows, lanes = fact_place(j, half, camps, pieces, width)
            for copy in (
                pltpu.make_async_copy(
                    camp_ref.at[block], stage.at[n, pl.ds(j * camps, camps)], sem.at[0, n * half + j]
                ),
                pltpu.make_async_copy(fact_ref.at[block], stage.at[n, rows, lanes], sem.at[1, n * half + j]),
            ):
                copy.start()
                arriving.append(copy)
        leaving.append(pltpu.make_async_copy(stage.at[n], out, sem.at[2, n]))
    for copy in arriving:
        copy.wait()
    eye = lax.broadcasted_iota(jnp.int32, (camps, camps), 0) == lax.broadcasted_iota(jnp.int32, (camps, camps), 1)
    piece = lax.broadcasted_iota(jnp.int32, (pieces, camps), 0)

    def scales(n, carry):
        for j in range(half):
            block = stage[n, j * camps : (j + 1) * camps].astype(jnp.float32)
            total = jnp.broadcast_to(jnp.sum(block * block, axis=1, keepdims=True), (camps, camps))
            total = jnp.sum(jnp.where(eye, total, 0.0), axis=0, keepdims=True)
            rows, lanes = fact_place(j, half, camps, pieces, width)
            facts = stage[n, rows, lanes].astype(jnp.float32)
            scale = lax.rsqrt(total * (1.0 / width) + epsilon) * facts[pieces - 2 : pieces - 1]
            high = scale.astype(jnp.bfloat16).astype(jnp.float32)
            facts = jnp.where(piece == pieces - 2, high, jnp.where(piece == pieces - 1, scale - high, facts))
            stage[n, rows, lanes] = facts.astype(stage.dtype)
        return carry

    lax.fori_loop(0, len(sends), scales, 0, unroll=3 if len(sends) % 3 == 0 else 2 if len(sends) % 2 == 0 else 1)
    for copy in leaving:
        copy.start()
    for copy in leaving:
        copy.wait()


def user_kernel(user_ref, scale_ref):
    rows = user_ref[0].astype(jnp.float32)
    scale = lax.rsqrt(jnp.sum(rows * rows, axis=1, keepdims=True) * (1.0 / rows.shape[1]) + epsilon)
    scale_ref[0] = jnp.broadcast_to(scale * (sharpness / rows.shape[1] * gain), scale_ref.shape[1:])


def updated(duals, spend, limit):
    return jnp.maximum(0.0, duals + temper * jnp.log((spend + limit) / (2.0 * limit)))


def totals(match_ref, mine_ref, other_ref):
    return jnp.dot(
        match_ref[0], mine_ref[...], preferred_element_type=jnp.float32
    ) + jnp.dot(match_ref[1], other_ref[...], preferred_element_type=jnp.float32)


def start_rows(user_hbm, scale_hbm, user_ref, scale_ref, sem):
    def start(k, carry):
        pltpu.make_async_copy(user_hbm.at[k], user_ref.at[k], sem.at[0, k]).start()
        pltpu.make_async_copy(scale_hbm.at[k], scale_ref.at[k], sem.at[1, k]).start()
        return carry

    lax.fori_loop(0, user_ref.shape[0], start, 0)


def item_landed(item, item_ref, item_sem):
    pltpu.make_async_copy(item_ref.at[item], item_ref.at[item], item_sem.at[item]).wait()


def sweep_users(
    user_hbm, scale_hbm, user_ref, scale_ref, item_ref, row_sem, item_sem, item_scale_ref, dual_scr,
    dots_a, dots_b, finish, fanout, keep
):
    clusters, users, _ = user_ref.shape
    camps = item_scale_ref.shape[1]
    width = item_ref.shape[2]
    rows = 64

    def landed(k):
        pltpu.make_async_copy(user_hbm.at[k], user_ref.at[k], row_sem.at[0, k]).wait()
        pltpu.make_async_copy(scale_hbm.at[k], scale_ref.at[k], row_sem.at[1, k]).wait()
        for e in range(fanout):
            item_landed(k * fanout + e, item_ref, item_sem)

    def multiply(k, dots):
        blocks = item_ref[pl.ds(pl.multiple_of(k * fanout, fanout), fanout)].reshape(fanout * camps, width)
        dots[...] = lax.dot_general(
            user_ref[k], blocks, (((1,), (1,)), ((), ())), preferred_element_type=jnp.float32
        )

    def cluster(k, dots):
        first = pl.multiple_of(k * fanout, fanout)
        item_scale = item_scale_ref[pl.ds(first, fanout), :]
        shift = dual_scr[pl.ds(first, fanout), :]
        scales = [jnp.broadcast_to(item_scale[e : e + 1], (rows, camps)) for e in range(fanout)]
        shifts = [jnp.broadcast_to(shift[e : e + 1], (rows, camps)) for e in range(fanout)]
        sums = [jnp.zeros((8, camps), jnp.float32) for _ in range(fanout)]
        for start in range(0, users, rows):
            user_scale = scale_ref[k, start : start + rows, :]
            weights = []
            for e in range(fanout):
                raw = dots[start : start + rows, e * camps : (e + 1) * camps]
                weights.append(jnp.exp2(raw * user_scale * scales[e] - shifts[e]))
            den = 1.0 + jnp.sum(functools.reduce(jnp.add, weights), axis=1, keepdims=True)
            sums = finish(k, start, rows, weights, den, sums)
        finish(k, None, rows, None, None, sums)

    landed(0)
    multiply(0, dots_a)

    def two(n, carry):
        k = 2 * n
        landed(k + 1)

        @pl.when(k + 2 < clusters)
        def _():
            landed(k + 2)

        multiply(k + 1, dots_b)
        cluster(k, dots_a)
        multiply(jnp.minimum(k + 2, clusters - 1), dots_a)
        cluster(k + 1, dots_b)
        keep(k).start()
        keep(k + 1).start()
        return carry

    lax.fori_loop(0, clusters // 2, two, 0)


def spend_finish(where_ref, size_ref, users, fanout, spend_scr, kept_ref=None):
    def finish(k, start, rows, weights, den, sums):
        if start is not None and kept_ref is not None:
            camps = weights[0].shape[1]
            for e in range(fanout):
                kept_ref[k, start : start + rows, e * camps : (e + 1) * camps] = weights[e].astype(kept_ref.dtype)
        if start is None:
            for e in range(fanout):
                spend_scr[pl.ds(k * fanout + e, 1), :] = jnp.sum(sums[e], axis=0, keepdims=True)
            return 0
        left = size_ref[k] - where_ref[1] * users - start
        share = jnp.where(lax.broadcasted_iota(jnp.int32, (rows, 1), 0) < left, 1.0 / den, 0.0)
        out = []
        for e in range(fanout):
            part = weights[e] * share
            total = sums[e]
            for r in range(0, rows, 8):
                total = total + part[r : r + 8]
            out.append(total)
        return out

    return finish


def halves(where_ref, spend_scr, mine_ref, theirs_ref):
    count = mine_ref.shape[0]
    rep = where_ref[1]
    mine_ref[...] = spend_scr[pl.ds(pl.multiple_of(rep * count, count), count), :]
    theirs_ref[...] = spend_scr[pl.ds(pl.multiple_of((1 - rep) * count, count), count), :]


def item_facts(fact_ref, fact_sem, dual_ref, limit_ref, live_ref, item_scale_ref):
    items = dual_ref.shape[0]

    def wait(item, carry):
        pltpu.make_async_copy(fact_ref.at[item], fact_ref.at[item], fact_sem.at[item]).wait()
        return carry

    lax.fori_loop(0, items, wait, 0, unroll=8)
    group = 8
    for first in range(0, items, group):
        facts = fact_ref[first : first + group].astype(jnp.float32)
        here = slice(first, first + group)
        dual_ref[here, :] = facts[:, 0] + facts[:, 1] + facts[:, 2]
        limit_ref[here, :] = facts[:, 3] + facts[:, 4] + facts[:, 5]
        live_ref[here, :] = facts[:, 6]
        item_scale_ref[here, :] = facts[:, 6] + facts[:, 7]


def first_kernel(
    shards, half, fanout, camps, pieces, where_ref, size_ref, item_at_ref, user_hbm, scale_hbm, *rest
):
    received, outs = rest[: 2 * shards], rest[2 * shards :][:7]
    mine_ref, theirs_ref, duals_ref, limit_ref, live_ref, item_scale_ref, kept_out = outs
    user_ref, scale_ref, item_ref, row_sem, item_sem, dots_a, dots_b, dual_scr, spend_scr = rest[-13:-4]
    landed_ref, fact_sem, kept_ref, out_sem = rest[-4:]
    cap = 2 * half
    rep = where_ref[1]
    users = user_ref.shape[1]
    width = item_ref.shape[2]

    def fetch(slot, block, facts):
        item = item_at_ref[slot]

        @pl.when(item >= 0)
        def _():
            pltpu.make_async_copy(block, item_ref.at[item], item_sem.at[item]).start()
            pltpu.make_async_copy(facts, landed_ref.at[item], fact_sem.at[item]).start()

    for n in range(shards):
        for j in range(half):
            for side, message in ((rep, received[2 * n]), (1 - rep, received[2 * n + 1])):
                rows, lanes = fact_place(j, half, camps, pieces, width)
                fetch(n * cap + side * half + j, message.at[pl.ds(j * camps, camps)], message.at[rows, lanes])
    start_rows(user_hbm, scale_hbm, user_ref, scale_ref, row_sem)
    item_facts(landed_ref, fact_sem, duals_ref, limit_ref, live_ref, item_scale_ref)

    def keep(k):
        return pltpu.make_async_copy(kept_ref.at[k], kept_out.at[k], out_sem.at[k])

    dual_scr[...] = jnp.where(live_ref[...] > 0.0, duals_ref[...] * gain, masked)
    finish = spend_finish(where_ref, size_ref, users, fanout, spend_scr, kept_ref)
    sweep_users(
        user_hbm, scale_hbm, user_ref, scale_ref, item_ref, row_sem, item_sem, item_scale_ref,
        dual_scr, dots_a, dots_b, finish, fanout, keep
    )
    halves(where_ref, spend_scr, mine_ref, theirs_ref)

    def kept(k, carry):
        keep(k).wait()
        return carry

    lax.fori_loop(0, user_ref.shape[0], kept, 0)


def start_kept(kept_hbm, kept_ref, sem):
    def start(k, carry):
        pltpu.make_async_copy(kept_hbm.at[k], kept_ref.at[k], sem.at[k]).start()
        return carry

    lax.fori_loop(0, kept_ref.shape[0], start, 0)


def reweigh(kept_hbm, kept_ref, sem, ratio_scr, finish, fanout):
    clusters, users, wide = kept_ref.shape
    camps = wide // fanout
    rows = 64

    def cluster(k):
        ratio = ratio_scr[pl.ds(pl.multiple_of(k * fanout, fanout), fanout), :]
        ratios = [jnp.broadcast_to(ratio[e : e + 1], (rows, camps)) for e in range(fanout)]
        sums = [jnp.zeros((8, camps), jnp.float32) for _ in range(fanout)]
        for start in range(0, users, rows):
            kept = [
                kept_ref[k, start : start + rows, e * camps : (e + 1) * camps].astype(jnp.float32)
                for e in range(fanout)
            ]
            weights = [one * by for one, by in zip(kept, ratios)]
            den = 1.0 + jnp.sum(functools.reduce(jnp.add, weights), axis=1, keepdims=True)
            sums = finish(k, start, rows, kept, den, sums)
        finish(k, None, rows, None, None, sums)

    def two(n, carry):
        for k in (2 * n, 2 * n + 1):
            pltpu.make_async_copy(kept_hbm.at[k], kept_ref.at[k], sem.at[k]).wait()
        cluster(2 * n)
        cluster(2 * n + 1)
        return carry

    lax.fori_loop(0, clusters // 2, two, 0)


def second_kernel(
    fanout, where_ref, size_ref, duals_ref, limit_ref, match_ref, got_ref, other_ref, kept_hbm, mine_ref, theirs_ref,
    next_ref, kept_ref, sem, ratio_scr, spend_scr
):
    start_kept(kept_hbm, kept_ref, sem)
    duals = updated(duals_ref[...], totals(match_ref, got_ref, other_ref), limit_ref[...])
    next_ref[...] = duals
    ratio_scr[...] = jnp.exp2((duals_ref[...] - duals) * gain)
    finish = spend_finish(where_ref, size_ref, kept_ref.shape[1], fanout, spend_scr)
    reweigh(kept_hbm, kept_ref, sem, ratio_scr, finish, fanout)
    spend_scr[...] = spend_scr[...] * ratio_scr[...]
    halves(where_ref, spend_scr, mine_ref, theirs_ref)


def third_kernel(
    fanout, where_ref, size_ref, start_ref, duals_ref, limit_ref, match_ref, got_ref, other_ref, own_match_ref,
    got_one_ref, other_one_ref, own_dual_ref, own_limit_ref, kept_hbm, user_dual_ref, own_out_ref, kept_ref, sem,
    ratio_scr, row_scr
):
    start_kept(kept_hbm, kept_ref, sem)
    duals = updated(duals_ref[...], totals(match_ref, got_ref, other_ref), limit_ref[...])
    ratio_scr[...] = jnp.exp2((start_ref[...] - duals) * gain)
    own = updated(own_dual_ref[...], totals(own_match_ref, got_one_ref, other_one_ref), own_limit_ref[...])
    own_out_ref[...] = updated(own, totals(own_match_ref, got_ref, other_ref), own_limit_ref[...])
    users = kept_ref.shape[1]
    partial = []

    def finish(k, start, rows, weights, den, sums):
        if start is None:
            return 0
        lanes = 128
        offset = start % lanes
        wide = jnp.broadcast_to(den, (rows, lanes))
        eye = offset + lax.broadcasted_iota(jnp.int32, (rows, lanes), 0) == lax.broadcasted_iota(
            jnp.int32, (rows, lanes), 1
        )
        row = jnp.sum(jnp.where(eye, wide, 0.0), axis=0, keepdims=True)
        if offset:
            row = row + partial.pop()
        if offset + rows < lanes:
            partial.append(row)
            return sums
        base = start - offset
        place = where_ref[1] * users + base + lax.broadcasted_iota(jnp.int32, (1, lanes), 1)
        row_scr[k, base // lanes : base // lanes + 1, :] = jnp.where(
            place < size_ref[k], temper * jnp.log(row), 0.0
        )
        return sums

    reweigh(kept_hbm, kept_ref, sem, ratio_scr, finish, fanout)
    for n in range(row_scr.shape[1]):
        user_dual_ref[:, n * 128 : (n + 1) * 128] = row_scr[:, n, :]


def program(
    user_emb, elig_owner, elig_local, cluster_size, camp_emb, camp_count, dual_init, spend_limit
):
    shards = lax.axis_size("shard")
    reps = lax.axis_size("rep")
    me = lax.axis_index("shard").astype(jnp.int32)
    rep = lax.axis_index("rep").astype(jnp.int32)
    clusters, users, width = user_emb.shape
    blocks, camps, _ = camp_emb.shape
    fanout = elig_owner.shape[1]
    items = clusters * fanout
    cap = 2 * items // shards
    half = cap // reps
    part = items // reps
    swap = [(0, 1), (1, 0)]
    f32 = jnp.float32

    owners = elig_owner.T.reshape(-1)
    locals_ = elig_local.T.reshape(-1)
    asked = jnp.arange(items, dtype=jnp.int32)
    item_ids = asked % clusters * fanout + asked // clusters
    shard_ids = jnp.arange(shards, dtype=jnp.int32)
    hot = (owners[:, None] == shard_ids[None, :]).astype(jnp.int32)
    rank = jnp.sum((jnp.cumsum(hot, axis=0) - hot) * hot, axis=1)
    slot = owners * cap + rank
    hit = slot[:, None] == jnp.arange(shards * cap, dtype=jnp.int32)[None, :]
    wanted = jnp.sum(jnp.where(hit, locals_[:, None], 0), axis=0).reshape(shards, cap)
    names = owners * blocks + locals_
    ask = jnp.concatenate([wanted, jnp.broadcast_to(names[None, :], (shards, items))], axis=1)
    heard = lax.all_to_all(ask, "shard", split_axis=0, concat_axis=0, tiled=True)
    where = jnp.stack([me, rep])

    def pieces(x):
        out = []
        for _ in range(3):
            piece = lax.reduce_precision(x, exponent_bits=8, mantissa_bits=7)
            out.append(piece)
            x = x - piece
        return out

    live = (jnp.arange(camps, dtype=jnp.int32)[None, :] < camp_count[:, None]).astype(f32)
    rows = pieces(dual_init) + pieces(spend_limit) + [live, jnp.zeros_like(live)]
    facts = jnp.stack(rows, axis=1).astype(camp_emb.dtype)
    message = half * camps + -(-half * camps // width) * len(rows)
    camp_rows, facts = in_hbm(camp_emb), in_hbm(facts)

    order = send_order(shards)
    sent = {}
    sends = [(shift, False) for shift in order] + [(0, False), (0, True)]
    for some in (sends[:4], sends[4:]):
        outs = pl.pallas_call(
            functools.partial(gather_kernel, half, some),
            out_shape=[pltpu.HBM((message, width), camp_emb.dtype)] * len(some),
            in_specs=[SMEM, SMEM, HBM, HBM],
            out_specs=[HBM] * len(some),
            scratch_shapes=[
                pltpu.VMEM((len(some), message, width), camp_emb.dtype),
                pltpu.SemaphoreType.DMA((3, len(some) * half)),
            ],
            compiler_params=pltpu.CompilerParams(vmem_limit_bytes=12 * 2**20),
            cost_estimate=pl.CostEstimate(flops=0, bytes_accessed=len(some) * 2**19, transcendentals=0),
        )(where, heard, camp_rows, facts)
        sent.update(zip(some, outs))

    got_blocks = {}
    for shift in order:
        got_blocks[shift] = lax.ppermute(sent[shift, False], "shard", [(i, i ^ shift) for i in range(shards)])

    heard, user_late, _ = lax.optimization_barrier((heard, user_emb, got_blocks[1]))
    all_names = heard[:, cap:].reshape(shards, fanout, clusters).transpose(0, 2, 1).reshape(shards, items)
    names = names.reshape(fanout, clusters).T.reshape(-1)
    item_of_slot = (
        jnp.sum(
            jnp.where(
                ((owners ^ me) * cap + rank)[:, None] == jnp.arange(shards * cap, dtype=jnp.int32)[None, :],
                (item_ids + 1)[:, None],
                0,
            ),
            axis=0,
        )
        - 1
    )
    user_scale = pl.pallas_call(
        user_kernel,
        out_shape=jax.ShapeDtypeStruct((clusters, users, camps), f32),
        grid=(clusters,),
        in_specs=[pl.BlockSpec((1, users, width), lambda k: (k, 0, 0))],
        out_specs=pl.BlockSpec((1, users, camps), lambda k: (k, 0, 0)),
        compiler_params=pltpu.CompilerParams(vmem_limit_bytes=16 * 2**20),
        cost_estimate=pl.CostEstimate(flops=8 * 2**20, bytes_accessed=8 * 2**20, transcendentals=0),
    )(in_hbm(user_late))

    def columns(which):
        return lax.dynamic_slice_in_dim(all_names, which * part, part, 1).reshape(1, -1)

    sides = (columns(rep), columns(1 - rep))
    own_names = me * blocks + jnp.arange(blocks, dtype=jnp.int32)
    match = jnp.stack([(names[:, None] == side).astype(jnp.bfloat16) for side in sides])
    own_match = jnp.stack([(own_names[:, None] == side).astype(jnp.bfloat16) for side in sides])

    gate = 2
    got_blocks[gate], item_of_slot, user_scale, match, own_match = lax.optimization_barrier(
        (got_blocks[gate], item_of_slot, user_scale, match, own_match)
    )
    received = [sent[0, False], sent[0, True]]
    for shift in range(1, shards):
        received += [got_blocks[shift], lax.ppermute(got_blocks[shift], "rep", swap)]
    user_rows, user_scale = in_hbm(user_emb), in_hbm(user_scale)

    def exchange(mine, theirs):
        total = mine + lax.ppermute(theirs, "rep", swap)
        spread = jnp.broadcast_to(total.astype(jnp.bfloat16)[None], (shards, part, camps))
        got = lax.all_to_all(spread, "shard", split_axis=0, concat_axis=0, tiled=True)
        got = got.reshape(shards * part, camps)
        return in_vmem(got), in_vmem(lax.ppermute(got, "rep", swap))

    spend_out = [jax.ShapeDtypeStruct((part, camps), f32)] * 2
    work = [
        pltpu.VMEM((clusters, users, width), user_emb.dtype),
        pltpu.VMEM((clusters, users, camps), f32),
        pltpu.VMEM((items, camps, width), camp_emb.dtype),
        pltpu.SemaphoreType.DMA((2, clusters)),
        pltpu.SemaphoreType.DMA((items,)),
        pltpu.VMEM((users, fanout * camps), f32),
        pltpu.VMEM((users, fanout * camps), f32),
        pltpu.VMEM((items, camps), f32),
    ]
    spend_work = [pltpu.VMEM((items, camps), f32)]
    limits = pltpu.CompilerParams(vmem_limit_bytes=32 * 2**20)

    mine, theirs, item_dual, item_limit, _, _, kept = pl.pallas_call(
        functools.partial(first_kernel, shards, half, fanout, camps, len(rows)),
        out_shape=spend_out
        + [jax.ShapeDtypeStruct((items, camps), f32)] * 4
        + [pltpu.HBM((clusters, users, fanout * camps), jnp.bfloat16)],
        in_specs=[SMEM] * 3 + [HBM] * 2 + [ANY] * len(received),
        out_specs=[VMEM] * 6 + [HBM],
        scratch_shapes=work
        + spend_work
        + [
            pltpu.VMEM((items, len(rows), camps), camp_emb.dtype),
            pltpu.SemaphoreType.DMA((items,)),
            pltpu.VMEM((clusters, users, fanout * camps), jnp.bfloat16),
            pltpu.SemaphoreType.DMA((clusters,)),
        ],
        compiler_params=limits,
    )(where, cluster_size, item_of_slot, user_rows, user_scale, *received)
    kept = in_hbm(kept)
    got_one, other_one = exchange(mine, theirs)
    again = [
        pltpu.VMEM((clusters, users, fanout * camps), jnp.bfloat16),
        pltpu.SemaphoreType.DMA((clusters,)),
        pltpu.VMEM((items, camps), f32),
    ]

    mine, theirs, next_dual = pl.pallas_call(
        functools.partial(second_kernel, fanout),
        out_shape=spend_out + [jax.ShapeDtypeStruct((items, camps), f32)],
        in_specs=[SMEM] * 2 + [VMEM] * 5 + [HBM],
        out_specs=[VMEM] * 3,
        scratch_shapes=again + spend_work,
        compiler_params=limits,
    )(where, cluster_size, item_dual, item_limit, match, got_one, other_one, kept)
    got_two, other_two = exchange(mine, theirs)

    user_dual, own_dual = pl.pallas_call(
        functools.partial(third_kernel, fanout),
        out_shape=[
            jax.ShapeDtypeStruct((clusters, users), f32),
            jax.ShapeDtypeStruct((blocks, camps), f32),
        ],
        in_specs=[SMEM] * 2 + [VMEM] * 11 + [HBM],
        out_specs=[VMEM] * 2,
        scratch_shapes=again + [pltpu.VMEM((clusters, users // 128, 128), f32)],
        compiler_params=limits,
    )(where, cluster_size, item_dual, next_dual, item_limit, match, got_two, other_two, own_match, got_one, other_one,
      dual_init, spend_limit, kept)
    return (user_dual, own_dual)


def solution(mesh):
    return jax.shard_map(
        program,
        mesh=mesh,
        in_specs=(
            P("shard", "rep", None),
            P("shard", None),
            P("shard", None),
            P("shard"),
            P("shard", None, None),
            P("shard"),
            P("shard", None),
            P("shard", None),
        ),
        out_specs=(P("shard", "rep"), P("shard", None)),
        check_vma=False,
    )
```

```python
import functools
import math

import jax
import jax.numpy as jnp
from jax import lax
from jax.experimental import pallas as pl
from jax.experimental.pallas import tpu as pltpu
from jax.sharding import PartitionSpec as P


epsilon = 1e-06
temper = 0.25
sharpness = 16.0
gain = 1.0 / (temper * math.log(2.0))
masked = 1e30


VMEM = pl.BlockSpec(memory_space=pltpu.VMEM)
SMEM = pl.BlockSpec(memory_space=pltpu.SMEM)
ANY = pl.BlockSpec(memory_space=pl.ANY)
HBM = pl.BlockSpec(memory_space=pltpu.HBM)


def in_hbm(x):
    return pltpu.with_memory_space_constraint(x, pltpu.HBM)


def in_vmem(x):
    return pltpu.with_memory_space_constraint(x, pltpu.VMEM)


def send_order(shards):
    top = shards // 2
    far = [top + n for n in range(top)]
    first = far[: top // 2]
    return first + list(range(1, top)) + far[top // 2 :]


def fact_place(j, half, camps, pieces, width):
    across = width // camps
    return pl.ds(half * camps + j // across * pieces, pieces), pl.ds(j % across * camps, camps)


def gather_kernel(half, sends, where_ref, asked_ref, camp_ref, fact_ref, *rest):
    outs, (stage, sem) = rest[:-2], rest[-2:]
    me, rep = where_ref[0], where_ref[1]
    _, camps, width = camp_ref.shape
    pieces = fact_ref.shape[1]
    arriving, leaving = [], []
    for n, ((shift, other), out) in enumerate(zip(sends, outs)):
        for j in range(half):
            block = asked_ref[me ^ shift, (1 - rep if other else rep) * half + j]
            rows, lanes = fact_place(j, half, camps, pieces, width)
            for copy in (
                pltpu.make_async_copy(
                    camp_ref.at[block], stage.at[n, pl.ds(j * camps, camps)], sem.at[0, n * half + j]
                ),
                pltpu.make_async_copy(fact_ref.at[block], stage.at[n, rows, lanes], sem.at[1, n * half + j]),
            ):
                copy.start()
                arriving.append(copy)
        leaving.append(pltpu.make_async_copy(stage.at[n], out, sem.at[2, n]))
    for copy in arriving:
        copy.wait()
    eye = lax.broadcasted_iota(jnp.int32, (camps, camps), 0) == lax.broadcasted_iota(jnp.int32, (camps, camps), 1)
    piece = lax.broadcasted_iota(jnp.int32, (pieces, camps), 0)

    def scales(n, carry):
        for j in range(half):
            block = stage[n, j * camps : (j + 1) * camps].astype(jnp.float32)
            total = jnp.broadcast_to(jnp.sum(block * block, axis=1, keepdims=True), (camps, camps))
            total = jnp.sum(jnp.where(eye, total, 0.0), axis=0, keepdims=True)
            rows, lanes = fact_place(j, half, camps, pieces, width)
            facts = stage[n, rows, lanes].astype(jnp.float32)
            scale = lax.rsqrt(total * (1.0 / width) + epsilon) * facts[pieces - 2 : pieces - 1]
            high = scale.astype(jnp.bfloat16).astype(jnp.float32)
            facts = jnp.where(piece == pieces - 2, high, jnp.where(piece == pieces - 1, scale - high, facts))
            stage[n, rows, lanes] = facts.astype(stage.dtype)
        return carry

    lax.fori_loop(0, len(sends), scales, 0, unroll=3 if len(sends) % 3 == 0 else 2 if len(sends) % 2 == 0 else 1)
    for copy in leaving:
        copy.start()
    for copy in leaving:
        copy.wait()


def user_kernel(user_ref, scale_ref):
    rows = user_ref[0].astype(jnp.float32)
    scale = lax.rsqrt(jnp.sum(rows * rows, axis=1, keepdims=True) * (1.0 / rows.shape[1]) + epsilon)
    scale_ref[0] = jnp.broadcast_to(scale * (sharpness / rows.shape[1] * gain), scale_ref.shape[1:])


def updated(duals, spend, limit):
    return jnp.maximum(0.0, duals + temper * jnp.log((spend + limit) / (2.0 * limit)))


def totals(match_ref, mine_ref, other_ref):
    return jnp.dot(
        match_ref[0], mine_ref[...], preferred_element_type=jnp.float32
    ) + jnp.dot(match_ref[1], other_ref[...], preferred_element_type=jnp.float32)


def start_rows(user_hbm, scale_hbm, user_ref, scale_ref, sem):
    def start(k, carry):
        pltpu.make_async_copy(user_hbm.at[k], user_ref.at[k], sem.at[0, k]).start()
        pltpu.make_async_copy(scale_hbm.at[k], scale_ref.at[k], sem.at[1, k]).start()
        return carry

    lax.fori_loop(0, user_ref.shape[0], start, 0)


def item_landed(item, item_ref, item_sem):
    pltpu.make_async_copy(item_ref.at[item], item_ref.at[item], item_sem.at[item]).wait()


def sweep_users(
    user_hbm, scale_hbm, user_ref, scale_ref, item_ref, row_sem, item_sem, item_scale_ref, dual_scr,
    dots_a, dots_b, finish, fanout
):
    clusters, users, _ = user_ref.shape
    camps = item_scale_ref.shape[1]
    width = item_ref.shape[2]
    rows = 64

    def landed(k):
        pltpu.make_async_copy(user_hbm.at[k], user_ref.at[k], row_sem.at[0, k]).wait()
        pltpu.make_async_copy(scale_hbm.at[k], scale_ref.at[k], row_sem.at[1, k]).wait()
        for e in range(fanout):
            item_landed(k * fanout + e, item_ref, item_sem)

    def multiply(k, dots):
        blocks = item_ref[pl.ds(pl.multiple_of(k * fanout, fanout), fanout)].reshape(fanout * camps, width)
        dots[...] = lax.dot_general(
            user_ref[k], blocks, (((1,), (1,)), ((), ())), preferred_element_type=jnp.float32
        )

    def cluster(k, dots):
        first = pl.multiple_of(k * fanout, fanout)
        item_scale = item_scale_ref[pl.ds(first, fanout), :]
        shift = dual_scr[pl.ds(first, fanout), :]
        scales = [jnp.broadcast_to(item_scale[e : e + 1], (rows, camps)) for e in range(fanout)]
        shifts = [jnp.broadcast_to(shift[e : e + 1], (rows, camps)) for e in range(fanout)]
        sums = [jnp.zeros((8, camps), jnp.float32) for _ in range(fanout)]
        for start in range(0, users, rows):
            user_scale = scale_ref[k, start : start + rows, :]
            weights = []
            for e in range(fanout):
                raw = dots[start : start + rows, e * camps : (e + 1) * camps]
                weights.append(jnp.exp2(raw * user_scale * scales[e] - shifts[e]))
            den = 1.0 + jnp.sum(functools.reduce(jnp.add, weights), axis=1, keepdims=True)
            sums = finish(k, start, rows, weights, den, sums)
        finish(k, None, rows, None, None, sums)

    landed(0)
    multiply(0, dots_a)

    def two(n, carry):
        k = 2 * n
        landed(k + 1)

        @pl.when(k + 2 < clusters)
        def _():
            landed(k + 2)

        multiply(k + 1, dots_b)
        cluster(k, dots_a)
        multiply(jnp.minimum(k + 2, clusters - 1), dots_a)
        cluster(k + 1, dots_b)
        return carry

    lax.fori_loop(0, clusters // 2, two, 0)


def spend_finish(where_ref, size_ref, users, fanout, spend_scr, kept_ref=None):
    def finish(k, start, rows, weights, den, sums):
        if start is not None and kept_ref is not None:
            camps = weights[0].shape[1]
            for e in range(fanout):
                kept_ref[k, start : start + rows, e * camps : (e + 1) * camps] = weights[e].astype(kept_ref.dtype)
        if start is None:
            for e in range(fanout):
                spend_scr[pl.ds(k * fanout + e, 1), :] = jnp.sum(sums[e], axis=0, keepdims=True)
            return 0
        left = size_ref[k] - where_ref[1] * users - start
        share = jnp.where(lax.broadcasted_iota(jnp.int32, (rows, 1), 0) < left, 1.0 / den, 0.0)
        out = []
        for e in range(fanout):
            part = weights[e] * share
            total = sums[e]
            for r in range(0, rows, 8):
                total = total + part[r : r + 8]
            out.append(total)
        return out

    return finish


def halves(where_ref, spend_scr, mine_ref, theirs_ref):
    count = mine_ref.shape[0]
    rep = where_ref[1]
    mine_ref[...] = spend_scr[pl.ds(pl.multiple_of(rep * count, count), count), :]
    theirs_ref[...] = spend_scr[pl.ds(pl.multiple_of((1 - rep) * count, count), count), :]


def item_facts(fact_ref, fact_sem, dual_ref, limit_ref, live_ref, item_scale_ref):
    items = dual_ref.shape[0]

    def wait(item, carry):
        pltpu.make_async_copy(fact_ref.at[item], fact_ref.at[item], fact_sem.at[item]).wait()
        return carry

    lax.fori_loop(0, items, wait, 0, unroll=8)
    group = 8
    for first in range(0, items, group):
        facts = fact_ref[first : first + group].astype(jnp.float32)
        here = slice(first, first + group)
        dual_ref[here, :] = facts[:, 0] + facts[:, 1] + facts[:, 2]
        limit_ref[here, :] = facts[:, 3] + facts[:, 4] + facts[:, 5]
        live_ref[here, :] = facts[:, 6]
        item_scale_ref[here, :] = facts[:, 6] + facts[:, 7]


def first_kernel(
    shards, half, fanout, camps, pieces, where_ref, size_ref, item_at_ref, user_hbm, scale_hbm, *rest
):
    received, outs = rest[: 2 * shards], rest[2 * shards :][:7]
    mine_ref, theirs_ref, duals_ref, limit_ref, live_ref, item_scale_ref, kept_ref = outs
    user_ref, scale_ref, item_ref, row_sem, item_sem, dots_a, dots_b, dual_scr, spend_scr = rest[-11:-2]
    landed_ref, fact_sem = rest[-2:]
    cap = 2 * half
    rep = where_ref[1]
    users = user_ref.shape[1]
    width = item_ref.shape[2]

    def fetch(slot, block, facts):
        item = item_at_ref[slot]

        @pl.when(item >= 0)
        def _():
            pltpu.make_async_copy(block, item_ref.at[item], item_sem.at[item]).start()
            pltpu.make_async_copy(facts, landed_ref.at[item], fact_sem.at[item]).start()

    for n in range(shards):
        for j in range(half):
            for side, message in ((rep, received[2 * n]), (1 - rep, received[2 * n + 1])):
                rows, lanes = fact_place(j, half, camps, pieces, width)
                fetch(n * cap + side * half + j, message.at[pl.ds(j * camps, camps)], message.at[rows, lanes])
    start_rows(user_hbm, scale_hbm, user_ref, scale_ref, row_sem)
    item_facts(landed_ref, fact_sem, duals_ref, limit_ref, live_ref, item_scale_ref)
    dual_scr[...] = jnp.where(live_ref[...] > 0.0, duals_ref[...] * gain, masked)
    finish = spend_finish(where_ref, size_ref, users, fanout, spend_scr, kept_ref)
    sweep_users(
        user_hbm, scale_hbm, user_ref, scale_ref, item_ref, row_sem, item_sem, item_scale_ref,
        dual_scr, dots_a, dots_b, finish, fanout
    )
    halves(where_ref, spend_scr, mine_ref, theirs_ref)


def reweigh(kept_ref, ratio_scr, finish, fanout):
    clusters, users, wide = kept_ref.shape
    camps = wide // fanout
    rows = 64

    def cluster(k):
        ratio = ratio_scr[pl.ds(pl.multiple_of(k * fanout, fanout), fanout), :]
        ratios = [jnp.broadcast_to(ratio[e : e + 1], (rows, camps)) for e in range(fanout)]
        sums = [jnp.zeros((8, camps), jnp.float32) for _ in range(fanout)]
        for start in range(0, users, rows):
            kept = [
                kept_ref[k, start : start + rows, e * camps : (e + 1) * camps].astype(jnp.float32)
                for e in range(fanout)
            ]
            weights = [one * by for one, by in zip(kept, ratios)]
            den = 1.0 + jnp.sum(functools.reduce(jnp.add, weights), axis=1, keepdims=True)
            sums = finish(k, start, rows, kept, den, sums)
        finish(k, None, rows, None, None, sums)

    def two(n, carry):
        cluster(2 * n)
        cluster(2 * n + 1)
        return carry

    lax.fori_loop(0, clusters // 2, two, 0)


def second_kernel(
    fanout, where_ref, size_ref, duals_ref, limit_ref, match_ref, got_ref, other_ref, kept_ref, mine_ref, theirs_ref,
    next_ref, ratio_scr, spend_scr
):
    duals = updated(duals_ref[...], totals(match_ref, got_ref, other_ref), limit_ref[...])
    next_ref[...] = duals
    ratio_scr[...] = jnp.exp2((duals_ref[...] - duals) * gain)
    finish = spend_finish(where_ref, size_ref, kept_ref.shape[1], fanout, spend_scr)
    reweigh(kept_ref, ratio_scr, finish, fanout)
    spend_scr[...] = spend_scr[...] * ratio_scr[...]
    halves(where_ref, spend_scr, mine_ref, theirs_ref)


def third_kernel(
    fanout, where_ref, size_ref, start_ref, duals_ref, limit_ref, match_ref, got_ref, other_ref, own_match_ref,
    got_one_ref, other_one_ref, own_dual_ref, own_limit_ref, kept_ref, user_dual_ref, own_out_ref,
    ratio_scr, row_scr
):
    duals = updated(duals_ref[...], totals(match_ref, got_ref, other_ref), limit_ref[...])
    ratio_scr[...] = jnp.exp2((start_ref[...] - duals) * gain)
    own = updated(own_dual_ref[...], totals(own_match_ref, got_one_ref, other_one_ref), own_limit_ref[...])
    own_out_ref[...] = updated(own, totals(own_match_ref, got_ref, other_ref), own_limit_ref[...])
    users = kept_ref.shape[1]
    partial = []

    def finish(k, start, rows, weights, den, sums):
        if start is None:
            return 0
        lanes = 128
        offset = start % lanes
        wide = jnp.broadcast_to(den, (rows, lanes))
        eye = offset + lax.broadcasted_iota(jnp.int32, (rows, lanes), 0) == lax.broadcasted_iota(
            jnp.int32, (rows, lanes), 1
        )
        row = jnp.sum(jnp.where(eye, wide, 0.0), axis=0, keepdims=True)
        if offset:
            row = row + partial.pop()
        if offset + rows < lanes:
            partial.append(row)
            return sums
        base = start - offset
        place = where_ref[1] * users + base + lax.broadcasted_iota(jnp.int32, (1, lanes), 1)
        row_scr[k, base // lanes : base // lanes + 1, :] = jnp.where(
            place < size_ref[k], temper * jnp.log(row), 0.0
        )
        return sums

    reweigh(kept_ref, ratio_scr, finish, fanout)
    for n in range(row_scr.shape[1]):
        user_dual_ref[:, n * 128 : (n + 1) * 128] = row_scr[:, n, :]


def program(
    user_emb, elig_owner, elig_local, cluster_size, camp_emb, camp_count, dual_init, spend_limit
):
    shards = lax.axis_size("shard")
    reps = lax.axis_size("rep")
    me = lax.axis_index("shard").astype(jnp.int32)
    rep = lax.axis_index("rep").astype(jnp.int32)
    clusters, users, width = user_emb.shape
    blocks, camps, _ = camp_emb.shape
    fanout = elig_owner.shape[1]
    items = clusters * fanout
    cap = 2 * items // shards
    half = cap // reps
    part = items // reps
    swap = [(0, 1), (1, 0)]
    f32 = jnp.float32

    owners = elig_owner.T.reshape(-1)
    locals_ = elig_local.T.reshape(-1)
    asked = jnp.arange(items, dtype=jnp.int32)
    item_ids = asked % clusters * fanout + asked // clusters
    shard_ids = jnp.arange(shards, dtype=jnp.int32)
    hot = (owners[:, None] == shard_ids[None, :]).astype(jnp.int32)
    rank = jnp.sum((jnp.cumsum(hot, axis=0) - hot) * hot, axis=1)
    slot = owners * cap + rank
    hit = slot[:, None] == jnp.arange(shards * cap, dtype=jnp.int32)[None, :]
    wanted = jnp.sum(jnp.where(hit, locals_[:, None], 0), axis=0).reshape(shards, cap)
    names = owners * blocks + locals_
    ask = jnp.concatenate([wanted, jnp.broadcast_to(names[None, :], (shards, items))], axis=1)
    heard = lax.all_to_all(ask, "shard", split_axis=0, concat_axis=0, tiled=True)
    where = jnp.stack([me, rep])

    def pieces(x):
        out = []
        for _ in range(3):
            piece = lax.reduce_precision(x, exponent_bits=8, mantissa_bits=7)
            out.append(piece)
            x = x - piece
        return out

    live = (jnp.arange(camps, dtype=jnp.int32)[None, :] < camp_count[:, None]).astype(f32)
    rows = pieces(dual_init) + pieces(spend_limit) + [live, jnp.zeros_like(live)]
    facts = jnp.stack(rows, axis=1).astype(camp_emb.dtype)
    message = half * camps + -(-half * camps // width) * len(rows)
    camp_rows, facts = in_hbm(camp_emb), in_hbm(facts)

    order = send_order(shards)
    sent = {}
    sends = [(shift, False) for shift in order] + [(0, False), (0, True)]
    for some in (sends[:4], sends[4:]):
        outs = pl.pallas_call(
            functools.partial(gather_kernel, half, some),
            out_shape=[pltpu.HBM((message, width), camp_emb.dtype)] * len(some),
            in_specs=[SMEM, SMEM, HBM, HBM],
            out_specs=[HBM] * len(some),
            scratch_shapes=[
                pltpu.VMEM((len(some), message, width), camp_emb.dtype),
                pltpu.SemaphoreType.DMA((3, len(some) * half)),
            ],
            compiler_params=pltpu.CompilerParams(vmem_limit_bytes=12 * 2**20),
            cost_estimate=pl.CostEstimate(flops=0, bytes_accessed=len(some) * 2**19, transcendentals=0),
        )(where, heard, camp_rows, facts)
        sent.update(zip(some, outs))

    got_blocks = {}
    for shift in order:
        got_blocks[shift] = lax.ppermute(sent[shift, False], "shard", [(i, i ^ shift) for i in range(shards)])

    heard, user_late, _ = lax.optimization_barrier((heard, user_emb, got_blocks[1]))
    all_names = heard[:, cap:].reshape(shards, fanout, clusters).transpose(0, 2, 1).reshape(shards, items)
    names = names.reshape(fanout, clusters).T.reshape(-1)
    item_of_slot = (
        jnp.sum(
            jnp.where(
                ((owners ^ me) * cap + rank)[:, None] == jnp.arange(shards * cap, dtype=jnp.int32)[None, :],
                (item_ids + 1)[:, None],
                0,
            ),
            axis=0,
        )
        - 1
    )
    user_scale = pl.pallas_call(
        user_kernel,
        out_shape=jax.ShapeDtypeStruct((clusters, users, camps), f32),
        grid=(clusters,),
        in_specs=[pl.BlockSpec((1, users, width), lambda k: (k, 0, 0))],
        out_specs=pl.BlockSpec((1, users, camps), lambda k: (k, 0, 0)),
        compiler_params=pltpu.CompilerParams(vmem_limit_bytes=16 * 2**20),
        cost_estimate=pl.CostEstimate(flops=8 * 2**20, bytes_accessed=8 * 2**20, transcendentals=0),
    )(in_hbm(user_late))

    def columns(which):
        return lax.dynamic_slice_in_dim(all_names, which * part, part, 1).reshape(1, -1)

    sides = (columns(rep), columns(1 - rep))
    own_names = me * blocks + jnp.arange(blocks, dtype=jnp.int32)
    match = jnp.stack([(names[:, None] == side).astype(jnp.bfloat16) for side in sides])
    own_match = jnp.stack([(own_names[:, None] == side).astype(jnp.bfloat16) for side in sides])

    gate = 2
    got_blocks[gate], item_of_slot, user_scale, match, own_match = lax.optimization_barrier(
        (got_blocks[gate], item_of_slot, user_scale, match, own_match)
    )
    received = [sent[0, False], sent[0, True]]
    for shift in range(1, shards):
        received += [got_blocks[shift], lax.ppermute(got_blocks[shift], "rep", swap)]
    user_rows, user_scale = in_hbm(user_emb), in_hbm(user_scale)

    def exchange(mine, theirs):
        total = mine + lax.ppermute(theirs, "rep", swap)
        spread = jnp.broadcast_to(total.astype(jnp.bfloat16)[None], (shards, part, camps))
        got = lax.all_to_all(spread, "shard", split_axis=0, concat_axis=0, tiled=True)
        got = got.reshape(shards * part, camps)
        return in_vmem(got), in_vmem(lax.ppermute(got, "rep", swap))

    spend_out = [jax.ShapeDtypeStruct((part, camps), f32)] * 2
    work = [
        pltpu.VMEM((clusters, users, width), user_emb.dtype),
        pltpu.VMEM((clusters, users, camps), f32),
        pltpu.VMEM((items, camps, width), camp_emb.dtype),
        pltpu.SemaphoreType.DMA((2, clusters)),
        pltpu.SemaphoreType.DMA((items,)),
        pltpu.VMEM((users, fanout * camps), f32),
        pltpu.VMEM((users, fanout * camps), f32),
        pltpu.VMEM((items, camps), f32),
    ]
    spend_work = [pltpu.VMEM((items, camps), f32)]
    limits = pltpu.CompilerParams(vmem_limit_bytes=32 * 2**20)

    mine, theirs, item_dual, item_limit, _, _, kept = pl.pallas_call(
        functools.partial(first_kernel, shards, half, fanout, camps, len(rows)),
        out_shape=spend_out
        + [jax.ShapeDtypeStruct((items, camps), f32)] * 4
        + [pltpu.VMEM((clusters, users, fanout * camps), jnp.bfloat16)],
        in_specs=[SMEM] * 3 + [HBM] * 2 + [ANY] * len(received),
        out_specs=[VMEM] * 7,
        scratch_shapes=work
        + spend_work
        + [
            pltpu.VMEM((items, len(rows), camps), camp_emb.dtype),
            pltpu.SemaphoreType.DMA((items,)),
        ],
        compiler_params=limits,
    )(where, cluster_size, item_of_slot, user_rows, user_scale, *received)
    kept = in_vmem(kept)
    got_one, other_one = exchange(mine, theirs)
    again = [pltpu.VMEM((items, camps), f32)]

    mine, theirs, next_dual = pl.pallas_call(
        functools.partial(second_kernel, fanout),
        out_shape=spend_out + [jax.ShapeDtypeStruct((items, camps), f32)],
        in_specs=[SMEM] * 2 + [VMEM] * 6,
        out_specs=[VMEM] * 3,
        scratch_shapes=again + spend_work,
        compiler_params=limits,
    )(where, cluster_size, item_dual, item_limit, match, got_one, other_one, kept)
    got_two, other_two = exchange(mine, theirs)

    user_dual, own_dual = pl.pallas_call(
        functools.partial(third_kernel, fanout),
        out_shape=[
            jax.ShapeDtypeStruct((clusters, users), f32),
            jax.ShapeDtypeStruct((blocks, camps), f32),
        ],
        in_specs=[SMEM] * 2 + [VMEM] * 12,
        out_specs=[VMEM] * 2,
        scratch_shapes=again + [pltpu.VMEM((clusters, users // 128, 128), f32)],
        compiler_params=limits,
    )(where, cluster_size, item_dual, next_dual, item_limit, match, got_two, other_two, own_match, got_one, other_one,
      dual_init, spend_limit, kept)
    return (user_dual, own_dual)


def solution(mesh):
    return jax.shard_map(
        program,
        mesh=mesh,
        in_specs=(
            P("shard", "rep", None),
            P("shard", None),
            P("shard", None),
            P("shard"),
            P("shard", None, None),
            P("shard"),
            P("shard", None),
            P("shard", None),
        ),
        out_specs=(P("shard", "rep"), P("shard", None)),
        check_vma=False,
    )
```

```python
import functools
import math

import jax
import jax.numpy as jnp
from jax import lax
from jax.experimental import pallas as pl
from jax.experimental.pallas import tpu as pltpu
from jax.sharding import PartitionSpec as P


epsilon = 1e-06
temper = 0.25
sharpness = 16.0
gain = 1.0 / (temper * math.log(2.0))
masked = 1e30


VMEM = pl.BlockSpec(memory_space=pltpu.VMEM)
SMEM = pl.BlockSpec(memory_space=pltpu.SMEM)
ANY = pl.BlockSpec(memory_space=pl.ANY)
HBM = pl.BlockSpec(memory_space=pltpu.HBM)


def in_hbm(x):
    return pltpu.with_memory_space_constraint(x, pltpu.HBM)


def in_vmem(x):
    return pltpu.with_memory_space_constraint(x, pltpu.VMEM)


def send_order(shards):
    top = shards // 2
    far = [top + n for n in range(top)]
    first = far[: top // 2]
    return first + list(range(1, top)) + far[top // 2 :]


def fact_place(j, half, camps, pieces, width):
    across = width // camps
    return pl.ds(half * camps + j // across * pieces, pieces), pl.ds(j % across * camps, camps)


def gather_kernel(half, sends, where_ref, asked_ref, camp_ref, fact_ref, *rest):
    outs, (stage, sem) = rest[:-2], rest[-2:]
    me, rep = where_ref[0], where_ref[1]
    _, camps, width = camp_ref.shape
    pieces = fact_ref.shape[1]
    arriving, leaving = [], []
    for n, ((shift, other), out) in enumerate(zip(sends, outs)):
        for j in range(half):
            block = asked_ref[me ^ shift, (1 - rep if other else rep) * half + j]
            rows, lanes = fact_place(j, half, camps, pieces, width)
            for copy in (
                pltpu.make_async_copy(
                    camp_ref.at[block], stage.at[n, pl.ds(j * camps, camps)], sem.at[0, n * half + j]
                ),
                pltpu.make_async_copy(fact_ref.at[block], stage.at[n, rows, lanes], sem.at[1, n * half + j]),
            ):
                copy.start()
                arriving.append(copy)
        leaving.append(pltpu.make_async_copy(stage.at[n], out, sem.at[2, n]))
    for copy in arriving:
        copy.wait()
    eye = lax.broadcasted_iota(jnp.int32, (camps, camps), 0) == lax.broadcasted_iota(jnp.int32, (camps, camps), 1)
    piece = lax.broadcasted_iota(jnp.int32, (pieces, camps), 0)

    def scales(n, carry):
        for j in range(half):
            block = stage[n, j * camps : (j + 1) * camps].astype(jnp.float32)
            total = jnp.broadcast_to(jnp.sum(block * block, axis=1, keepdims=True), (camps, camps))
            total = jnp.sum(jnp.where(eye, total, 0.0), axis=0, keepdims=True)
            rows, lanes = fact_place(j, half, camps, pieces, width)
            facts = stage[n, rows, lanes].astype(jnp.float32)
            scale = lax.rsqrt(total * (1.0 / width) + epsilon) * facts[pieces - 2 : pieces - 1]
            high = scale.astype(jnp.bfloat16).astype(jnp.float32)
            facts = jnp.where(piece == pieces - 2, high, jnp.where(piece == pieces - 1, scale - high, facts))
            stage[n, rows, lanes] = facts.astype(stage.dtype)
        return carry

    lax.fori_loop(0, len(sends), scales, 0, unroll=3 if len(sends) % 3 == 0 else 2 if len(sends) % 2 == 0 else 1)
    for copy in leaving:
        copy.start()
    for copy in leaving:
        copy.wait()


def user_kernel(user_ref, row_ref, scale_ref, sem):
    clusters, _, width = row_ref.shape

    def copy(k):
        return pltpu.make_async_copy(user_ref.at[k], row_ref.at[k], sem.at[k])

    def start(k, carry):
        copy(k).start()
        return carry

    def cluster(k, carry):
        copy(k).wait()
        rows = row_ref[k].astype(jnp.float32)
        scale = lax.rsqrt(jnp.sum(rows * rows, axis=1, keepdims=True) * (1.0 / width) + epsilon)
        scale_ref[k] = jnp.broadcast_to(scale * (sharpness / width * gain), scale_ref.shape[1:])
        return carry

    lax.fori_loop(0, clusters, start, 0)
    lax.fori_loop(0, clusters, cluster, 0)


def updated(duals, spend, limit):
    return jnp.maximum(0.0, duals + temper * jnp.log((spend + limit) / (2.0 * limit)))


def totals(match_ref, mine_ref, other_ref):
    return jnp.dot(
        match_ref[0], mine_ref[...], preferred_element_type=jnp.float32
    ) + jnp.dot(match_ref[1], other_ref[...], preferred_element_type=jnp.float32)


def item_landed(item, item_ref, item_sem):
    pltpu.make_async_copy(item_ref.at[item], item_ref.at[item], item_sem.at[item]).wait()


def sweep_users(user_ref, scale_ref, item_ref, item_sem, item_scale_ref, dual_scr, dots_a, dots_b, finish, fanout):
    clusters, users, _ = user_ref.shape
    camps = item_scale_ref.shape[1]
    width = item_ref.shape[2]
    rows = 64

    def landed(k):
        for e in range(fanout):
            item_landed(k * fanout + e, item_ref, item_sem)

    def multiply(k, dots):
        blocks = item_ref[pl.ds(pl.multiple_of(k * fanout, fanout), fanout)].reshape(fanout * camps, width)
        dots[...] = lax.dot_general(
            user_ref[k], blocks, (((1,), (1,)), ((), ())), preferred_element_type=jnp.float32
        )

    def cluster(k, dots):
        first = pl.multiple_of(k * fanout, fanout)
        item_scale = item_scale_ref[pl.ds(first, fanout), :]
        shift = dual_scr[pl.ds(first, fanout), :]
        scales = [jnp.broadcast_to(item_scale[e : e + 1], (rows, camps)) for e in range(fanout)]
        shifts = [jnp.broadcast_to(shift[e : e + 1], (rows, camps)) for e in range(fanout)]
        sums = [jnp.zeros((8, camps), jnp.float32) for _ in range(fanout)]
        for start in range(0, users, rows):
            user_scale = scale_ref[k, start : start + rows, :]
            weights = []
            for e in range(fanout):
                raw = dots[start : start + rows, e * camps : (e + 1) * camps]
                weights.append(jnp.exp2(raw * user_scale * scales[e] - shifts[e]))
            den = 1.0 + jnp.sum(functools.reduce(jnp.add, weights), axis=1, keepdims=True)
            sums = finish(k, start, rows, weights, den, sums)
        finish(k, None, rows, None, None, sums)

    landed(0)
    multiply(0, dots_a)

    def two(n, carry):
        k = 2 * n
        landed(k + 1)

        @pl.when(k + 2 < clusters)
        def _():
            landed(k + 2)

        multiply(k + 1, dots_b)
        cluster(k, dots_a)
        multiply(jnp.minimum(k + 2, clusters - 1), dots_a)
        cluster(k + 1, dots_b)
        return carry

    lax.fori_loop(0, clusters // 2, two, 0)


def spend_finish(where_ref, size_ref, users, fanout, spend_scr, kept_ref=None):
    def finish(k, start, rows, weights, den, sums):
        if start is not None and kept_ref is not None:
            camps = weights[0].shape[1]
            for e in range(fanout):
                kept_ref[k, start : start + rows, e * camps : (e + 1) * camps] = weights[e].astype(kept_ref.dtype)
        if start is None:
            for e in range(fanout):
                spend_scr[pl.ds(k * fanout + e, 1), :] = jnp.sum(sums[e], axis=0, keepdims=True)
            return 0
        left = size_ref[k] - where_ref[1] * users - start
        share = jnp.where(lax.broadcasted_iota(jnp.int32, (rows, 1), 0) < left, 1.0 / den, 0.0)
        out = []
        for e in range(fanout):
            part = weights[e] * share
            total = sums[e]
            for r in range(0, rows, 8):
                total = total + part[r : r + 8]
            out.append(total)
        return out

    return finish


def halves(where_ref, spend_scr, mine_ref, theirs_ref):
    count = mine_ref.shape[0]
    rep = where_ref[1]
    mine_ref[...] = spend_scr[pl.ds(pl.multiple_of(rep * count, count), count), :]
    theirs_ref[...] = spend_scr[pl.ds(pl.multiple_of((1 - rep) * count, count), count), :]


def item_facts(fact_ref, fact_sem, dual_ref, limit_ref, live_ref, item_scale_ref):
    items = dual_ref.shape[0]

    def wait(item, carry):
        pltpu.make_async_copy(fact_ref.at[item], fact_ref.at[item], fact_sem.at[item]).wait()
        return carry

    lax.fori_loop(0, items, wait, 0, unroll=8)
    group = 8
    for first in range(0, items, group):
        facts = fact_ref[first : first + group].astype(jnp.float32)
        here = slice(first, first + group)
        dual_ref[here, :] = facts[:, 0] + facts[:, 1] + facts[:, 2]
        limit_ref[here, :] = facts[:, 3] + facts[:, 4] + facts[:, 5]
        live_ref[here, :] = facts[:, 6]
        item_scale_ref[here, :] = facts[:, 6] + facts[:, 7]


def first_kernel(
    shards, half, fanout, camps, pieces, where_ref, size_ref, item_at_ref, user_ref, scale_ref, *rest
):
    received, outs = rest[: 2 * shards], rest[2 * shards :][:7]
    mine_ref, theirs_ref, duals_ref, limit_ref, live_ref, item_scale_ref, kept_ref = outs
    item_ref, item_sem, dots_a, dots_b, dual_scr, spend_scr = rest[-8:-2]
    landed_ref, fact_sem = rest[-2:]
    cap = 2 * half
    rep = where_ref[1]
    users = user_ref.shape[1]
    width = item_ref.shape[2]

    def fetch(slot, block, facts):
        item = item_at_ref[slot]

        @pl.when(item >= 0)
        def _():
            pltpu.make_async_copy(block, item_ref.at[item], item_sem.at[item]).start()
            pltpu.make_async_copy(facts, landed_ref.at[item], fact_sem.at[item]).start()

    for n in range(shards):
        for j in range(half):
            for side, message in ((rep, received[2 * n]), (1 - rep, received[2 * n + 1])):
                rows, lanes = fact_place(j, half, camps, pieces, width)
                fetch(n * cap + side * half + j, message.at[pl.ds(j * camps, camps)], message.at[rows, lanes])
    item_facts(landed_ref, fact_sem, duals_ref, limit_ref, live_ref, item_scale_ref)
    dual_scr[...] = jnp.where(live_ref[...] > 0.0, duals_ref[...] * gain, masked)
    finish = spend_finish(where_ref, size_ref, users, fanout, spend_scr, kept_ref)
    sweep_users(user_ref, scale_ref, item_ref, item_sem, item_scale_ref, dual_scr, dots_a, dots_b, finish, fanout)
    halves(where_ref, spend_scr, mine_ref, theirs_ref)


def reweigh(kept_ref, ratio_scr, finish, fanout):
    clusters, users, wide = kept_ref.shape
    camps = wide // fanout
    rows = 64

    def cluster(k):
        ratio = ratio_scr[pl.ds(pl.multiple_of(k * fanout, fanout), fanout), :]
        ratios = [jnp.broadcast_to(ratio[e : e + 1], (rows, camps)) for e in range(fanout)]
        sums = [jnp.zeros((8, camps), jnp.float32) for _ in range(fanout)]
        for start in range(0, users, rows):
            kept = [
                kept_ref[k, start : start + rows, e * camps : (e + 1) * camps].astype(jnp.float32)
                for e in range(fanout)
            ]
            weights = [one * by for one, by in zip(kept, ratios)]
            den = 1.0 + jnp.sum(functools.reduce(jnp.add, weights), axis=1, keepdims=True)
            sums = finish(k, start, rows, kept, den, sums)
        finish(k, None, rows, None, None, sums)

    def two(n, carry):
        cluster(2 * n)
        cluster(2 * n + 1)
        return carry

    lax.fori_loop(0, clusters // 2, two, 0)


def second_kernel(
    fanout, where_ref, size_ref, duals_ref, limit_ref, match_ref, got_ref, other_ref, kept_ref, mine_ref, theirs_ref,
    next_ref, ratio_scr, spend_scr
):
    duals = updated(duals_ref[...], totals(match_ref, got_ref, other_ref), limit_ref[...])
    next_ref[...] = duals
    ratio_scr[...] = jnp.exp2((duals_ref[...] - duals) * gain)
    finish = spend_finish(where_ref, size_ref, kept_ref.shape[1], fanout, spend_scr)
    reweigh(kept_ref, ratio_scr, finish, fanout)
    spend_scr[...] = spend_scr[...] * ratio_scr[...]
    halves(where_ref, spend_scr, mine_ref, theirs_ref)


def third_kernel(
    fanout, where_ref, size_ref, start_ref, duals_ref, limit_ref, match_ref, got_ref, other_ref, own_match_ref,
    got_one_ref, other_one_ref, own_dual_ref, own_limit_ref, kept_ref, user_dual_ref, own_out_ref,
    ratio_scr, row_scr
):
    duals = updated(duals_ref[...], totals(match_ref, got_ref, other_ref), limit_ref[...])
    ratio_scr[...] = jnp.exp2((start_ref[...] - duals) * gain)
    own = updated(own_dual_ref[...], totals(own_match_ref, got_one_ref, other_one_ref), own_limit_ref[...])
    own_out_ref[...] = updated(own, totals(own_match_ref, got_ref, other_ref), own_limit_ref[...])
    users = kept_ref.shape[1]
    partial = []

    def finish(k, start, rows, weights, den, sums):
        if start is None:
            return 0
        lanes = 128
        offset = start % lanes
        wide = jnp.broadcast_to(den, (rows, lanes))
        eye = offset + lax.broadcasted_iota(jnp.int32, (rows, lanes), 0) == lax.broadcasted_iota(
            jnp.int32, (rows, lanes), 1
        )
        row = jnp.sum(jnp.where(eye, wide, 0.0), axis=0, keepdims=True)
        if offset:
            row = row + partial.pop()
        if offset + rows < lanes:
            partial.append(row)
            return sums
        base = start - offset
        place = where_ref[1] * users + base + lax.broadcasted_iota(jnp.int32, (1, lanes), 1)
        row_scr[k, base // lanes : base // lanes + 1, :] = jnp.where(
            place < size_ref[k], temper * jnp.log(row), 0.0
        )
        return sums

    reweigh(kept_ref, ratio_scr, finish, fanout)
    for n in range(row_scr.shape[1]):
        user_dual_ref[:, n * 128 : (n + 1) * 128] = row_scr[:, n, :]


def program(
    user_emb, elig_owner, elig_local, cluster_size, camp_emb, camp_count, dual_init, spend_limit
):
    shards = lax.axis_size("shard")
    reps = lax.axis_size("rep")
    me = lax.axis_index("shard").astype(jnp.int32)
    rep = lax.axis_index("rep").astype(jnp.int32)
    clusters, users, width = user_emb.shape
    blocks, camps, _ = camp_emb.shape
    fanout = elig_owner.shape[1]
    items = clusters * fanout
    cap = 2 * items // shards
    half = cap // reps
    part = items // reps
    swap = [(0, 1), (1, 0)]
    f32 = jnp.float32

    owners = elig_owner.T.reshape(-1)
    locals_ = elig_local.T.reshape(-1)
    asked = jnp.arange(items, dtype=jnp.int32)
    item_ids = asked % clusters * fanout + asked // clusters
    shard_ids = jnp.arange(shards, dtype=jnp.int32)
    hot = (owners[:, None] == shard_ids[None, :]).astype(jnp.int32)
    rank = jnp.sum((jnp.cumsum(hot, axis=0) - hot) * hot, axis=1)
    slot = owners * cap + rank
    hit = slot[:, None] == jnp.arange(shards * cap, dtype=jnp.int32)[None, :]
    wanted = jnp.sum(jnp.where(hit, locals_[:, None], 0), axis=0).reshape(shards, cap)
    names = owners * blocks + locals_
    ask = jnp.concatenate([wanted, jnp.broadcast_to(names[None, :], (shards, items))], axis=1)
    heard = lax.all_to_all(ask, "shard", split_axis=0, concat_axis=0, tiled=True)
    where = jnp.stack([me, rep])

    def pieces(x):
        out = []
        for _ in range(3):
            piece = lax.reduce_precision(x, exponent_bits=8, mantissa_bits=7)
            out.append(piece)
            x = x - piece
        return out

    live = (jnp.arange(camps, dtype=jnp.int32)[None, :] < camp_count[:, None]).astype(f32)
    rows = pieces(dual_init) + pieces(spend_limit) + [live, jnp.zeros_like(live)]
    facts = jnp.stack(rows, axis=1).astype(camp_emb.dtype)
    message = half * camps + -(-half * camps // width) * len(rows)
    camp_rows, facts = in_hbm(camp_emb), in_hbm(facts)

    order = send_order(shards)
    sent = {}
    sends = [(shift, False) for shift in order] + [(0, False), (0, True)]
    for some in (sends[:4], sends[4:]):
        outs = pl.pallas_call(
            functools.partial(gather_kernel, half, some),
            out_shape=[pltpu.HBM((message, width), camp_emb.dtype)] * len(some),
            in_specs=[SMEM, SMEM, HBM, HBM],
            out_specs=[HBM] * len(some),
            scratch_shapes=[
                pltpu.VMEM((len(some), message, width), camp_emb.dtype),
                pltpu.SemaphoreType.DMA((3, len(some) * half)),
            ],
            compiler_params=pltpu.CompilerParams(vmem_limit_bytes=12 * 2**20),
            cost_estimate=pl.CostEstimate(flops=0, bytes_accessed=len(some) * 2**19, transcendentals=0),
        )(where, heard, camp_rows, facts)
        sent.update(zip(some, outs))

    got_blocks = {}
    for shift in order:
        got_blocks[shift] = lax.ppermute(sent[shift, False], "shard", [(i, i ^ shift) for i in range(shards)])

    heard, user_late, _ = lax.optimization_barrier((heard, user_emb, got_blocks[1]))
    all_names = heard[:, cap:].reshape(shards, fanout, clusters).transpose(0, 2, 1).reshape(shards, items)
    names = names.reshape(fanout, clusters).T.reshape(-1)
    item_of_slot = (
        jnp.sum(
            jnp.where(
                ((owners ^ me) * cap + rank)[:, None] == jnp.arange(shards * cap, dtype=jnp.int32)[None, :],
                (item_ids + 1)[:, None],
                0,
            ),
            axis=0,
        )
        - 1
    )
    user_rows, user_scale = pl.pallas_call(
        user_kernel,
        out_shape=[
            pltpu.VMEM((clusters, users, width), user_emb.dtype),
            pltpu.VMEM((clusters, users, camps), f32),
        ],
        in_specs=[HBM],
        out_specs=[VMEM] * 2,
        scratch_shapes=[pltpu.SemaphoreType.DMA((clusters,))],
        compiler_params=pltpu.CompilerParams(vmem_limit_bytes=12 * 2**20),
        cost_estimate=pl.CostEstimate(flops=8 * 2**20, bytes_accessed=8 * 2**20, transcendentals=0),
    )(in_hbm(user_late))

    def columns(which):
        return lax.dynamic_slice_in_dim(all_names, which * part, part, 1).reshape(1, -1)

    sides = (columns(rep), columns(1 - rep))
    own_names = me * blocks + jnp.arange(blocks, dtype=jnp.int32)
    match = jnp.stack([(names[:, None] == side).astype(jnp.bfloat16) for side in sides])
    own_match = jnp.stack([(own_names[:, None] == side).astype(jnp.bfloat16) for side in sides])

    gate = 2
    got_blocks[gate], item_of_slot, user_rows, user_scale, match, own_match = lax.optimization_barrier(
        (got_blocks[gate], item_of_slot, user_rows, user_scale, match, own_match)
    )
    received = [sent[0, False], sent[0, True]]
    for shift in range(1, shards):
        received += [got_blocks[shift], lax.ppermute(got_blocks[shift], "rep", swap)]
    user_rows, user_scale = in_vmem(user_rows), in_vmem(user_scale)

    def exchange(mine, theirs):
        total = mine + lax.ppermute(theirs, "rep", swap)
        spread = jnp.broadcast_to(total.astype(jnp.bfloat16)[None], (shards, part, camps))
        got = lax.all_to_all(spread, "shard", split_axis=0, concat_axis=0, tiled=True)
        got = got.reshape(shards * part, camps)
        return in_vmem(got), in_vmem(lax.ppermute(got, "rep", swap))

    spend_out = [jax.ShapeDtypeStruct((part, camps), f32)] * 2
    work = [
        pltpu.VMEM((items, camps, width), camp_emb.dtype),
        pltpu.SemaphoreType.DMA((items,)),
        pltpu.VMEM((users, fanout * camps), f32),
        pltpu.VMEM((users, fanout * camps), f32),
        pltpu.VMEM((items, camps), f32),
    ]
    spend_work = [pltpu.VMEM((items, camps), f32)]
    limits = pltpu.CompilerParams(vmem_limit_bytes=32 * 2**20)

    mine, theirs, item_dual, item_limit, _, _, kept = pl.pallas_call(
        functools.partial(first_kernel, shards, half, fanout, camps, len(rows)),
        out_shape=spend_out
        + [jax.ShapeDtypeStruct((items, camps), f32)] * 4
        + [pltpu.VMEM((clusters, users, fanout * camps), jnp.bfloat16)],
        in_specs=[SMEM] * 3 + [VMEM] * 2 + [ANY] * len(received),
        out_specs=[VMEM] * 7,
        scratch_shapes=work
        + spend_work
        + [
            pltpu.VMEM((items, len(rows), camps), camp_emb.dtype),
            pltpu.SemaphoreType.DMA((items,)),
        ],
        compiler_params=limits,
    )(where, cluster_size, item_of_slot, user_rows, user_scale, *received)
    kept = in_vmem(kept)
    got_one, other_one = exchange(mine, theirs)
    again = [pltpu.VMEM((items, camps), f32)]

    mine, theirs, next_dual = pl.pallas_call(
        functools.partial(second_kernel, fanout),
        out_shape=spend_out + [jax.ShapeDtypeStruct((items, camps), f32)],
        in_specs=[SMEM] * 2 + [VMEM] * 6,
        out_specs=[VMEM] * 3,
        scratch_shapes=again + spend_work,
        compiler_params=limits,
    )(where, cluster_size, item_dual, item_limit, match, got_one, other_one, kept)
    got_two, other_two = exchange(mine, theirs)

    user_dual, own_dual = pl.pallas_call(
        functools.partial(third_kernel, fanout),
        out_shape=[
            jax.ShapeDtypeStruct((clusters, users), f32),
            jax.ShapeDtypeStruct((blocks, camps), f32),
        ],
        in_specs=[SMEM] * 2 + [VMEM] * 12,
        out_specs=[VMEM] * 2,
        scratch_shapes=again + [pltpu.VMEM((clusters, users // 128, 128), f32)],
        compiler_params=limits,
    )(where, cluster_size, item_dual, next_dual, item_limit, match, got_two, other_two, own_match, got_one, other_one,
      dual_init, spend_limit, kept)
    return (user_dual, own_dual)


def solution(mesh):
    return jax.shard_map(
        program,
        mesh=mesh,
        in_specs=(
            P("shard", "rep", None),
            P("shard", None),
            P("shard", None),
            P("shard"),
            P("shard", None, None),
            P("shard"),
            P("shard", None),
            P("shard", None),
        ),
        out_specs=(P("shard", "rep"), P("shard", None)),
        check_vma=False,
    )
```

```python
import functools
import math

import jax
import jax.numpy as jnp
from jax import lax
from jax.experimental import pallas as pl
from jax.experimental.pallas import tpu as pltpu
from jax.sharding import PartitionSpec as P


epsilon = 1e-06
temper = 0.25
sharpness = 16.0
gain = 1.0 / (temper * math.log(2.0))
masked = 1e30


VMEM = pl.BlockSpec(memory_space=pltpu.VMEM)
SMEM = pl.BlockSpec(memory_space=pltpu.SMEM)
ANY = pl.BlockSpec(memory_space=pl.ANY)
HBM = pl.BlockSpec(memory_space=pltpu.HBM)


def in_hbm(x):
    return pltpu.with_memory_space_constraint(x, pltpu.HBM)


def in_vmem(x):
    return pltpu.with_memory_space_constraint(x, pltpu.VMEM)


def send_order(shards):
    top = shards // 2
    far = [top + n for n in range(top)]
    first = far[: top // 2]
    return first + list(range(1, top)) + far[top // 2 :]


def fact_place(j, half, camps, pieces, width):
    across = width // camps
    return pl.ds(half * camps + j // across * pieces, pieces), pl.ds(j % across * camps, camps)


def gather_kernel(half, sends, where_ref, asked_ref, camp_ref, fact_ref, *rest):
    outs, (stage, sem) = rest[:-2], rest[-2:]
    me, rep = where_ref[0], where_ref[1]
    _, camps, width = camp_ref.shape
    pieces = fact_ref.shape[1]
    arriving, leaving = [], []
    for n, ((shift, other), out) in enumerate(zip(sends, outs)):
        for j in range(half):
            block = asked_ref[me ^ shift, (1 - rep if other else rep) * half + j]
            rows, lanes = fact_place(j, half, camps, pieces, width)
            for copy in (
                pltpu.make_async_copy(
                    camp_ref.at[block], stage.at[n, pl.ds(j * camps, camps)], sem.at[0, n * half + j]
                ),
                pltpu.make_async_copy(fact_ref.at[block], stage.at[n, rows, lanes], sem.at[1, n * half + j]),
            ):
                copy.start(priority=j % 2)
                arriving.append(copy)
        leaving.append(pltpu.make_async_copy(stage.at[n], out, sem.at[2, n]))
    for copy in arriving:
        copy.wait()
    eye = lax.broadcasted_iota(jnp.int32, (camps, camps), 0) == lax.broadcasted_iota(jnp.int32, (camps, camps), 1)
    piece = lax.broadcasted_iota(jnp.int32, (pieces, camps), 0)

    def scales(n, carry):
        for j in range(half):
            block = stage[n, j * camps : (j + 1) * camps].astype(jnp.float32)
            total = jnp.broadcast_to(jnp.sum(block * block, axis=1, keepdims=True), (camps, camps))
            total = jnp.sum(jnp.where(eye, total, 0.0), axis=0, keepdims=True)
            rows, lanes = fact_place(j, half, camps, pieces, width)
            facts = stage[n, rows, lanes].astype(jnp.float32)
            scale = lax.rsqrt(total * (1.0 / width) + epsilon) * facts[pieces - 2 : pieces - 1]
            high = scale.astype(jnp.bfloat16).astype(jnp.float32)
            facts = jnp.where(piece == pieces - 2, high, jnp.where(piece == pieces - 1, scale - high, facts))
            stage[n, rows, lanes] = facts.astype(stage.dtype)
        return carry

    lax.fori_loop(0, len(sends), scales, 0, unroll=3 if len(sends) % 3 == 0 else 2 if len(sends) % 2 == 0 else 1)
    for n, copy in enumerate(leaving):
        copy.start(priority=n % 2)
    for copy in leaving:
        copy.wait()


def user_kernel(user_ref, row_ref, scale_ref, sem):
    clusters, _, width = row_ref.shape

    def copy(k):
        return pltpu.make_async_copy(user_ref.at[k], row_ref.at[k], sem.at[k])

    def start(k, carry):
        copy(k).start()
        return carry

    def cluster(k, carry):
        copy(k).wait()
        rows = row_ref[k].astype(jnp.float32)
        scale = lax.rsqrt(jnp.sum(rows * rows, axis=1, keepdims=True) * (1.0 / width) + epsilon)
        scale_ref[k] = jnp.broadcast_to(scale * (sharpness / width * gain), scale_ref.shape[1:])
        return carry

    lax.fori_loop(0, clusters, start, 0)
    lax.fori_loop(0, clusters, cluster, 0)


def updated(duals, spend, limit):
    return jnp.maximum(0.0, duals + temper * jnp.log((spend + limit) / (2.0 * limit)))


def totals(match_ref, mine_ref, other_ref):
    return jnp.dot(
        match_ref[0], mine_ref[...], preferred_element_type=jnp.float32
    ) + jnp.dot(match_ref[1], other_ref[...], preferred_element_type=jnp.float32)


def item_landed(item, item_ref, item_sem):
    pltpu.make_async_copy(item_ref.at[item], item_ref.at[item], item_sem.at[item]).wait()


def sweep_users(user_ref, scale_ref, item_ref, item_sem, item_scale_ref, dual_scr, dots_a, dots_b, finish, fanout):
    clusters, users, _ = user_ref.shape
    camps = item_scale_ref.shape[1]
    width = item_ref.shape[2]
    rows = 64

    def landed(k):
        for e in range(fanout):
            item_landed(k * fanout + e, item_ref, item_sem)

    def multiply(k, dots):
        blocks = item_ref[pl.ds(pl.multiple_of(k * fanout, fanout), fanout)].reshape(fanout * camps, width)
        dots[...] = lax.dot_general(
            user_ref[k], blocks, (((1,), (1,)), ((), ())), preferred_element_type=jnp.float32
        )

    def cluster(k, dots):
        first = pl.multiple_of(k * fanout, fanout)
        item_scale = item_scale_ref[pl.ds(first, fanout), :]
        shift = dual_scr[pl.ds(first, fanout), :]
        scales = [jnp.broadcast_to(item_scale[e : e + 1], (rows, camps)) for e in range(fanout)]
        shifts = [jnp.broadcast_to(shift[e : e + 1], (rows, camps)) for e in range(fanout)]
        sums = [jnp.zeros((8, camps), jnp.float32) for _ in range(fanout)]
        for start in range(0, users, rows):
            user_scale = scale_ref[k, start : start + rows, :]
            weights = []
            for e in range(fanout):
                raw = dots[start : start + rows, e * camps : (e + 1) * camps]
                weights.append(jnp.exp2(raw * user_scale * scales[e] - shifts[e]))
            den = 1.0 + jnp.sum(functools.reduce(jnp.add, weights), axis=1, keepdims=True)
            sums = finish(k, start, rows, weights, den, sums)
        finish(k, None, rows, None, None, sums)

    landed(0)
    multiply(0, dots_a)

    def two(n, carry):
        k = 2 * n
        landed(k + 1)

        @pl.when(k + 2 < clusters)
        def _():
            landed(k + 2)

        multiply(k + 1, dots_b)
        cluster(k, dots_a)
        multiply(jnp.minimum(k + 2, clusters - 1), dots_a)
        cluster(k + 1, dots_b)
        return carry

    lax.fori_loop(0, clusters // 2, two, 0)


def spend_finish(where_ref, size_ref, users, fanout, spend_scr, kept_ref=None):
    def finish(k, start, rows, weights, den, sums):
        if start is not None and kept_ref is not None:
            camps = weights[0].shape[1]
            for e in range(fanout):
                kept_ref[k, start : start + rows, e * camps : (e + 1) * camps] = weights[e].astype(kept_ref.dtype)
        if start is None:
            for e in range(fanout):
                spend_scr[pl.ds(k * fanout + e, 1), :] = jnp.sum(sums[e], axis=0, keepdims=True)
            return 0
        left = size_ref[k] - where_ref[1] * users - start
        share = jnp.where(lax.broadcasted_iota(jnp.int32, (rows, 1), 0) < left, 1.0 / den, 0.0)
        out = []
        for e in range(fanout):
            part = weights[e] * share
            total = sums[e]
            for r in range(0, rows, 8):
                total = total + part[r : r + 8]
            out.append(total)
        return out

    return finish


def halves(where_ref, spend_scr, mine_ref, theirs_ref):
    count = mine_ref.shape[0]
    rep = where_ref[1]
    mine_ref[...] = spend_scr[pl.ds(pl.multiple_of(rep * count, count), count), :]
    theirs_ref[...] = spend_scr[pl.ds(pl.multiple_of((1 - rep) * count, count), count), :]


def item_facts(fact_ref, fact_sem, dual_ref, limit_ref, live_ref, item_scale_ref):
    items = dual_ref.shape[0]

    def wait(item, carry):
        pltpu.make_async_copy(fact_ref.at[item], fact_ref.at[item], fact_sem.at[item]).wait()
        return carry

    lax.fori_loop(0, items, wait, 0, unroll=8)
    group = 8
    for first in range(0, items, group):
        facts = fact_ref[first : first + group].astype(jnp.float32)
        here = slice(first, first + group)
        dual_ref[here, :] = facts[:, 0] + facts[:, 1] + facts[:, 2]
        limit_ref[here, :] = facts[:, 3] + facts[:, 4] + facts[:, 5]
        live_ref[here, :] = facts[:, 6]
        item_scale_ref[here, :] = facts[:, 6] + facts[:, 7]


def first_kernel(
    shards, half, fanout, camps, pieces, where_ref, size_ref, item_at_ref, user_ref, scale_ref, *rest
):
    received, outs = rest[: 2 * shards], rest[2 * shards :][:7]
    mine_ref, theirs_ref, duals_ref, limit_ref, live_ref, item_scale_ref, kept_ref = outs
    item_ref, item_sem, dots_a, dots_b, dual_scr, spend_scr = rest[-8:-2]
    landed_ref, fact_sem = rest[-2:]
    cap = 2 * half
    rep = where_ref[1]
    users = user_ref.shape[1]
    width = item_ref.shape[2]

    def fetch(slot, queue, block, facts):
        item = item_at_ref[slot]

        @pl.when(item >= 0)
        def _():
            pltpu.make_async_copy(block, item_ref.at[item], item_sem.at[item]).start(priority=queue)
            pltpu.make_async_copy(facts, landed_ref.at[item], fact_sem.at[item]).start(priority=1 - queue)

    for n in range(shards):
        for j in range(half):
            for side, message in ((rep, received[2 * n]), (1 - rep, received[2 * n + 1])):
                rows, lanes = fact_place(j, half, camps, pieces, width)
                fetch(n * cap + side * half + j, j % 2, message.at[pl.ds(j * camps, camps)], message.at[rows, lanes])
    item_facts(landed_ref, fact_sem, duals_ref, limit_ref, live_ref, item_scale_ref)
    dual_scr[...] = jnp.where(live_ref[...] > 0.0, duals_ref[...] * gain, masked)
    finish = spend_finish(where_ref, size_ref, users, fanout, spend_scr, kept_ref)
    sweep_users(user_ref, scale_ref, item_ref, item_sem, item_scale_ref, dual_scr, dots_a, dots_b, finish, fanout)
    halves(where_ref, spend_scr, mine_ref, theirs_ref)


def reweigh(kept_ref, ratio_scr, finish, fanout):
    clusters, users, wide = kept_ref.shape
    camps = wide // fanout
    rows = 64

    def cluster(k):
        ratio = ratio_scr[pl.ds(pl.multiple_of(k * fanout, fanout), fanout), :]
        ratios = [jnp.broadcast_to(ratio[e : e + 1], (rows, camps)) for e in range(fanout)]
        sums = [jnp.zeros((8, camps), jnp.float32) for _ in range(fanout)]
        for start in range(0, users, rows):
            kept = [
                kept_ref[k, start : start + rows, e * camps : (e + 1) * camps].astype(jnp.float32)
                for e in range(fanout)
            ]
            weights = [one * by for one, by in zip(kept, ratios)]
            den = 1.0 + jnp.sum(functools.reduce(jnp.add, weights), axis=1, keepdims=True)
            sums = finish(k, start, rows, kept, den, sums)
        finish(k, None, rows, None, None, sums)

    def two(n, carry):
        cluster(2 * n)
        cluster(2 * n + 1)
        return carry

    lax.fori_loop(0, clusters // 2, two, 0)


def second_kernel(
    fanout, where_ref, size_ref, duals_ref, limit_ref, match_ref, got_ref, other_ref, kept_ref, mine_ref, theirs_ref,
    next_ref, ratio_scr, spend_scr
):
    duals = updated(duals_ref[...], totals(match_ref, got_ref, other_ref), limit_ref[...])
    next_ref[...] = duals
    ratio_scr[...] = jnp.exp2((duals_ref[...] - duals) * gain)
    finish = spend_finish(where_ref, size_ref, kept_ref.shape[1], fanout, spend_scr)
    reweigh(kept_ref, ratio_scr, finish, fanout)
    spend_scr[...] = spend_scr[...] * ratio_scr[...]
    halves(where_ref, spend_scr, mine_ref, theirs_ref)


def third_kernel(
    fanout, where_ref, size_ref, start_ref, duals_ref, limit_ref, match_ref, got_ref, other_ref, own_match_ref,
    got_one_ref, other_one_ref, own_dual_ref, own_limit_ref, kept_ref, user_dual_ref, own_out_ref,
    ratio_scr, row_scr
):
    duals = updated(duals_ref[...], totals(match_ref, got_ref, other_ref), limit_ref[...])
    ratio_scr[...] = jnp.exp2((start_ref[...] - duals) * gain)
    own = updated(own_dual_ref[...], totals(own_match_ref, got_one_ref, other_one_ref), own_limit_ref[...])
    own_out_ref[...] = updated(own, totals(own_match_ref, got_ref, other_ref), own_limit_ref[...])
    users = kept_ref.shape[1]
    partial = []

    def finish(k, start, rows, weights, den, sums):
        if start is None:
            return 0
        lanes = 128
        offset = start % lanes
        wide = jnp.broadcast_to(den, (rows, lanes))
        eye = offset + lax.broadcasted_iota(jnp.int32, (rows, lanes), 0) == lax.broadcasted_iota(
            jnp.int32, (rows, lanes), 1
        )
        row = jnp.sum(jnp.where(eye, wide, 0.0), axis=0, keepdims=True)
        if offset:
            row = row + partial.pop()
        if offset + rows < lanes:
            partial.append(row)
            return sums
        base = start - offset
        place = where_ref[1] * users + base + lax.broadcasted_iota(jnp.int32, (1, lanes), 1)
        row_scr[k, base // lanes : base // lanes + 1, :] = jnp.where(
            place < size_ref[k], temper * jnp.log(row), 0.0
        )
        return sums

    reweigh(kept_ref, ratio_scr, finish, fanout)
    for n in range(row_scr.shape[1]):
        user_dual_ref[:, n * 128 : (n + 1) * 128] = row_scr[:, n, :]


def program(
    user_emb, elig_owner, elig_local, cluster_size, camp_emb, camp_count, dual_init, spend_limit
):
    shards = lax.axis_size("shard")
    reps = lax.axis_size("rep")
    me = lax.axis_index("shard").astype(jnp.int32)
    rep = lax.axis_index("rep").astype(jnp.int32)
    clusters, users, width = user_emb.shape
    blocks, camps, _ = camp_emb.shape
    fanout = elig_owner.shape[1]
    items = clusters * fanout
    cap = 2 * items // shards
    half = cap // reps
    part = items // reps
    swap = [(0, 1), (1, 0)]
    f32 = jnp.float32

    owners = elig_owner.T.reshape(-1)
    locals_ = elig_local.T.reshape(-1)
    asked = jnp.arange(items, dtype=jnp.int32)
    item_ids = asked % clusters * fanout + asked // clusters
    shard_ids = jnp.arange(shards, dtype=jnp.int32)
    hot = (owners[:, None] == shard_ids[None, :]).astype(jnp.int32)
    rank = jnp.sum((jnp.cumsum(hot, axis=0) - hot) * hot, axis=1)
    slot = owners * cap + rank
    hit = slot[:, None] == jnp.arange(shards * cap, dtype=jnp.int32)[None, :]
    wanted = jnp.sum(jnp.where(hit, locals_[:, None], 0), axis=0).reshape(shards, cap)
    names = owners * blocks + locals_
    ask = jnp.concatenate([wanted, jnp.broadcast_to(names[None, :], (shards, items))], axis=1)
    heard = lax.all_to_all(ask, "shard", split_axis=0, concat_axis=0, tiled=True)
    where = jnp.stack([me, rep])

    def pieces(x):
        out = []
        for _ in range(3):
            piece = lax.reduce_precision(x, exponent_bits=8, mantissa_bits=7)
            out.append(piece)
            x = x - piece
        return out

    live = (jnp.arange(camps, dtype=jnp.int32)[None, :] < camp_count[:, None]).astype(f32)
    rows = pieces(dual_init) + pieces(spend_limit) + [live, jnp.zeros_like(live)]
    facts = jnp.stack(rows, axis=1).astype(camp_emb.dtype)
    message = half * camps + -(-half * camps // width) * len(rows)
    camp_rows, facts = in_hbm(camp_emb), in_hbm(facts)

    order = send_order(shards)
    sent = {}
    sends = [(shift, False) for shift in order] + [(0, False), (0, True)]
    for some in (sends[:4], sends[4:]):
        outs = pl.pallas_call(
            functools.partial(gather_kernel, half, some),
            out_shape=[pltpu.HBM((message, width), camp_emb.dtype)] * len(some),
            in_specs=[SMEM, SMEM, HBM, HBM],
            out_specs=[HBM] * len(some),
            scratch_shapes=[
                pltpu.VMEM((len(some), message, width), camp_emb.dtype),
                pltpu.SemaphoreType.DMA((3, len(some) * half)),
            ],
            compiler_params=pltpu.CompilerParams(vmem_limit_bytes=12 * 2**20),
            cost_estimate=pl.CostEstimate(flops=0, bytes_accessed=len(some) * 2**19, transcendentals=0),
        )(where, heard, camp_rows, facts)
        sent.update(zip(some, outs))

    got_blocks = {}
    for shift in order:
        got_blocks[shift] = lax.ppermute(sent[shift, False], "shard", [(i, i ^ shift) for i in range(shards)])

    heard, user_late, _ = lax.optimization_barrier((heard, user_emb, got_blocks[1]))
    all_names = heard[:, cap:].reshape(shards, fanout, clusters).transpose(0, 2, 1).reshape(shards, items)
    names = names.reshape(fanout, clusters).T.reshape(-1)
    item_of_slot = (
        jnp.sum(
            jnp.where(
                ((owners ^ me) * cap + rank)[:, None] == jnp.arange(shards * cap, dtype=jnp.int32)[None, :],
                (item_ids + 1)[:, None],
                0,
            ),
            axis=0,
        )
        - 1
    )
    user_rows, user_scale = pl.pallas_call(
        user_kernel,
        out_shape=[
            pltpu.VMEM((clusters, users, width), user_emb.dtype),
            pltpu.VMEM((clusters, users, camps), f32),
        ],
        in_specs=[HBM],
        out_specs=[VMEM] * 2,
        scratch_shapes=[pltpu.SemaphoreType.DMA((clusters,))],
        compiler_params=pltpu.CompilerParams(vmem_limit_bytes=12 * 2**20),
        cost_estimate=pl.CostEstimate(flops=8 * 2**20, bytes_accessed=8 * 2**20, transcendentals=0),
    )(in_hbm(user_late))

    def columns(which):
        return lax.dynamic_slice_in_dim(all_names, which * part, part, 1).reshape(1, -1)

    sides = (columns(rep), columns(1 - rep))
    own_names = me * blocks + jnp.arange(blocks, dtype=jnp.int32)
    match = jnp.stack([(names[:, None] == side).astype(jnp.bfloat16) for side in sides])
    own_match = jnp.stack([(own_names[:, None] == side).astype(jnp.bfloat16) for side in sides])

    gate = 2
    got_blocks[gate], item_of_slot, user_rows, user_scale, match, own_match = lax.optimization_barrier(
        (got_blocks[gate], item_of_slot, user_rows, user_scale, match, own_match)
    )
    received = [sent[0, False], sent[0, True]]
    for shift in range(1, shards):
        received += [got_blocks[shift], lax.ppermute(got_blocks[shift], "rep", swap)]
    user_rows, user_scale = in_vmem(user_rows), in_vmem(user_scale)

    def exchange(mine, theirs):
        total = mine + lax.ppermute(theirs, "rep", swap)
        spread = jnp.broadcast_to(total.astype(jnp.bfloat16)[None], (shards, part, camps))
        got = lax.all_to_all(spread, "shard", split_axis=0, concat_axis=0, tiled=True)
        got = got.reshape(shards * part, camps)
        return in_vmem(got), in_vmem(lax.ppermute(got, "rep", swap))

    spend_out = [jax.ShapeDtypeStruct((part, camps), f32)] * 2
    work = [
        pltpu.VMEM((items, camps, width), camp_emb.dtype),
        pltpu.SemaphoreType.DMA((items,)),
        pltpu.VMEM((users, fanout * camps), f32),
        pltpu.VMEM((users, fanout * camps), f32),
        pltpu.VMEM((items, camps), f32),
    ]
    spend_work = [pltpu.VMEM((items, camps), f32)]
    limits = pltpu.CompilerParams(vmem_limit_bytes=32 * 2**20)

    mine, theirs, item_dual, item_limit, _, _, kept = pl.pallas_call(
        functools.partial(first_kernel, shards, half, fanout, camps, len(rows)),
        out_shape=spend_out
        + [jax.ShapeDtypeStruct((items, camps), f32)] * 4
        + [pltpu.VMEM((clusters, users, fanout * camps), jnp.bfloat16)],
        in_specs=[SMEM] * 3 + [VMEM] * 2 + [ANY] * len(received),
        out_specs=[VMEM] * 7,
        scratch_shapes=work
        + spend_work
        + [
            pltpu.VMEM((items, len(rows), camps), camp_emb.dtype),
            pltpu.SemaphoreType.DMA((items,)),
        ],
        compiler_params=limits,
    )(where, cluster_size, item_of_slot, user_rows, user_scale, *received)
    kept = in_vmem(kept)
    got_one, other_one = exchange(mine, theirs)
    again = [pltpu.VMEM((items, camps), f32)]

    mine, theirs, next_dual = pl.pallas_call(
        functools.partial(second_kernel, fanout),
        out_shape=spend_out + [jax.ShapeDtypeStruct((items, camps), f32)],
        in_specs=[SMEM] * 2 + [VMEM] * 6,
        out_specs=[VMEM] * 3,
        scratch_shapes=again + spend_work,
        compiler_params=limits,
    )(where, cluster_size, item_dual, item_limit, match, got_one, other_one, kept)
    got_two, other_two = exchange(mine, theirs)

    user_dual, own_dual = pl.pallas_call(
        functools.partial(third_kernel, fanout),
        out_shape=[
            jax.ShapeDtypeStruct((clusters, users), f32),
            jax.ShapeDtypeStruct((blocks, camps), f32),
        ],
        in_specs=[SMEM] * 2 + [VMEM] * 12,
        out_specs=[VMEM] * 2,
        scratch_shapes=again + [pltpu.VMEM((clusters, users // 128, 128), f32)],
        compiler_params=limits,
    )(where, cluster_size, item_dual, next_dual, item_limit, match, got_two, other_two, own_match, got_one, other_one,
      dual_init, spend_limit, kept)
    return (user_dual, own_dual)


def solution(mesh):
    return jax.shard_map(
        program,
        mesh=mesh,
        in_specs=(
            P("shard", "rep", None),
            P("shard", None),
            P("shard", None),
            P("shard"),
            P("shard", None, None),
            P("shard"),
            P("shard", None),
            P("shard", None),
        ),
        out_specs=(P("shard", "rep"), P("shard", None)),
        check_vma=False,
    )
```
